32 devices in a mesh: rep: 4 (over x, core), shard: 8 (over z, y).
Axes of the slice: x: 2, y: 2, z: 4, core: 2. Of those that a mesh axis runs over, the one named last changes fastest.
Arguments:
- inputs: bfloat16 [2, 8192, 768], P(None, ('rep', 'shard')), may hold values from -6 to 6
- cotangent: bfloat16 [2, 8192, 768], P(None, ('rep', 'shard')), may hold values from -6 to 6
- segment_ids: int32 [2, 8192], P(None, 'rep'), may hold values from 0 to 9, as said below
- memory_slot: int32 [2, 8192], P(None, ('rep', 'shard')), may hold values from -1 to 19, as said below
- memory_table: bfloat16 [20, 768], P(None, 'shard'), may hold values from -6 to 6
- qkv_weight: bfloat16 [2, 768, 2304], P(None, 'shard'), may hold values from -0.21875 to 0.21875
- query_bias: bfloat16 [2, 768], P(None, 'shard'), may hold values from -3 to 3
- value_bias: bfloat16 [2, 768], P(None, 'shard'), may hold values from -3 to 3
- proj_weight: bfloat16 [2, 768, 768], P(None, 'shard'), may hold values from -4 to 4
- proj_bias: bfloat16 [2, 768], P(None, 'shard'), may hold values from -2 to 2
- attn_gain: bfloat16 [2, 768], P(None, 'shard'), may hold values from 0.099609375 to 1.8984375
- attn_shift: bfloat16 [2, 768], P(None, 'shard'), may hold values from -2 to 2
- up_weight: bfloat16 [2, 768, 3072], P(None, 'shard'), may hold values from -0.21875 to 0.21875
- up_bias: bfloat16 [2, 3072], P(None, 'shard'), may hold values from -3 to 3
- down_weight: bfloat16 [2, 3072, 768], P(None, 'shard'), may hold values from -0.109375 to 0.109375
- down_bias: bfloat16 [2, 768], P(None, 'shard'), may hold values from -2 to 2
- ffn_gain: bfloat16 [2, 768], P(None, 'shard'), may hold values from 0.099609375 to 1.8984375
- ffn_shift: bfloat16 [2, 768], P(None, 'shard'), may hold values from -2 to 2
Outputs:
- layer_output: float32 [2, 8192, 768], P(None, ('rep', 'shard'))
- input_grad: float32 [2, 8192, 768], P(None, ('rep', 'shard'))
- memory_grad: float32 [20, 768], P(None, 'shard')
- qkv_grad: float32 [2, 768, 2304], P(None, 'shard')
- querybias_grad: float32 [2, 768], P(None, 'shard')
- valuebias_grad: float32 [2, 768], P(None, 'shard')
- proj_grad: float32 [2, 768, 768], P(None, 'shard')
- projbias_grad: float32 [2, 768], P(None, 'shard')
- attngain_grad: float32 [2, 768], P(None, 'shard')
- attnshift_grad: float32 [2, 768], P(None, 'shard')
- upweight_grad: float32 [2, 768, 3072], P(None, 'shard')
- upbias_grad: float32 [2, 3072], P(None, 'shard')
- downweight_grad: float32 [2, 3072, 768], P(None, 'shard')
- downbias_grad: float32 [2, 768], P(None, 'shard')
- ffngain_grad: float32 [2, 768], P(None, 'shard')
- ffnshift_grad: float32 [2, 768], P(None, 'shard')
The draws below stay inside these ranges and needn't reach their ends.
Inputs may be any that keep to these rules, and one draw needn't show every extreme that they name: `segment_ids`: within each sequence (a run of 2048 tokens of one micro-batch) ids start at 0 and never fall; each id marks one document of at most 1024 tokens, one document of every sequence has exactly 1024, and every document except a sequence's first and last has 128 or more. `memory_slot`: the first 10 tokens of each document hold 0 to 9 in order (read memory); the last 10 tokens hold 10 to 19 in order (write memory) where they are not read tokens; all others hold -1.
All inputs are finite; a program needn't handle non-finite values.
Results may differ from the reference program's by a relative error of at most 0.028.
Values may be sent and summed in bfloat16 or wider, within the bound.
A program may use at most 320 MiB of HBM per device.

```python
import math
import jax
import jax.numpy as jnp
from jax import lax

D = 768
FF = 3072
HEADS = 12
HEAD_DIM = 64
LAYERS = 2
MICRO = 2
DOC_MAX = 1024
MEM_TOK = 10
DOC_MIN = 128
MEMS = 20
SEQ = 2048
TOKENS = 8192


def document_layout(key):
    seq_count = MICRO * (TOKENS // SEQ)
    per_side = SEQ // DOC_MIN + 2
    base_key = jax.random.fold_in(key, 7321)
    key_list = jax.random.split(base_key, 3)
    long_start = jax.random.randint(key_list[0], (seq_count,), 0, SEQ - DOC_MAX + 1).astype(jnp.int32)
    right_len = jax.random.randint(key_list[1], (seq_count, per_side), DOC_MIN, DOC_MAX + 1).astype(jnp.int32)
    left_len = jax.random.randint(key_list[2], (seq_count, per_side), DOC_MIN, DOC_MAX + 1).astype(jnp.int32)
    densest = jnp.arange(seq_count).astype(jnp.int32) == 0
    long_start = jnp.where(densest, min(1, SEQ - DOC_MAX), long_start).astype(jnp.int32)
    right_len = jnp.where(densest[:, None], DOC_MIN, right_len).astype(jnp.int32)
    right_edges = long_start[:, None] + DOC_MAX + jnp.cumsum(right_len, axis=1).astype(jnp.int32)
    left_edges = long_start[:, None] - jnp.cumsum(left_len, axis=1).astype(jnp.int32)
    edges = jnp.concatenate([long_start[:, None], long_start[:, None] + DOC_MAX, right_edges, left_edges], axis=1)
    usable = jnp.logical_and(edges > 0, edges < SEQ)
    places = jnp.arange(SEQ).astype(jnp.int32)
    below = jnp.logical_and(usable[:, None, :], edges[:, None, :] <= places[None, :, None])
    above = jnp.logical_and(usable[:, None, :], edges[:, None, :] > places[None, :, None])
    seg_ids = jnp.sum(below.astype(jnp.int32), axis=2).astype(jnp.int32)
    first_pos = jnp.max(jnp.where(below, edges[:, None, :], 0), axis=2)
    last_pos = jnp.min(jnp.where(above, edges[:, None, :], SEQ), axis=2)
    from_start = places[None, :] - first_pos
    to_end = last_pos - 1 - places[None, :]
    slot_ids = jnp.where(from_start < MEM_TOK, from_start, jnp.where(to_end < MEM_TOK, 2 * MEM_TOK - 1 - to_end, -1))
    return (seg_ids.astype(jnp.int32), slot_ids.astype(jnp.int32))


def draw_segment_ids(key, part):
    seg_ids, slot_ids = document_layout(key)
    return seg_ids.reshape(MICRO, TOKENS)


def draw_memory_slot(key, part):
    seg_ids, slot_ids = document_layout(key)
    return slot_ids.reshape(MICRO, TOKENS)


def block_levels(stream_key, shape, cuts, low, high):
    factor_of = 1.0
    for dim, shards_of in cuts:
        steps = jax.random.uniform(jax.random.fold_in(jax.random.fold_in(stream_key, 6), dim), (shards_of,), jnp.float32, low / len(cuts), high / len(cuts))
        factor_of = factor_of * jnp.repeat(jnp.exp(steps), shape[dim] // shards_of).reshape((-1,) + (1,) * (len(shape) - 1 - dim))
    return factor_of


def bell_draw(key, shape, deviation, reach, shards=(), held_as=jnp.bfloat16):
    level = block_levels(key, shape, shards, -0.22, 0.18) if shards else 1.0
    values = jax.random.normal(key, shape, jnp.float32) * deviation * level
    return jnp.minimum(jnp.maximum(values, -reach), reach).astype(held_as)


def setup_inputs(seed: int = 0) -> dict:
    key_of = jax.random.split(jax.random.key(seed), 19)
    return {
        "inputs": bell_draw(key_of[0], (MICRO, TOKENS, D), 1.0, 6.0, ((1, 32),)),
        "cotangent": bell_draw(key_of[1], (MICRO, TOKENS, D), 1.0, 6.0, ((1, 32),)),
        "segment_ids": draw_segment_ids(jax.random.fold_in(key_of[18], 71), 0),
        "memory_slot": draw_memory_slot(jax.random.fold_in(key_of[18], 71), 0),
        "memory_table": bell_draw(key_of[4], (MEMS, D), 1.0, 6.0, ((1, 8),)),
        "qkv_weight": bell_draw(key_of[5], (LAYERS, D, 3 * D), D ** -0.5, 0.21875, ((1, 8),)),
        "query_bias": bell_draw(key_of[6], (LAYERS, D), 0.5, 3.0, ((1, 8),)),
        "value_bias": bell_draw(key_of[7], (LAYERS, D), 0.5, 3.0, ((1, 8),)),
        "proj_weight": bell_draw(key_of[8], (LAYERS, D, D), 2 ** -0.5, 4.0, ((1, 8),)),
        "proj_bias": bell_draw(key_of[9], (LAYERS, D), 0.3, 2.0, ((1, 8),)),
        "attn_gain": jnp.clip(1.0 + 0.18 * jax.random.normal(key_of[10], (LAYERS, D), jnp.float32), 0.099609375, 1.8984375).astype(jnp.bfloat16),
        "attn_shift": bell_draw(key_of[11], (LAYERS, D), 0.3, 2.0, ((1, 8),)),
        "up_weight": bell_draw(key_of[12], (LAYERS, D, FF), D ** -0.5, 0.21875, ((1, 8),)),
        "up_bias": bell_draw(key_of[13], (LAYERS, FF), 0.5, 3.0, ((1, 8),)),
        "down_weight": bell_draw(key_of[14], (LAYERS, FF, D), FF ** -0.5, 0.109375, ((1, 8),)),
        "down_bias": bell_draw(key_of[15], (LAYERS, D), 0.3, 2.0, ((1, 8),)),
        "ffn_gain": jnp.clip(1.0 + 0.18 * jax.random.normal(key_of[16], (LAYERS, D), jnp.float32), 0.099609375, 1.8984375).astype(jnp.bfloat16),
        "ffn_shift": bell_draw(key_of[17], (LAYERS, D), 0.3, 2.0, ((1, 8),)),
    }


highest = lax.Precision.HIGHEST

@jax.custom_vjp
def low(v):
    return lax.optimization_barrier(v.astype(jnp.bfloat16)).astype(jnp.float32)

@jax.custom_vjp
def low_back(v):
    return v

def low_keep(v):
    return (low(v), None)

def low_pass(kept, grad):
    return (grad,)

def back_keep(v):
    return (v, None)

def back_low(kept, grad):
    return (low(grad),)
low.defvjp(low_keep, low_pass)
low_back.defvjp(back_keep, back_low)

def layer_norm(tensor, norm_gain, norm_shift):
    center = tensor - lax.optimization_barrier(jnp.mean(tensor, axis=-1, keepdims=True))
    inverse = lax.rsqrt(lax.optimization_barrier(jnp.mean(center * center, axis=-1, keepdims=True)) + 1e-12)
    return center * inverse * norm_gain + norm_shift

def attention(query_rows, key_rows, value_rows, seg_ids):
    block_rows = math.gcd(SEQ, 512)
    block_count = SEQ // block_rows
    query_blocks = query_rows.reshape(block_count, block_rows, HEADS, HEAD_DIM)
    seg_blocks = seg_ids.reshape(block_count, block_rows)
    key_heads = key_rows.reshape(SEQ, HEADS, HEAD_DIM)
    value_heads = value_rows.reshape(SEQ, HEADS, HEAD_DIM)

    def one_block(block_items):
        query_part, seg_part = block_items
        scores = jnp.einsum('qhe,khe->hqk', query_part, key_heads, precision=highest) * 0.125
        scores = low_back(scores)
        allowed = seg_part[None, :, None] == seg_ids[None, None, :]
        scores = jnp.where(allowed, scores, -1e+30)
        row_top = lax.optimization_barrier(jnp.max(scores, axis=-1, keepdims=True))
        raised = jnp.exp(scores - row_top)
        attn_probs = low(raised / lax.optimization_barrier(jnp.sum(raised, axis=-1, keepdims=True)))
        return jnp.einsum('hqk,khe->qhe', attn_probs, value_heads, precision=highest)
    mixed_out = lax.map(jax.checkpoint(one_block), (query_blocks, seg_blocks))
    return mixed_out.reshape(SEQ, HEADS * HEAD_DIM)

def one_layer(hidden, seg_ids, weights):
    qkv_w, query_b, value_b, proj_w, proj_b, attn_g, attn_s, up_w, up_b, down_w, down_b, ffn_g, ffn_s = weights
    hidden_low = low(hidden)
    mixed_all = jnp.dot(hidden_low, qkv_w, precision=highest)
    query_rows = low(low_back(mixed_all[:, :D] + query_b))
    key_rows = low(low_back(mixed_all[:, D:2 * D]))
    value_rows = low(low_back(mixed_all[:, 2 * D:] + value_b))
    context = low(low_back(attention(query_rows, key_rows, value_rows, seg_ids)))
    attn_out = low_back(jnp.dot(context, proj_w, precision=highest) + proj_b)
    settled = layer_norm(hidden + attn_out, attn_g, attn_s)
    before = low_back(jnp.dot(low(settled), up_w, precision=highest) + up_b)
    active = low(jax.nn.gelu(before, approximate=False))
    ffn_out = low_back(jnp.dot(active, down_w, precision=highest) + down_b)
    return layer_norm(settled + ffn_out, ffn_g, ffn_s)

def forward(tokens_in, slot_hot, seg_ids, params):
    hidden = tokens_in + jnp.dot(slot_hot, params[13], precision=highest)
    for layer_num in range(LAYERS):
        hidden = one_layer(hidden, seg_ids, tuple((item[layer_num] for item in params[:13])))
    return hidden

def reference(inputs, cotangent, segment_ids, memory_slot, memory_table, qkv_weight, query_bias, value_bias, proj_weight, proj_bias, attn_gain, attn_shift, up_weight, up_bias, down_weight, down_bias, ffn_gain, ffn_shift):
    params = tuple((item.astype(jnp.float32) for item in (qkv_weight, query_bias, value_bias, proj_weight, proj_bias, attn_gain, attn_shift, up_weight, up_bias, down_weight, down_bias, ffn_gain, ffn_shift, memory_table)))
    seq_count = MICRO * (TOKENS // SEQ)
    token_seqs = inputs.astype(jnp.float32).reshape(seq_count, SEQ, D)
    cot_seqs = cotangent.astype(jnp.float32).reshape(seq_count, SEQ, D)
    seg_seqs = segment_ids.reshape(seq_count, SEQ)
    slot_seqs = memory_slot.reshape(seq_count, SEQ)
    slot_range = jnp.arange(MEMS).astype(jnp.int32)

    def one_seq(grads_sum, seq_items):
        tok_seq, cot_seq, seg_seq, slot_seq = seq_items
        slot_hot = (slot_seq.astype(jnp.int32)[:, None] == slot_range[None, :]).astype(jnp.float32)
        result, pull_back = jax.vjp(lambda tok_arg, param_arg: forward(tok_arg, slot_hot, seg_seq, param_arg), tok_seq, params)
        grad_tok, grad_params = pull_back(cot_seq)
        return (jax.tree.map(jnp.add, grads_sum, grad_params), (result, grad_tok))
    zero_grads = jax.tree.map(jnp.zeros_like, params)
    grads_sum, (results, grad_toks) = lax.scan(one_seq, zero_grads, (token_seqs, cot_seqs, seg_seqs, slot_seqs))
    return (results.reshape(MICRO, TOKENS, D), grad_toks.reshape(MICRO, TOKENS, D), grads_sum[13], grads_sum[0], grads_sum[1], grads_sum[2], grads_sum[3], grads_sum[4], grads_sum[5], grads_sum[6], grads_sum[7], grads_sum[8], grads_sum[9], grads_sum[10], grads_sum[11], grads_sum[12])
```

```python
import jax
import jax.numpy as jnp
from jax import lax
from jax.experimental import pallas as pl
from jax.experimental.pallas import tpu as pltpu
from jax.sharding import PartitionSpec as P

HEADS = 12
HEAD_DIM = 64
LAYERS = 2
MEMS = 20
REACH = 4


norm_eps = 1e-12
masked_score = -1e30


def passed_along(block, axis, distance):
    devices = range(lax.axis_size(axis))
    route = [(i - distance, i) for i in devices if i - distance in devices]
    return lax.ppermute(block, axis, route)


def layer_norm(tensor, norm_gain, norm_shift):
    center = tensor - jnp.mean(tensor, axis=-1, keepdims=True)
    inverse = lax.rsqrt(jnp.mean(center * center, axis=-1, keepdims=True) + norm_eps)
    normed = center * inverse
    return (normed * norm_gain + norm_shift, normed, inverse)


def norm_backward(grad_out, normed, inverse, norm_gain):
    scaled = grad_out * norm_gain
    inner_term = (
        scaled
        - jnp.mean(scaled, axis=-1, keepdims=True)
        - normed * jnp.mean(scaled * normed, axis=-1, keepdims=True)
    )
    return (
        inner_term * inverse,
        jnp.sum(grad_out * normed, axis=(0, 1)),
        jnp.sum(grad_out, axis=(0, 1)),
    )


def gelu_exact(tensor):
    return jax.nn.gelu(tensor, approximate=False)


def split_heads(tensor):
    return tensor.reshape(tensor.shape[0], tensor.shape[1], HEADS, HEAD_DIM)


def merge_heads(tensor):
    return tensor.reshape(tensor.shape[0], tensor.shape[1], HEADS * HEAD_DIM)


def product(left_side, right_side):
    return jnp.einsum("btd,de->bte", left_side, right_side, preferred_element_type=jnp.float32)


def product_back(left_side, right_side):
    return jnp.einsum("bte,de->btd", left_side, right_side, preferred_element_type=jnp.float32)


def weight_grad(left_side, right_side):
    return jnp.einsum("btd,bte->de", left_side, right_side, preferred_element_type=jnp.float32)


def token_sum(tensor):
    return jnp.sum(tensor.astype(jnp.float32), axis=(0, 1))


def piece_mask(segment_ids, seg_here, my_index, shards, row_count, offset):
    target = my_index + offset
    inside = jnp.logical_and(target >= 0, target < shards)
    start_row = jnp.clip(target, 0, shards - 1) * row_count
    seg_there = lax.dynamic_slice_in_dim(segment_ids, start_row, row_count, 1)
    key_mask = jnp.logical_and(seg_here[:, None, :, None] == seg_there[:, None, None, :], inside)
    return (key_mask, jnp.any(key_mask))


def scaled_scores(query_heads, key_part, key_mask):
    scores = (
        jnp.einsum(
            "bqhe,bkhe->bhqk",
            query_heads,
            split_heads(key_part),
            preferred_element_type=jnp.float32,
        )
        * 0.125
    )
    return jnp.where(key_mask, scores, masked_score)


def stats_update(carry_in, query_heads, key_part, key_mask):
    old_max, old_sum = carry_in
    scores = scaled_scores(query_heads, key_part, key_mask)
    new_max = jnp.maximum(old_max, jnp.max(scores, axis=-1))
    fresh = jnp.sum(jnp.where(key_mask, jnp.exp(scores - new_max[..., None]), 0.0), axis=-1)
    return (new_max, old_sum * jnp.exp(old_max - new_max) + fresh)


def stats_keep(carry_in, query_heads, key_part, key_mask):
    return carry_in


def mix_update(context, query_heads, key_part, value_part, key_mask, log_sum):
    scores = scaled_scores(query_heads, key_part, key_mask)
    soft_probs = jnp.where(key_mask, jnp.exp(scores - log_sum[..., None]), 0.0).astype(jnp.bfloat16)
    return context + jnp.einsum(
        "bhqk,bkhe->bqhe", soft_probs, split_heads(value_part), preferred_element_type=jnp.float32
    )


def mix_keep(context, query_heads, key_part, value_part, key_mask, log_sum):
    return context


def piece_update(
    grad_query, query_heads, grad_heads, key_part, value_part, key_mask, log_sum, row_delta
):
    scores = scaled_scores(query_heads, key_part, key_mask)
    soft_probs = jnp.where(key_mask, jnp.exp(scores - log_sum[..., None]), 0.0)
    grad_probs = jnp.einsum(
        "bqhe,bkhe->bhqk", grad_heads, split_heads(value_part), preferred_element_type=jnp.float32
    )
    grad_scores = (soft_probs * (grad_probs - row_delta[..., None])).astype(jnp.bfloat16)
    grad_query = grad_query + jnp.einsum(
        "bhqk,bkhe->bqhe", grad_scores, split_heads(key_part), preferred_element_type=jnp.float32
    )
    key_grad = jnp.einsum(
        "bhqk,bqhe->bkhe", grad_scores, query_heads, preferred_element_type=jnp.float32
    )
    value_grad = jnp.einsum(
        "bhqk,bqhe->bkhe",
        soft_probs.astype(jnp.bfloat16),
        grad_heads,
        preferred_element_type=jnp.float32,
    )
    return (grad_query, merge_heads(key_grad), merge_heads(value_grad))


def piece_skip(
    grad_query, query_heads, grad_heads, key_part, value_part, key_mask, log_sum, row_delta
):
    empty = jnp.zeros(key_part.shape, jnp.float32)
    return (grad_query, empty, empty)


def attend_forward(query_rows, key_rows, value_rows, offsets, key_masks):
    micro_count, row_count = (query_rows.shape[0], query_rows.shape[1])
    query_heads = split_heads(query_rows)
    pieces = [(key_rows, value_rows)]
    for offset in offsets:
        pieces.append(passed_along((key_rows, value_rows), "shard", -offset))
    row_max = jnp.full((micro_count, HEADS, row_count), masked_score, jnp.float32)
    row_sum = jnp.zeros((micro_count, HEADS, row_count), jnp.float32)
    for (key_part, value_part), (key_mask, is_live) in zip(pieces, key_masks):
        row_max, row_sum = lax.cond(
            is_live, stats_update, stats_keep, (row_max, row_sum), query_heads, key_part, key_mask
        )
    log_sum = row_max + jnp.log(row_sum)
    context = jnp.zeros((micro_count, row_count, HEADS, HEAD_DIM), jnp.float32)
    for (key_part, value_part), (key_mask, is_live) in zip(pieces, key_masks):
        context = lax.cond(
            is_live,
            mix_update,
            mix_keep,
            context,
            query_heads,
            key_part,
            value_part,
            key_mask,
            log_sum,
        )
    return (merge_heads(context), log_sum, pieces)


def attend_backward(query_rows, grad_context, context, log_sum, pieces, key_masks, offsets):
    query_heads = split_heads(query_rows)
    grad_heads = split_heads(grad_context)
    row_delta = jnp.transpose(
        jnp.sum(split_heads(grad_context.astype(jnp.float32) * context), axis=-1), (0, 2, 1)
    )
    grad_query = jnp.zeros(query_heads.shape, jnp.float32)
    own_keys = jnp.zeros(query_rows.shape, jnp.float32)
    own_values = jnp.zeros(query_rows.shape, jnp.float32)
    for index_num in range(len(pieces)):
        key_part, value_part = pieces[index_num]
        key_mask, is_live = key_masks[index_num]
        grad_query, key_grad, value_grad = lax.cond(
            is_live,
            piece_update,
            piece_skip,
            grad_query,
            query_heads,
            grad_heads,
            key_part,
            value_part,
            key_mask,
            log_sum,
            row_delta,
        )
        if index_num == 0:
            own_keys = key_grad
            own_values = value_grad
        else:
            back_keys, back_values = (
                passed_along(key_grad.astype(jnp.bfloat16), "shard", offsets[index_num - 1]).astype(
                    key_grad.dtype
                ),
                passed_along(
                    value_grad.astype(jnp.bfloat16), "shard", offsets[index_num - 1]
                ).astype(value_grad.dtype),
            )
            own_keys = own_keys + back_keys
            own_values = own_values + back_values
    query_out = (merge_heads(grad_query) * 0.125).astype(jnp.bfloat16)
    return (query_out, (own_keys * 0.125).astype(jnp.bfloat16), own_values.astype(jnp.bfloat16))


def layer_forward(hidden, weights, offsets, key_masks):
    (
        qkv_w,
        query_b,
        value_b,
        proj_w,
        proj_b,
        attn_g,
        attn_s,
        up_w,
        up_b,
        down_w,
        down_b,
        ffn_g,
        ffn_s,
    ) = weights
    model_width = qkv_w.shape[0]
    hidden_low = hidden.astype(jnp.bfloat16)
    mixed_all = product(hidden_low, qkv_w)
    query_rows = (mixed_all[..., :model_width] + query_b.astype(jnp.float32)).astype(jnp.bfloat16)
    key_rows = mixed_all[..., model_width : 2 * model_width].astype(jnp.bfloat16)
    value_rows = (mixed_all[..., 2 * model_width :] + value_b.astype(jnp.float32)).astype(
        jnp.bfloat16
    )
    context, log_sum, pieces = attend_forward(query_rows, key_rows, value_rows, offsets, key_masks)
    context_low = context.astype(jnp.bfloat16)
    attn_out = product(context_low, proj_w) + proj_b.astype(jnp.float32)
    settled, normed_one, inverse_one = layer_norm(
        hidden + attn_out, attn_g.astype(jnp.float32), attn_s.astype(jnp.float32)
    )
    settled_low = settled.astype(jnp.bfloat16)
    before = product(settled_low, up_w) + up_b.astype(jnp.float32)
    active = gelu_exact(before).astype(jnp.bfloat16)
    ffn_out = product(active, down_w) + down_b.astype(jnp.float32)
    result, normed_two, inverse_two = layer_norm(
        settled + ffn_out, ffn_g.astype(jnp.float32), ffn_s.astype(jnp.float32)
    )
    saved_state = (
        hidden_low,
        query_rows,
        key_rows,
        value_rows,
        context,
        log_sum,
        pieces,
        context_low,
        normed_one,
        inverse_one,
        settled_low,
        before,
        active,
        normed_two,
        inverse_two,
    )
    return (result, saved_state)


def layer_backward(grad_out, weights, saved_state, offsets, key_masks):
    (
        qkv_w,
        query_b,
        value_b,
        proj_w,
        proj_b,
        attn_g,
        attn_s,
        up_w,
        up_b,
        down_w,
        down_b,
        ffn_g,
        ffn_s,
    ) = weights
    (
        hidden_low,
        query_rows,
        key_rows,
        value_rows,
        context,
        log_sum,
        pieces,
        context_low,
        normed_one,
        inverse_one,
        settled_low,
        before,
        active,
        normed_two,
        inverse_two,
    ) = saved_state
    grad_two, ffngain_part, ffnshift_part = norm_backward(
        grad_out, normed_two, inverse_two, ffn_g.astype(jnp.float32)
    )
    grad_ffn = grad_two.astype(jnp.bfloat16)
    downweight_part = weight_grad(active, grad_ffn)
    downbias_part = token_sum(grad_ffn)
    grad_active = product_back(grad_ffn, down_w)
    gelu_pull = jax.vjp(gelu_exact, before)[1]
    grad_before = gelu_pull(grad_active)[0].astype(jnp.bfloat16)
    upweight_part = weight_grad(settled_low, grad_before)
    upbias_part = token_sum(grad_before)
    grad_settled = grad_two + product_back(grad_before, up_w)
    grad_one, attngain_part, attnshift_part = norm_backward(
        grad_settled, normed_one, inverse_one, attn_g.astype(jnp.float32)
    )
    grad_attn = grad_one.astype(jnp.bfloat16)
    proj_part = weight_grad(context_low, grad_attn)
    projbias_part = token_sum(grad_attn)
    grad_context = product_back(grad_attn, proj_w).astype(jnp.bfloat16)
    pieces = [(key_rows, value_rows)]
    for offset in offsets:
        pieces.append(passed_along((key_rows, value_rows), "shard", -offset))
    grad_query, grad_keys, grad_values = attend_backward(
        query_rows, grad_context, context, log_sum, pieces, key_masks, offsets
    )
    grad_mixed = jnp.concatenate([grad_query, grad_keys, grad_values], axis=-1)
    qkv_part = weight_grad(hidden_low, grad_mixed)
    querybias_part = token_sum(grad_query)
    valuebias_part = token_sum(grad_values)
    grad_hidden = grad_one + product_back(grad_mixed, qkv_w)
    layer_grads = (
        qkv_part,
        querybias_part,
        valuebias_part,
        proj_part,
        projbias_part,
        attngain_part,
        attnshift_part,
        upweight_part,
        upbias_part,
        downweight_part,
        downbias_part,
        ffngain_part,
        ffnshift_part,
    )
    return (grad_hidden, layer_grads)


def on_device(
    inputs,
    cotangent,
    segment_ids,
    memory_slot,
    memory_table,
    qkv_weight,
    query_bias,
    value_bias,
    proj_weight,
    proj_bias,
    attn_gain,
    attn_shift,
    up_weight,
    up_bias,
    down_weight,
    down_bias,
    ffn_gain,
    ffn_shift,
):
    shards = lax.axis_size("shard")
    my_index = lax.axis_index("shard")
    row_count = inputs.shape[1]
    reach_out = min(REACH, shards - 1)
    offsets = [offset for offset in range(-reach_out, reach_out + 1) if offset != 0]
    seg_here = lax.dynamic_slice_in_dim(segment_ids, my_index * row_count, row_count, 1)
    key_masks = [piece_mask(segment_ids, seg_here, my_index, shards, row_count, 0)]
    for offset in offsets:
        key_masks.append(piece_mask(segment_ids, seg_here, my_index, shards, row_count, offset))
    gathered = (
        lax.all_gather(qkv_weight, "shard", axis=1, tiled=True),
        lax.all_gather(query_bias, "shard", axis=1, tiled=True),
        lax.all_gather(value_bias, "shard", axis=1, tiled=True),
        lax.all_gather(proj_weight, "shard", axis=1, tiled=True),
        lax.all_gather(proj_bias, "shard", axis=1, tiled=True),
        lax.all_gather(attn_gain, "shard", axis=1, tiled=True),
        lax.all_gather(attn_shift, "shard", axis=1, tiled=True),
        lax.all_gather(up_weight, "shard", axis=1, tiled=True),
        lax.all_gather(up_bias, "shard", axis=1, tiled=True),
        lax.all_gather(down_weight, "shard", axis=1, tiled=True),
        lax.all_gather(down_bias, "shard", axis=1, tiled=True),
        lax.all_gather(ffn_gain, "shard", axis=1, tiled=True),
        lax.all_gather(ffn_shift, "shard", axis=1, tiled=True),
        lax.all_gather(memory_table, "shard", axis=1, tiled=True),
    )
    slot_range = jnp.arange(MEMS, dtype=jnp.int32)
    slot_hot = (memory_slot[..., None] == slot_range).astype(jnp.float32)
    hidden = inputs.astype(jnp.float32) + jnp.einsum(
        "btm,md->btd", slot_hot, gathered[13].astype(jnp.float32), precision=lax.Precision.HIGHEST
    )
    saved_list = []
    for layer_num in range(LAYERS):
        weights = tuple((item[layer_num] for item in gathered[:13]))
        hidden, saved_state = layer_forward(hidden, weights, offsets, key_masks)
        saved_list.append(saved_state)
    regathered = (
        lax.all_gather(qkv_weight, "shard", axis=1, tiled=True),
        lax.all_gather(query_bias, "shard", axis=1, tiled=True),
        lax.all_gather(value_bias, "shard", axis=1, tiled=True),
        lax.all_gather(proj_weight, "shard", axis=1, tiled=True),
        lax.all_gather(proj_bias, "shard", axis=1, tiled=True),
        lax.all_gather(attn_gain, "shard", axis=1, tiled=True),
        lax.all_gather(attn_shift, "shard", axis=1, tiled=True),
        lax.all_gather(up_weight, "shard", axis=1, tiled=True),
        lax.all_gather(up_bias, "shard", axis=1, tiled=True),
        lax.all_gather(down_weight, "shard", axis=1, tiled=True),
        lax.all_gather(down_bias, "shard", axis=1, tiled=True),
        lax.all_gather(ffn_gain, "shard", axis=1, tiled=True),
        lax.all_gather(ffn_shift, "shard", axis=1, tiled=True),
    )
    grad_hidden = cotangent.astype(jnp.float32)
    grads_by_layer = [None] * LAYERS
    for layer_num in range(LAYERS - 1, -1, -1):
        weights = tuple((item[layer_num] for item in regathered))
        grad_hidden, layer_grads = layer_backward(
            grad_hidden, weights, saved_list[layer_num], offsets, key_masks
        )
        grads_by_layer[layer_num] = layer_grads
    memory_full = jnp.einsum("btm,btd->md", slot_hot, grad_hidden, precision=lax.Precision.HIGHEST)
    stacked = [
        jnp.stack([grads_by_layer[layer_num][member] for layer_num in range(LAYERS)])
        for member in range(13)
    ]
    shares = (
        lax.psum_scatter(stacked[0], "shard", scatter_dimension=1, tiled=True),
        lax.psum_scatter(stacked[1], "shard", scatter_dimension=1, tiled=True),
        lax.psum_scatter(stacked[2], "shard", scatter_dimension=1, tiled=True),
        lax.psum_scatter(stacked[3], "shard", scatter_dimension=1, tiled=True),
        lax.psum_scatter(stacked[4], "shard", scatter_dimension=1, tiled=True),
        lax.psum_scatter(stacked[5], "shard", scatter_dimension=1, tiled=True),
        lax.psum_scatter(stacked[6], "shard", scatter_dimension=1, tiled=True),
        lax.psum_scatter(stacked[7], "shard", scatter_dimension=1, tiled=True),
        lax.psum_scatter(stacked[8], "shard", scatter_dimension=1, tiled=True),
        lax.psum_scatter(stacked[9], "shard", scatter_dimension=1, tiled=True),
        lax.psum_scatter(stacked[10], "shard", scatter_dimension=1, tiled=True),
        lax.psum_scatter(stacked[11], "shard", scatter_dimension=1, tiled=True),
        lax.psum_scatter(stacked[12], "shard", scatter_dimension=1, tiled=True),
        lax.psum_scatter(memory_full, "shard", scatter_dimension=1, tiled=True),
    )
    totals = (
        lax.psum(shares[0].astype(jnp.bfloat16), "rep").astype(jnp.float32),
        lax.psum(shares[1].astype(jnp.bfloat16), "rep").astype(jnp.float32),
        lax.psum(shares[2].astype(jnp.bfloat16), "rep").astype(jnp.float32),
        lax.psum(shares[3].astype(jnp.bfloat16), "rep").astype(jnp.float32),
        lax.psum(shares[4].astype(jnp.bfloat16), "rep").astype(jnp.float32),
        lax.psum(shares[5].astype(jnp.bfloat16), "rep").astype(jnp.float32),
        lax.psum(shares[6].astype(jnp.bfloat16), "rep").astype(jnp.float32),
        lax.psum(shares[7].astype(jnp.bfloat16), "rep").astype(jnp.float32),
        lax.psum(shares[8].astype(jnp.bfloat16), "rep").astype(jnp.float32),
        lax.psum(shares[9].astype(jnp.bfloat16), "rep").astype(jnp.float32),
        lax.psum(shares[10].astype(jnp.bfloat16), "rep").astype(jnp.float32),
        lax.psum(shares[11].astype(jnp.bfloat16), "rep").astype(jnp.float32),
        lax.psum(shares[12].astype(jnp.bfloat16), "rep").astype(jnp.float32),
        lax.psum(shares[13].astype(jnp.bfloat16), "rep").astype(jnp.float32),
    )
    return (
        hidden,
        grad_hidden,
        totals[13],
        totals[0],
        totals[1],
        totals[2],
        totals[3],
        totals[4],
        totals[5],
        totals[6],
        totals[7],
        totals[8],
        totals[9],
        totals[10],
        totals[11],
        totals[12],
    )


BLOCK = 256
GROUP = 4
BF16 = jnp.bfloat16
F32 = jnp.float32


def mm(left, right, left_dim, right_dim):
    return lax.dot_general(
        left, right, (((left_dim,), (right_dim,)), ((), ())), preferred_element_type=F32
    )


def exchange(tensor, axis, mask):
    count = lax.axis_size(axis)
    return lax.ppermute(tensor, axis, [(i, i ^ mask) for i in range(count)])


def ordered(first_is_mine, mine, other):
    return jnp.stack(
        [jnp.where(first_is_mine, mine, other), jnp.where(first_is_mine, other, mine)]
    )


def gather_small(tensor):
    index = lax.axis_index("shard")
    for bit in range(3):
        other = exchange(tensor, "shard", 1 << bit)
        tensor = ordered((index >> bit) & 1 == 0, tensor, other)
    return tensor.reshape((8,) + tensor.shape[3:])


def sum_small(tensor):
    for axis, bits in (("rep", 2), ("shard", 3)):
        for bit in range(bits):
            tensor = tensor + exchange(tensor, axis, 1 << bit)
    return tensor


def to_groups(tensor, index):
    low = index < GROUP
    mine = jnp.where(low, tensor[0], tensor[1])
    other = exchange(jnp.where(low, tensor[1], tensor[0]), "shard", GROUP)
    both = ordered(low, mine, other)
    return both.reshape((2 * tensor.shape[1],) + tensor.shape[2:])


def from_groups(tensor, index):
    low = index < GROUP
    half = tensor.shape[0] // 2
    mine = jnp.where(low, tensor[:half], tensor[half:])
    other = exchange(
        jnp.where(low, tensor[half:], tensor[:half]).astype(BF16), "shard", GROUP
    ).astype(tensor.dtype)
    return ordered(low, mine, other)


def swap(tensor):
    shape = tensor.shape
    flat = tensor.reshape((shape[0] * shape[1],) + shape[2:])
    moved = lax.all_to_all(
        flat, "shard", 0, 0, axis_index_groups=[[0, 1, 2, 3], [4, 5, 6, 7]], tiled=True
    )
    return moved.reshape(shape)


def block_cols(block):
    half = block // GROUP
    return pl.ds(pl.multiple_of(half * BLOCK, BLOCK), BLOCK)


def flipped(tensor):
    return jnp.transpose(tensor.astype(F32)).astype(BF16)


def pair_mask(seg_col, seg_row, keys, queries):
    col = seg_col[pl.ds(pl.multiple_of(keys * BLOCK, BLOCK), BLOCK), :]
    col = jnp.concatenate([col] * (BLOCK // 128), axis=1)
    return col == seg_row[queries]


def attend_kernel(
    lo_ref, hi_ref, x_ref, seg_col, seg_row, low_ref, out_ref, lse_ref, keys_nat, acc, top, total,
):
    heads = x_ref.shape[1] // (3 * HEAD_DIM)
    width = heads * HEAD_DIM
    blocks = seg_row.shape[0]

    def flip(block, carry):
        for h in range(heads):
            keys_nat[h, block] = flipped(
                x_ref[block % GROUP, width + h * HEAD_DIM : width + (h + 1) * HEAD_DIM, block_cols(block)]
            )
        return carry

    lax.fori_loop(0, blocks, flip, 0)

    def per_query(i, carry):
        src, cols = (i % GROUP, block_cols(i))
        for h in range(heads):
            top[h] = jnp.full(top.shape[1:], masked_score, F32)
            total[h] = jnp.zeros(total.shape[1:], F32)
            acc[h] = jnp.zeros(acc.shape[1:], F32)

        def per_key(j, inner):
            allowed = pair_mask(seg_col, seg_row, j, i)
            for h in range(heads):
                query = x_ref[src, h * HEAD_DIM : (h + 1) * HEAD_DIM, cols]
                value = x_ref[
                    j % GROUP, 2 * width + h * HEAD_DIM : 2 * width + (h + 1) * HEAD_DIM, block_cols(j)
                ]
                scores = jnp.where(allowed, mm(keys_nat[h, j], query, 1, 0), masked_score)
                old = top[h]
                new = jnp.maximum(old, jnp.max(scores, axis=0, keepdims=True))
                raised = jnp.exp(scores - new)
                fade = jnp.exp(old - new)
                top[h] = new
                total[h] = total[h] * fade + jnp.sum(raised, axis=0, keepdims=True)
                acc[h] = acc[h] * fade + mm(value, raised.astype(BF16), 1, 0)
            return inner

        lax.fori_loop(lo_ref[i], hi_ref[i], per_key, 0)
        for h in range(heads):
            out = acc[h] / total[h]
            out_ref[src, h * HEAD_DIM : (h + 1) * HEAD_DIM, cols] = out
            low_ref[src, h * HEAD_DIM : (h + 1) * HEAD_DIM, cols] = out.astype(BF16)
            lse_ref[h, i] = top[h] + jnp.log(total[h])
        return carry

    lax.fori_loop(0, blocks, per_query, 0)


def attend_back_kernel(
    lo_ref, hi_ref, x_ref, go_ref, out_ref, lse_ref, seg_col, seg_row, dx_ref,
    keys_nat, values_nat, delta, dq, dk, dv,
):
    heads = x_ref.shape[1] // (3 * HEAD_DIM)
    width = heads * HEAD_DIM
    blocks = seg_row.shape[0]

    def prepare(block, carry):
        src, cols = (block % GROUP, block_cols(block))
        for h in range(heads):
            low, high = (h * HEAD_DIM, (h + 1) * HEAD_DIM)
            keys_nat[h, block] = flipped(x_ref[src, width + low : width + high, cols])
            values_nat[h, block] = flipped(x_ref[src, 2 * width + low : 2 * width + high, cols])
            delta[h, block] = jnp.sum(
                go_ref[src, low:high, cols].astype(F32) * out_ref[src, low:high, cols],
                axis=0,
                keepdims=True,
            )
            dq[h, block] = jnp.zeros(dq.shape[2:], F32)
        return carry

    lax.fori_loop(0, blocks, prepare, 0)

    def per_key(j, carry):
        key_src, key_cols = (j % GROUP, block_cols(j))
        for h in range(heads):
            dk[h] = jnp.zeros(dk.shape[1:], F32)
            dv[h] = jnp.zeros(dv.shape[1:], F32)

        def per_query(i, inner):
            src, cols = (i % GROUP, block_cols(i))
            allowed = pair_mask(seg_col, seg_row, j, i)
            for h in range(heads):
                low, high = (h * HEAD_DIM, (h + 1) * HEAD_DIM)
                query = x_ref[src, low:high, cols]
                grad = go_ref[src, low:high, cols]
                scores = jnp.where(allowed, mm(keys_nat[h, j], query, 1, 0), masked_score)
                probs = jnp.exp(scores - lse_ref[h, i])
                grad_probs = mm(values_nat[h, j], grad, 1, 0)
                grad_scores = (probs * (grad_probs - delta[h, i])).astype(BF16)
                dv[h] += mm(grad, probs.astype(BF16), 1, 1)
                dk[h] += mm(query, grad_scores, 1, 1)
                dq[h, i] += mm(x_ref[key_src, width + low : width + high, key_cols], grad_scores, 1, 0)
            return inner

        lax.fori_loop(lo_ref[j], hi_ref[j], per_query, 0)
        for h in range(heads):
            low, high = (h * HEAD_DIM, (h + 1) * HEAD_DIM)
            dx_ref[key_src, width + low : width + high, key_cols] = dk[h].astype(BF16)
            dx_ref[key_src, 2 * width + low : 2 * width + high, key_cols] = dv[h].astype(BF16)
        return carry

    lax.fori_loop(0, blocks, per_key, 0)

    def finish(block, carry):
        src, cols = (block % GROUP, block_cols(block))
        for h in range(heads):
            dx_ref[src, h * HEAD_DIM : (h + 1) * HEAD_DIM, cols] = (dq[h, block] * 0.125).astype(BF16)
        return carry

    lax.fori_loop(0, blocks, finish, 0)


def in_vmem(count):
    return [pl.BlockSpec(memory_space=pltpu.VMEM)] * count


def attend(qkv, spans, seg_col, seg_row):
    heads = qkv.shape[1] // (3 * HEAD_DIM)
    blocks = seg_row.shape[0]
    return pl.pallas_call(
        attend_kernel,
        name="attend",
        out_shape=(
            jax.ShapeDtypeStruct((GROUP, heads * HEAD_DIM, qkv.shape[2]), BF16),
            jax.ShapeDtypeStruct((GROUP, heads * HEAD_DIM, qkv.shape[2]), F32),
            jax.ShapeDtypeStruct((heads, blocks, 1, BLOCK), F32),
        ),
        in_specs=[pl.BlockSpec(memory_space=pltpu.SMEM)] * 2 + in_vmem(3),
        out_specs=in_vmem(3),
        scratch_shapes=[
            pltpu.VMEM((heads, blocks, BLOCK, HEAD_DIM), BF16),
            pltpu.VMEM((heads, HEAD_DIM, BLOCK), F32),
            pltpu.VMEM((heads, 1, BLOCK), F32),
            pltpu.VMEM((heads, 1, BLOCK), F32),
        ],
    )(*spans, qkv, seg_col, seg_row)


def attend_back(qkv, grad_out, out, lse, spans, seg_col, seg_row):
    heads = qkv.shape[1] // (3 * HEAD_DIM)
    blocks = seg_row.shape[0]
    return pl.pallas_call(
        attend_back_kernel,
        name="attend_back",
        out_shape=jax.ShapeDtypeStruct(qkv.shape, BF16),
        in_specs=[pl.BlockSpec(memory_space=pltpu.SMEM)] * 2 + in_vmem(6),
        out_specs=in_vmem(1)[0],
        scratch_shapes=[
            pltpu.VMEM((heads, blocks, BLOCK, HEAD_DIM), BF16),
            pltpu.VMEM((heads, blocks, BLOCK, HEAD_DIM), BF16),
            pltpu.VMEM((heads, blocks, 1, BLOCK), F32),
            pltpu.VMEM((heads, blocks, HEAD_DIM, BLOCK), F32),
            pltpu.VMEM((heads, HEAD_DIM, BLOCK), F32),
            pltpu.VMEM((heads, HEAD_DIM, BLOCK), F32),
        ],
    )(*spans, qkv, grad_out, out, lse, seg_col, seg_row)


def norm_rows(tensor, gain, shift):
    center = tensor - jnp.mean(tensor, axis=-1, keepdims=True)
    inverse = lax.rsqrt(jnp.mean(center * center, axis=-1, keepdims=True) + norm_eps)
    normed = center * inverse
    return (normed * gain + shift, normed, inverse)


def norm_rows_back(grad, normed, inverse, gain):
    scaled = grad * gain
    inner = (
        scaled
        - jnp.mean(scaled, axis=-1, keepdims=True)
        - normed * jnp.mean(scaled * normed, axis=-1, keepdims=True)
    )
    return (inner * inverse, jnp.sum(grad * normed, axis=0), jnp.sum(grad, axis=0))


def fast_forward(hidden, mats, downs, vecs, spans, seg_col, seg_row):
    query_b, value_b, proj_b, attn_g, attn_s, down_b, ffn_g, ffn_s, up_b = vecs
    width = hidden.shape[1]
    hidden_low = hidden.astype(BF16)
    query = (mm(mats[0], hidden_low, 0, 1) + query_b[:, None]).astype(BF16) * BF16(0.125)
    keys = mm(mats[1], hidden_low, 0, 1).astype(BF16)
    values = (mm(mats[2], hidden_low, 0, 1) + value_b[:, None]).astype(BF16)
    share = width // GROUP
    packed = jnp.concatenate(
        [part.reshape(GROUP, share, part.shape[1]) for part in (query, keys, values)], axis=1
    )
    qkv = swap(packed)
    low, out, lse = attend(qkv, spans, seg_col, seg_row)
    context = swap(low).reshape(width, low.shape[2])
    attn_out = mm(context, mats[3], 0, 0) + proj_b
    settled, normed_one, inverse_one = norm_rows(hidden + attn_out, attn_g, attn_s)
    settled_low = settled.astype(BF16)
    ffn_out = down_b
    actives, slopes = ([], [])
    for part in range(len(mats) - 4):
        before = mm(settled_low, mats[4 + part], 1, 0) + up_b[part * width : (part + 1) * width]
        below = 0.5 * (1.0 + lax.erf(before * 0.7071067811865476))
        active = (before * below).astype(BF16)
        slopes.append((below + before * jnp.exp(-0.5 * before * before) * 0.3989422804014327).astype(BF16))
        actives.append(active)
        ffn_out = ffn_out + mm(active, downs[part * width : (part + 1) * width], 1, 0)
    result, normed_two, inverse_two = norm_rows(settled + ffn_out, ffn_g, ffn_s)
    return result, (
        hidden_low, qkv, out, lse, context, normed_one, inverse_one, settled_low,
        actives, slopes, normed_two, inverse_two,
    )


def fast_backward(grad, mats, downs, vecs, saved, spans, seg_col, seg_row):
    query_b, value_b, proj_b, attn_g, attn_s, down_b, ffn_g, ffn_s, up_b = vecs
    (
        hidden_low, qkv, out, lse, context, normed_one, inverse_one, settled_low,
        actives, slopes, normed_two, inverse_two,
    ) = saved
    width = grad.shape[1]
    grad_two, ffn_g_sum, ffn_s_sum = norm_rows_back(grad, normed_two, inverse_two, ffn_g)
    grad_ffn = grad_two.astype(BF16)
    down_b_sum = jnp.sum(grad_ffn.astype(F32), axis=0)
    grad_settled = grad_two
    mat_grads = [None] * len(mats)
    down_grads, up_b_sums = ([], [])
    for part in range(len(actives)):
        rows = slice(part * width, (part + 1) * width)
        grad_before = (mm(grad_ffn, downs[rows], 1, 1) * slopes[part].astype(F32)).astype(BF16)
        down_grads.append(mm(actives[part], grad_ffn, 0, 0).astype(BF16))
        mat_grads[4 + part] = mm(settled_low, grad_before, 0, 0).astype(BF16)
        up_b_sums.append(jnp.sum(grad_before.astype(F32), axis=0))
        grad_settled = grad_settled + mm(grad_before, mats[4 + part], 1, 1)
    grad_one, attn_g_sum, attn_s_sum = norm_rows_back(grad_settled, normed_one, inverse_one, attn_g)
    grad_attn = grad_one.astype(BF16)
    proj_b_sum = jnp.sum(grad_attn.astype(F32), axis=0)
    grad_context = mm(mats[3], grad_attn, 1, 1).astype(BF16)
    mat_grads[3] = mm(context, grad_attn, 1, 0).astype(BF16)
    grad_out = swap(grad_context.reshape(GROUP, width // GROUP, grad_context.shape[1]))
    moved = swap(attend_back(qkv, grad_out, out, lse, spans, seg_col, seg_row))
    share = width // GROUP
    pieces = [
        moved[:, part * share : (part + 1) * share].reshape(width, moved.shape[2]) for part in range(3)
    ]
    grad_hidden = grad_one
    for part in range(3):
        mat_grads[part] = mm(hidden_low, pieces[part], 0, 1).astype(BF16)
        grad_hidden = grad_hidden + mm(pieces[part], mats[part], 0, 1)
    query_b_sum = jnp.sum(pieces[0].astype(F32), axis=1)
    value_b_sum = jnp.sum(pieces[2].astype(F32), axis=1)
    sums = [
        query_b_sum, value_b_sum, proj_b_sum, attn_g_sum, attn_s_sum, down_b_sum, ffn_g_sum, ffn_s_sum,
    ] + up_b_sums
    return grad_hidden, mat_grads, down_grads, sums


def gather_weights(mats, downs):
    return (
        lax.all_gather(mats, "shard", axis=1, tiled=True),
        lax.all_gather(downs, "shard", axis=0, tiled=True),
    )


def scatter_grads(mat_grads, down_grads):
    mats = lax.psum_scatter(jnp.stack(mat_grads), "shard", scatter_dimension=1, tiled=True)
    downs = lax.psum_scatter(
        jnp.concatenate(down_grads, axis=0), "shard", scatter_dimension=0, tiled=True
    )
    return (lax.psum(mats, "rep").astype(F32), lax.psum(downs, "rep").astype(F32))


def on_device_fast(
    inputs, cotangent, segment_ids, memory_slot, memory_table,
    qkv_weight, query_bias, value_bias, proj_weight, proj_bias, attn_gain, attn_shift,
    up_weight, up_bias, down_weight, down_bias, ffn_gain, ffn_shift,
):
    index = lax.axis_index("shard")
    width = inputs.shape[2]
    share = memory_table.shape[1]
    ups = up_weight.shape[2] // width

    weights = []
    for layer in range(LAYERS):
        own = jnp.concatenate([qkv_weight[layer], proj_weight[layer], up_weight[layer]], axis=1)
        own = jnp.stack([own[:, part * width : (part + 1) * width] for part in range(4 + ups)])
        weights.append(gather_weights(own, down_weight[layer]))

    vec_args = (
        query_bias, value_bias, proj_bias, attn_gain, attn_shift, down_bias, ffn_gain, ffn_shift,
    )
    plain = len(vec_args)
    rows = [item[layer][None] for layer in range(LAYERS) for item in vec_args]
    rows += [up_bias[layer].reshape(ups, share) for layer in range(LAYERS)]
    rows.append(memory_table)
    small = gather_small(jnp.concatenate(rows, axis=0)).astype(F32)
    wide = jnp.transpose(small, (1, 0, 2)).reshape(small.shape[1], width)
    vecs = []
    for layer in range(LAYERS):
        start = LAYERS * plain + layer * ups
        vecs.append(
            [wide[layer * plain + item] for item in range(plain)]
            + [small[:, start : start + ups].reshape(ups * width)]
        )
    table = wide[LAYERS * (plain + ups) :].astype(BF16)

    segs = jnp.where(index < GROUP, segment_ids[0], segment_ids[1])
    tiles = segs.reshape(-1, BLOCK)
    first, last = (tiles[:, 0], tiles[:, -1])
    spans = (
        jnp.sum((last[None, :] < first[:, None]).astype(jnp.int32), axis=1),
        jnp.sum((first[None, :] <= last[:, None]).astype(jnp.int32), axis=1),
    )
    seg_row = tiles[:, None, :]
    seg_col = jnp.broadcast_to(segs[:, None], (segs.shape[0], 128))

    slots = to_groups(memory_slot[..., None], index)[:, 0]
    slot_hot = slots[:, None] == jnp.arange(MEMS, dtype=jnp.int32)
    hidden = to_groups(inputs, index).astype(F32) + mm(slot_hot.astype(BF16), table, 1, 0)
    saved = []
    for layer in range(LAYERS):
        mats, downs = weights[layer]
        hidden, state = fast_forward(hidden, mats, downs, vecs[layer], spans, seg_col, seg_row)
        saved.append(state)
    layer_output = from_groups(hidden, index)

    grad = to_groups(cotangent, index).astype(F32)
    sums, shares = ([None] * LAYERS, [None] * LAYERS)
    for layer in range(LAYERS - 1, -1, -1):
        mats, downs = weights[layer]
        grad, mat_grads, down_grads, sums[layer] = fast_backward(
            grad, mats, downs, vecs[layer], saved[layer], spans, seg_col, seg_row
        )
        shares[layer] = scatter_grads(mat_grads, down_grads)
    input_grad = from_groups(grad, index)
    memory_sum = lax.dot_general(
        slot_hot.astype(F32), grad, (((0,), (0,)), ((), ())), precision=lax.Precision.HIGHEST
    )
    flat = jnp.concatenate([jnp.stack(sums[layer]) for layer in range(LAYERS)] + [memory_sum], axis=0)
    flat = sum_small(flat)
    per = plain + ups
    own = lax.dynamic_slice_in_dim(flat, index * share, share, 1)
    vec_grads = [
        jnp.stack([own[layer * per + item] for layer in range(LAYERS)]) for item in range(plain)
    ]
    up_sums = jnp.stack([flat[layer * per + plain : (layer + 1) * per].reshape(-1) for layer in range(LAYERS)])
    upbias_grad = lax.dynamic_slice_in_dim(up_sums, index * share * ups, share * ups, 1)
    memory_grad = own[LAYERS * per :]

    def wide_grad(low, high):
        return jnp.stack(
            [jnp.concatenate(list(shares[layer][0][low:high]), axis=1) for layer in range(LAYERS)]
        )

    return (
        layer_output,
        input_grad,
        memory_grad,
        wide_grad(0, 3),
        vec_grads[0],
        vec_grads[1],
        wide_grad(3, 4),
        vec_grads[2],
        vec_grads[3],
        vec_grads[4],
        wide_grad(4, 4 + ups),
        upbias_grad,
        jnp.stack([shares[layer][1] for layer in range(LAYERS)]),
        vec_grads[5],
        vec_grads[6],
        vec_grads[7],
    )


def fast_fits(mesh):
    return mesh.shape["shard"] == 2 * GROUP and mesh.shape["rep"] == 4


def solution(mesh):
    return jax.shard_map(
        on_device_fast if fast_fits(mesh) else on_device,
        mesh=mesh,
        in_specs=(
            P(None, ("rep", "shard"), None),
            P(None, ("rep", "shard"), None),
            P(None, "rep"),
            P(None, ("rep", "shard")),
            P(None, "shard"),
            P(None, "shard", None),
            P(None, "shard"),
            P(None, "shard"),
            P(None, "shard", None),
            P(None, "shard"),
            P(None, "shard"),
            P(None, "shard"),
            P(None, "shard", None),
            P(None, "shard"),
            P(None, "shard", None),
            P(None, "shard"),
            P(None, "shard"),
            P(None, "shard"),
        ),
        out_specs=(
            P(None, ("rep", "shard"), None),
            P(None, ("rep", "shard"), None),
            P(None, "shard"),
            P(None, "shard", None),
            P(None, "shard"),
            P(None, "shard"),
            P(None, "shard", None),
            P(None, "shard"),
            P(None, "shard"),
            P(None, "shard"),
            P(None, "shard", None),
            P(None, "shard"),
            P(None, "shard", None),
            P(None, "shard"),
            P(None, "shard"),
            P(None, "shard"),
        ),
        check_vma=False,
    )
```

```python
import jax
import jax.numpy as jnp
from jax import lax
from jax.experimental import pallas as pl
from jax.experimental.pallas import tpu as pltpu
from jax.sharding import PartitionSpec as P

HEADS = 12
HEAD_DIM = 64
LAYERS = 2
MEMS = 20
REACH = 4


norm_eps = 1e-12
masked_score = -1e30


def passed_along(block, axis, distance):
    devices = range(lax.axis_size(axis))
    route = [(i - distance, i) for i in devices if i - distance in devices]
    return lax.ppermute(block, axis, route)


def layer_norm(tensor, norm_gain, norm_shift):
    center = tensor - jnp.mean(tensor, axis=-1, keepdims=True)
    inverse = lax.rsqrt(jnp.mean(center * center, axis=-1, keepdims=True) + norm_eps)
    normed = center * inverse
    return (normed * norm_gain + norm_shift, normed, inverse)


def norm_backward(grad_out, normed, inverse, norm_gain):
    scaled = grad_out * norm_gain
    inner_term = (
        scaled
        - jnp.mean(scaled, axis=-1, keepdims=True)
        - normed * jnp.mean(scaled * normed, axis=-1, keepdims=True)
    )
    return (
        inner_term * inverse,
        jnp.sum(grad_out * normed, axis=(0, 1)),
        jnp.sum(grad_out, axis=(0, 1)),
    )


def gelu_exact(tensor):
    return jax.nn.gelu(tensor, approximate=False)


def split_heads(tensor):
    return tensor.reshape(tensor.shape[0], tensor.shape[1], HEADS, HEAD_DIM)


def merge_heads(tensor):
    return tensor.reshape(tensor.shape[0], tensor.shape[1], HEADS * HEAD_DIM)


def product(left_side, right_side):
    return jnp.einsum("btd,de->bte", left_side, right_side, preferred_element_type=jnp.float32)


def product_back(left_side, right_side):
    return jnp.einsum("bte,de->btd", left_side, right_side, preferred_element_type=jnp.float32)


def weight_grad(left_side, right_side):
    return jnp.einsum("btd,bte->de", left_side, right_side, preferred_element_type=jnp.float32)


def token_sum(tensor):
    return jnp.sum(tensor.astype(jnp.float32), axis=(0, 1))


def piece_mask(segment_ids, seg_here, my_index, shards, row_count, offset):
    target = my_index + offset
    inside = jnp.logical_and(target >= 0, target < shards)
    start_row = jnp.clip(target, 0, shards - 1) * row_count
    seg_there = lax.dynamic_slice_in_dim(segment_ids, start_row, row_count, 1)
    key_mask = jnp.logical_and(seg_here[:, None, :, None] == seg_there[:, None, None, :], inside)
    return (key_mask, jnp.any(key_mask))


def scaled_scores(query_heads, key_part, key_mask):
    scores = (
        jnp.einsum(
            "bqhe,bkhe->bhqk",
            query_heads,
            split_heads(key_part),
            preferred_element_type=jnp.float32,
        )
        * 0.125
    )
    return jnp.where(key_mask, scores, masked_score)


def stats_update(carry_in, query_heads, key_part, key_mask):
    old_max, old_sum = carry_in
    scores = scaled_scores(query_heads, key_part, key_mask)
    new_max = jnp.maximum(old_max, jnp.max(scores, axis=-1))
    fresh = jnp.sum(jnp.where(key_mask, jnp.exp(scores - new_max[..., None]), 0.0), axis=-1)
    return (new_max, old_sum * jnp.exp(old_max - new_max) + fresh)


def stats_keep(carry_in, query_heads, key_part, key_mask):
    return carry_in


def mix_update(context, query_heads, key_part, value_part, key_mask, log_sum):
    scores = scaled_scores(query_heads, key_part, key_mask)
    soft_probs = jnp.where(key_mask, jnp.exp(scores - log_sum[..., None]), 0.0).astype(jnp.bfloat16)
    return context + jnp.einsum(
        "bhqk,bkhe->bqhe", soft_probs, split_heads(value_part), preferred_element_type=jnp.float32
    )


def mix_keep(context, query_heads, key_part, value_part, key_mask, log_sum):
    return context


def piece_update(
    grad_query, query_heads, grad_heads, key_part, value_part, key_mask, log_sum, row_delta
):
    scores = scaled_scores(query_heads, key_part, key_mask)
    soft_probs = jnp.where(key_mask, jnp.exp(scores - log_sum[..., None]), 0.0)
    grad_probs = jnp.einsum(
        "bqhe,bkhe->bhqk", grad_heads, split_heads(value_part), preferred_element_type=jnp.float32
    )
    grad_scores = (soft_probs * (grad_probs - row_delta[..., None])).astype(jnp.bfloat16)
    grad_query = grad_query + jnp.einsum(
        "bhqk,bkhe->bqhe", grad_scores, split_heads(key_part), preferred_element_type=jnp.float32
    )
    key_grad = jnp.einsum(
        "bhqk,bqhe->bkhe", grad_scores, query_heads, preferred_element_type=jnp.float32
    )
    value_grad = jnp.einsum(
        "bhqk,bqhe->bkhe",
        soft_probs.astype(jnp.bfloat16),
        grad_heads,
        preferred_element_type=jnp.float32,
    )
    return (grad_query, merge_heads(key_grad), merge_heads(value_grad))


def piece_skip(
    grad_query, query_heads, grad_heads, key_part, value_part, key_mask, log_sum, row_delta
):
    empty = jnp.zeros(key_part.shape, jnp.float32)
    return (grad_query, empty, empty)


def attend_forward(query_rows, key_rows, value_rows, offsets, key_masks):
    micro_count, row_count = (query_rows.shape[0], query_rows.shape[1])
    query_heads = split_heads(query_rows)
    pieces = [(key_rows, value_rows)]
    for offset in offsets:
        pieces.append(passed_along((key_rows, value_rows), "shard", -offset))
    row_max = jnp.full((micro_count, HEADS, row_count), masked_score, jnp.float32)
    row_sum = jnp.zeros((micro_count, HEADS, row_count), jnp.float32)
    for (key_part, value_part), (key_mask, is_live) in zip(pieces, key_masks):
        row_max, row_sum = lax.cond(
            is_live, stats_update, stats_keep, (row_max, row_sum), query_heads, key_part, key_mask
        )
    log_sum = row_max + jnp.log(row_sum)
    context = jnp.zeros((micro_count, row_count, HEADS, HEAD_DIM), jnp.float32)
    for (key_part, value_part), (key_mask, is_live) in zip(pieces, key_masks):
        context = lax.cond(
            is_live,
            mix_update,
            mix_keep,
            context,
            query_heads,
            key_part,
            value_part,
            key_mask,
            log_sum,
        )
    return (merge_heads(context), log_sum, pieces)


def attend_backward(query_rows, grad_context, context, log_sum, pieces, key_masks, offsets):
    query_heads = split_heads(query_rows)
    grad_heads = split_heads(grad_context)
    row_delta = jnp.transpose(
        jnp.sum(split_heads(grad_context.astype(jnp.float32) * context), axis=-1), (0, 2, 1)
    )
    grad_query = jnp.zeros(query_heads.shape, jnp.float32)
    own_keys = jnp.zeros(query_rows.shape, jnp.float32)
    own_values = jnp.zeros(query_rows.shape, jnp.float32)
    for index_num in range(len(pieces)):
        key_part, value_part = pieces[index_num]
        key_mask, is_live = key_masks[index_num]
        grad_query, key_grad, value_grad = lax.cond(
            is_live,
            piece_update,
            piece_skip,
            grad_query,
            query_heads,
            grad_heads,
            key_part,
            value_part,
            key_mask,
            log_sum,
            row_delta,
        )
        if index_num == 0:
            own_keys = key_grad
            own_values = value_grad
        else:
            back_keys, back_values = (
                passed_along(key_grad.astype(jnp.bfloat16), "shard", offsets[index_num - 1]).astype(
                    key_grad.dtype
                ),
                passed_along(
                    value_grad.astype(jnp.bfloat16), "shard", offsets[index_num - 1]
                ).astype(value_grad.dtype),
            )
            own_keys = own_keys + back_keys
            own_values = own_values + back_values
    query_out = (merge_heads(grad_query) * 0.125).astype(jnp.bfloat16)
    return (query_out, (own_keys * 0.125).astype(jnp.bfloat16), own_values.astype(jnp.bfloat16))


def layer_forward(hidden, weights, offsets, key_masks):
    (
        qkv_w,
        query_b,
        value_b,
        proj_w,
        proj_b,
        attn_g,
        attn_s,
        up_w,
        up_b,
        down_w,
        down_b,
        ffn_g,
        ffn_s,
    ) = weights
    model_width = qkv_w.shape[0]
    hidden_low = hidden.astype(jnp.bfloat16)
    mixed_all = product(hidden_low, qkv_w)
    query_rows = (mixed_all[..., :model_width] + query_b.astype(jnp.float32)).astype(jnp.bfloat16)
    key_rows = mixed_all[..., model_width : 2 * model_width].astype(jnp.bfloat16)
    value_rows = (mixed_all[..., 2 * model_width :] + value_b.astype(jnp.float32)).astype(
        jnp.bfloat16
    )
    context, log_sum, pieces = attend_forward(query_rows, key_rows, value_rows, offsets, key_masks)
    context_low = context.astype(jnp.bfloat16)
    attn_out = product(context_low, proj_w) + proj_b.astype(jnp.float32)
    settled, normed_one, inverse_one = layer_norm(
        hidden + attn_out, attn_g.astype(jnp.float32), attn_s.astype(jnp.float32)
    )
    settled_low = settled.astype(jnp.bfloat16)
    before = product(settled_low, up_w) + up_b.astype(jnp.float32)
    active = gelu_exact(before).astype(jnp.bfloat16)
    ffn_out = product(active, down_w) + down_b.astype(jnp.float32)
    result, normed_two, inverse_two = layer_norm(
        settled + ffn_out, ffn_g.astype(jnp.float32), ffn_s.astype(jnp.float32)
    )
    saved_state = (
        hidden_low,
        query_rows,
        key_rows,
        value_rows,
        context,
        log_sum,
        pieces,
        context_low,
        normed_one,
        inverse_one,
        settled_low,
        before,
        active,
        normed_two,
        inverse_two,
    )
    return (result, saved_state)


def layer_backward(grad_out, weights, saved_state, offsets, key_masks):
    (
        qkv_w,
        query_b,
        value_b,
        proj_w,
        proj_b,
        attn_g,
        attn_s,
        up_w,
        up_b,
        down_w,
        down_b,
        ffn_g,
        ffn_s,
    ) = weights
    (
        hidden_low,
        query_rows,
        key_rows,
        value_rows,
        context,
        log_sum,
        pieces,
        context_low,
        normed_one,
        inverse_one,
        settled_low,
        before,
        active,
        normed_two,
        inverse_two,
    ) = saved_state
    grad_two, ffngain_part, ffnshift_part = norm_backward(
        grad_out, normed_two, inverse_two, ffn_g.astype(jnp.float32)
    )
    grad_ffn = grad_two.astype(jnp.bfloat16)
    downweight_part = weight_grad(active, grad_ffn)
    downbias_part = token_sum(grad_ffn)
    grad_active = product_back(grad_ffn, down_w)
    gelu_pull = jax.vjp(gelu_exact, before)[1]
    grad_before = gelu_pull(grad_active)[0].astype(jnp.bfloat16)
    upweight_part = weight_grad(settled_low, grad_before)
    upbias_part = token_sum(grad_before)
    grad_settled = grad_two + product_back(grad_before, up_w)
    grad_one, attngain_part, attnshift_part = norm_backward(
        grad_settled, normed_one, inverse_one, attn_g.astype(jnp.float32)
    )
    grad_attn = grad_one.astype(jnp.bfloat16)
    proj_part = weight_grad(context_low, grad_attn)
    projbias_part = token_sum(grad_attn)
    grad_context = product_back(grad_attn, proj_w).astype(jnp.bfloat16)
    pieces = [(key_rows, value_rows)]
    for offset in offsets:
        pieces.append(passed_along((key_rows, value_rows), "shard", -offset))
    grad_query, grad_keys, grad_values = attend_backward(
        query_rows, grad_context, context, log_sum, pieces, key_masks, offsets
    )
    grad_mixed = jnp.concatenate([grad_query, grad_keys, grad_values], axis=-1)
    qkv_part = weight_grad(hidden_low, grad_mixed)
    querybias_part = token_sum(grad_query)
    valuebias_part = token_sum(grad_values)
    grad_hidden = grad_one + product_back(grad_mixed, qkv_w)
    layer_grads = (
        qkv_part,
        querybias_part,
        valuebias_part,
        proj_part,
        projbias_part,
        attngain_part,
        attnshift_part,
        upweight_part,
        upbias_part,
        downweight_part,
        downbias_part,
        ffngain_part,
        ffnshift_part,
    )
    return (grad_hidden, layer_grads)


def on_device(
    inputs,
    cotangent,
    segment_ids,
    memory_slot,
    memory_table,
    qkv_weight,
    query_bias,
    value_bias,
    proj_weight,
    proj_bias,
    attn_gain,
    attn_shift,
    up_weight,
    up_bias,
    down_weight,
    down_bias,
    ffn_gain,
    ffn_shift,
):
    shards = lax.axis_size("shard")
    my_index = lax.axis_index("shard")
    row_count = inputs.shape[1]
    reach_out = min(REACH, shards - 1)
    offsets = [offset for offset in range(-reach_out, reach_out + 1) if offset != 0]
    seg_here = lax.dynamic_slice_in_dim(segment_ids, my_index * row_count, row_count, 1)
    key_masks = [piece_mask(segment_ids, seg_here, my_index, shards, row_count, 0)]
    for offset in offsets:
        key_masks.append(piece_mask(segment_ids, seg_here, my_index, shards, row_count, offset))
    gathered = (
        lax.all_gather(qkv_weight, "shard", axis=1, tiled=True),
        lax.all_gather(query_bias, "shard", axis=1, tiled=True),
        lax.all_gather(value_bias, "shard", axis=1, tiled=True),
        lax.all_gather(proj_weight, "shard", axis=1, tiled=True),
        lax.all_gather(proj_bias, "shard", axis=1, tiled=True),
        lax.all_gather(attn_gain, "shard", axis=1, tiled=True),
        lax.all_gather(attn_shift, "shard", axis=1, tiled=True),
        lax.all_gather(up_weight, "shard", axis=1, tiled=True),
        lax.all_gather(up_bias, "shard", axis=1, tiled=True),
        lax.all_gather(down_weight, "shard", axis=1, tiled=True),
        lax.all_gather(down_bias, "shard", axis=1, tiled=True),
        lax.all_gather(ffn_gain, "shard", axis=1, tiled=True),
        lax.all_gather(ffn_shift, "shard", axis=1, tiled=True),
        lax.all_gather(memory_table, "shard", axis=1, tiled=True),
    )
    slot_range = jnp.arange(MEMS, dtype=jnp.int32)
    slot_hot = (memory_slot[..., None] == slot_range).astype(jnp.float32)
    hidden = inputs.astype(jnp.float32) + jnp.einsum(
        "btm,md->btd", slot_hot, gathered[13].astype(jnp.float32), precision=lax.Precision.HIGHEST
    )
    saved_list = []
    for layer_num in range(LAYERS):
        weights = tuple((item[layer_num] for item in gathered[:13]))
        hidden, saved_state = layer_forward(hidden, weights, offsets, key_masks)
        saved_list.append(saved_state)
    regathered = (
        lax.all_gather(qkv_weight, "shard", axis=1, tiled=True),
        lax.all_gather(query_bias, "shard", axis=1, tiled=True),
        lax.all_gather(value_bias, "shard", axis=1, tiled=True),
        lax.all_gather(proj_weight, "shard", axis=1, tiled=True),
        lax.all_gather(proj_bias, "shard", axis=1, tiled=True),
        lax.all_gather(attn_gain, "shard", axis=1, tiled=True),
        lax.all_gather(attn_shift, "shard", axis=1, tiled=True),
        lax.all_gather(up_weight, "shard", axis=1, tiled=True),
        lax.all_gather(up_bias, "shard", axis=1, tiled=True),
        lax.all_gather(down_weight, "shard", axis=1, tiled=True),
        lax.all_gather(down_bias, "shard", axis=1, tiled=True),
        lax.all_gather(ffn_gain, "shard", axis=1, tiled=True),
        lax.all_gather(ffn_shift, "shard", axis=1, tiled=True),
    )
    grad_hidden = cotangent.astype(jnp.float32)
    grads_by_layer = [None] * LAYERS
    for layer_num in range(LAYERS - 1, -1, -1):
        weights = tuple((item[layer_num] for item in regathered))
        grad_hidden, layer_grads = layer_backward(
            grad_hidden, weights, saved_list[layer_num], offsets, key_masks
        )
        grads_by_layer[layer_num] = layer_grads
    memory_full = jnp.einsum("btm,btd->md", slot_hot, grad_hidden, precision=lax.Precision.HIGHEST)
    stacked = [
        jnp.stack([grads_by_layer[layer_num][member] for layer_num in range(LAYERS)])
        for member in range(13)
    ]
    shares = (
        lax.psum_scatter(stacked[0], "shard", scatter_dimension=1, tiled=True),
        lax.psum_scatter(stacked[1], "shard", scatter_dimension=1, tiled=True),
        lax.psum_scatter(stacked[2], "shard", scatter_dimension=1, tiled=True),
        lax.psum_scatter(stacked[3], "shard", scatter_dimension=1, tiled=True),
        lax.psum_scatter(stacked[4], "shard", scatter_dimension=1, tiled=True),
        lax.psum_scatter(stacked[5], "shard", scatter_dimension=1, tiled=True),
        lax.psum_scatter(stacked[6], "shard", scatter_dimension=1, tiled=True),
        lax.psum_scatter(stacked[7], "shard", scatter_dimension=1, tiled=True),
        lax.psum_scatter(stacked[8], "shard", scatter_dimension=1, tiled=True),
        lax.psum_scatter(stacked[9], "shard", scatter_dimension=1, tiled=True),
        lax.psum_scatter(stacked[10], "shard", scatter_dimension=1, tiled=True),
        lax.psum_scatter(stacked[11], "shard", scatter_dimension=1, tiled=True),
        lax.psum_scatter(stacked[12], "shard", scatter_dimension=1, tiled=True),
        lax.psum_scatter(memory_full, "shard", scatter_dimension=1, tiled=True),
    )
    totals = (
        lax.psum(shares[0].astype(jnp.bfloat16), "rep").astype(jnp.float32),
        lax.psum(shares[1].astype(jnp.bfloat16), "rep").astype(jnp.float32),
        lax.psum(shares[2].astype(jnp.bfloat16), "rep").astype(jnp.float32),
        lax.psum(shares[3].astype(jnp.bfloat16), "rep").astype(jnp.float32),
        lax.psum(shares[4].astype(jnp.bfloat16), "rep").astype(jnp.float32),
        lax.psum(shares[5].astype(jnp.bfloat16), "rep").astype(jnp.float32),
        lax.psum(shares[6].astype(jnp.bfloat16), "rep").astype(jnp.float32),
        lax.psum(shares[7].astype(jnp.bfloat16), "rep").astype(jnp.float32),
        lax.psum(shares[8].astype(jnp.bfloat16), "rep").astype(jnp.float32),
        lax.psum(shares[9].astype(jnp.bfloat16), "rep").astype(jnp.float32),
        lax.psum(shares[10].astype(jnp.bfloat16), "rep").astype(jnp.float32),
        lax.psum(shares[11].astype(jnp.bfloat16), "rep").astype(jnp.float32),
        lax.psum(shares[12].astype(jnp.bfloat16), "rep").astype(jnp.float32),
        lax.psum(shares[13].astype(jnp.bfloat16), "rep").astype(jnp.float32),
    )
    return (
        hidden,
        grad_hidden,
        totals[13],
        totals[0],
        totals[1],
        totals[2],
        totals[3],
        totals[4],
        totals[5],
        totals[6],
        totals[7],
        totals[8],
        totals[9],
        totals[10],
        totals[11],
        totals[12],
    )


BLOCK = 256
GROUP = 4
BF16 = jnp.bfloat16
F32 = jnp.float32


def mm(left, right, left_dim, right_dim):
    return lax.dot_general(
        left, right, (((left_dim,), (right_dim,)), ((), ())), preferred_element_type=F32
    )


def exchange(tensor, axis, mask):
    count = lax.axis_size(axis)
    return lax.ppermute(tensor, axis, [(i, i ^ mask) for i in range(count)])


def ordered(first_is_mine, mine, other):
    return jnp.stack(
        [jnp.where(first_is_mine, mine, other), jnp.where(first_is_mine, other, mine)]
    )


def gather_small(tensor):
    index = lax.axis_index("shard")
    for bit in range(3):
        other = exchange(tensor, "shard", 1 << bit)
        tensor = ordered((index >> bit) & 1 == 0, tensor, other)
    return tensor.reshape((8,) + tensor.shape[3:])


def sum_small(tensor):
    for axis, bits in (("rep", 2), ("shard", 3)):
        for bit in range(bits):
            tensor = tensor + exchange(tensor, axis, 1 << bit)
    return tensor


def to_groups(tensor, index):
    low = index < GROUP
    mine = jnp.where(low, tensor[0], tensor[1])
    other = exchange(jnp.where(low, tensor[1], tensor[0]), "shard", GROUP)
    both = ordered(low, mine, other)
    return both.reshape((2 * tensor.shape[1],) + tensor.shape[2:])


def from_groups(tensor, index):
    low = index < GROUP
    half = tensor.shape[0] // 2
    mine = jnp.where(low, tensor[:half], tensor[half:])
    other = exchange(
        jnp.where(low, tensor[half:], tensor[:half]).astype(BF16), "shard", GROUP
    ).astype(tensor.dtype)
    return ordered(low, mine, other)


def swap(tensor):
    shape = tensor.shape
    flat = tensor.reshape((shape[0] * shape[1],) + shape[2:])
    moved = lax.all_to_all(
        flat, "shard", 0, 0, axis_index_groups=[[0, 1, 2, 3], [4, 5, 6, 7]], tiled=True
    )
    return moved.reshape(shape)


def block_cols(block):
    half = block // GROUP
    return pl.ds(pl.multiple_of(half * BLOCK, BLOCK), BLOCK)


def flipped(tensor):
    return jnp.transpose(tensor.astype(F32)).astype(BF16)


def pair_mask(seg_col, seg_row, keys, queries):
    col = seg_col[pl.ds(pl.multiple_of(keys * BLOCK, BLOCK), BLOCK), :]
    col = jnp.concatenate([col] * (BLOCK // 128), axis=1)
    return col == seg_row[queries]


def attend_kernel(
    lo_ref, hi_ref, x_ref, seg_col, seg_row, low_ref, out_ref, lse_ref, keys_nat, acc, top, total,
):
    heads = x_ref.shape[1] // (3 * HEAD_DIM)
    width = heads * HEAD_DIM
    blocks = seg_row.shape[0]

    def flip(block, carry):
        for h in range(heads):
            keys_nat[h, block] = flipped(
                x_ref[block % GROUP, width + h * HEAD_DIM : width + (h + 1) * HEAD_DIM, block_cols(block)]
            )
        return carry

    lax.fori_loop(0, blocks, flip, 0)

    def per_query(i, carry):
        src, cols = (i % GROUP, block_cols(i))
        for h in range(heads):
            top[h] = jnp.full(top.shape[1:], masked_score, F32)
            total[h] = jnp.zeros(total.shape[1:], F32)
            acc[h] = jnp.zeros(acc.shape[1:], F32)

        def per_key(j, inner):
            allowed = pair_mask(seg_col, seg_row, j, i)
            for h in range(heads):
                query = x_ref[src, h * HEAD_DIM : (h + 1) * HEAD_DIM, cols]
                value = x_ref[
                    j % GROUP, 2 * width + h * HEAD_DIM : 2 * width + (h + 1) * HEAD_DIM, block_cols(j)
                ]
                scores = jnp.where(allowed, mm(keys_nat[h, j], query, 1, 0), masked_score)
                old = top[h]
                new = jnp.maximum(old, jnp.max(scores, axis=0, keepdims=True))
                raised = jnp.exp(scores - new)
                fade = jnp.exp(old - new)
                top[h] = new
                total[h] = total[h] * fade + jnp.sum(raised, axis=0, keepdims=True)
                acc[h] = acc[h] * fade + mm(value, raised.astype(BF16), 1, 0)
            return inner

        lax.fori_loop(lo_ref[i], hi_ref[i], per_key, 0)
        for h in range(heads):
            out = acc[h] / total[h]
            out_ref[src, h * HEAD_DIM : (h + 1) * HEAD_DIM, cols] = out
            low_ref[src, h * HEAD_DIM : (h + 1) * HEAD_DIM, cols] = out.astype(BF16)
            lse_ref[h, i] = top[h] + jnp.log(total[h])
        return carry

    lax.fori_loop(0, blocks, per_query, 0)


def attend_back_kernel(
    lo_ref, hi_ref, x_ref, go_ref, out_ref, lse_ref, seg_col, seg_row, dx_ref,
    keys_nat, values_nat, delta, dq, dk, dv,
):
    heads = x_ref.shape[1] // (3 * HEAD_DIM)
    width = heads * HEAD_DIM
    blocks = seg_row.shape[0]

    def prepare(block, carry):
        src, cols = (block % GROUP, block_cols(block))
        for h in range(heads):
            low, high = (h * HEAD_DIM, (h + 1) * HEAD_DIM)
            keys_nat[h, block] = flipped(x_ref[src, width + low : width + high, cols])
            values_nat[h, block] = flipped(x_ref[src, 2 * width + low : 2 * width + high, cols])
            delta[h, block] = jnp.sum(
                go_ref[src, low:high, cols].astype(F32) * out_ref[src, low:high, cols],
                axis=0,
                keepdims=True,
            )
            dq[h, block] = jnp.zeros(dq.shape[2:], F32)
        return carry

    lax.fori_loop(0, blocks, prepare, 0)

    def per_key(j, carry):
        key_src, key_cols = (j % GROUP, block_cols(j))
        for h in range(heads):
            dk[h] = jnp.zeros(dk.shape[1:], F32)
            dv[h] = jnp.zeros(dv.shape[1:], F32)

        def per_query(i, inner):
            src, cols = (i % GROUP, block_cols(i))
            allowed = pair_mask(seg_col, seg_row, j, i)
            for h in range(heads):
                low, high = (h * HEAD_DIM, (h + 1) * HEAD_DIM)
                query = x_ref[src, low:high, cols]
                grad = go_ref[src, low:high, cols]
                scores = jnp.where(allowed, mm(keys_nat[h, j], query, 1, 0), masked_score)
                probs = jnp.exp(scores - lse_ref[h, i])
                grad_probs = mm(values_nat[h, j], grad, 1, 0)
                grad_scores = (probs * (grad_probs - delta[h, i])).astype(BF16)
                dv[h] += mm(grad, probs.astype(BF16), 1, 1)
                dk[h] += mm(query, grad_scores, 1, 1)
                dq[h, i] += mm(x_ref[key_src, width + low : width + high, key_cols], grad_scores, 1, 0)
            return inner

        lax.fori_loop(lo_ref[j], hi_ref[j], per_query, 0)
        for h in range(heads):
            low, high = (h * HEAD_DIM, (h + 1) * HEAD_DIM)
            dx_ref[key_src, width + low : width + high, key_cols] = dk[h].astype(BF16)
            dx_ref[key_src, 2 * width + low : 2 * width + high, key_cols] = dv[h].astype(BF16)
        return carry

    lax.fori_loop(0, blocks, per_key, 0)

    def finish(block, carry):
        src, cols = (block % GROUP, block_cols(block))
        for h in range(heads):
            dx_ref[src, h * HEAD_DIM : (h + 1) * HEAD_DIM, cols] = (dq[h, block] * 0.125).astype(BF16)
        return carry

    lax.fori_loop(0, blocks, finish, 0)


def in_vmem(count):
    return [pl.BlockSpec(memory_space=pltpu.VMEM)] * count


def attend(qkv, spans, seg_col, seg_row):
    heads = qkv.shape[1] // (3 * HEAD_DIM)
    blocks = seg_row.shape[0]
    return pl.pallas_call(
        attend_kernel,
        name="attend",
        out_shape=(
            jax.ShapeDtypeStruct((GROUP, heads * HEAD_DIM, qkv.shape[2]), BF16),
            jax.ShapeDtypeStruct((GROUP, heads * HEAD_DIM, qkv.shape[2]), F32),
            jax.ShapeDtypeStruct((heads, blocks, 1, BLOCK), F32),
        ),
        in_specs=[pl.BlockSpec(memory_space=pltpu.SMEM)] * 2 + in_vmem(3),
        out_specs=in_vmem(3),
        scratch_shapes=[
            pltpu.VMEM((heads, blocks, BLOCK, HEAD_DIM), BF16),
            pltpu.VMEM((heads, HEAD_DIM, BLOCK), F32),
            pltpu.VMEM((heads, 1, BLOCK), F32),
            pltpu.VMEM((heads, 1, BLOCK), F32),
        ],
    )(*spans, qkv, seg_col, seg_row)


def attend_back(qkv, grad_out, out, lse, spans, seg_col, seg_row):
    heads = qkv.shape[1] // (3 * HEAD_DIM)
    blocks = seg_row.shape[0]
    return pl.pallas_call(
        attend_back_kernel,
        name="attend_back",
        out_shape=jax.ShapeDtypeStruct(qkv.shape, BF16),
        in_specs=[pl.BlockSpec(memory_space=pltpu.SMEM)] * 2 + in_vmem(6),
        out_specs=in_vmem(1)[0],
        scratch_shapes=[
            pltpu.VMEM((heads, blocks, BLOCK, HEAD_DIM), BF16),
            pltpu.VMEM((heads, blocks, BLOCK, HEAD_DIM), BF16),
            pltpu.VMEM((heads, blocks, 1, BLOCK), F32),
            pltpu.VMEM((heads, blocks, HEAD_DIM, BLOCK), F32),
            pltpu.VMEM((heads, HEAD_DIM, BLOCK), F32),
            pltpu.VMEM((heads, HEAD_DIM, BLOCK), F32),
        ],
    )(*spans, qkv, grad_out, out, lse, seg_col, seg_row)


def norm_rows(tensor, gain, shift):
    center = tensor - jnp.mean(tensor, axis=-1, keepdims=True)
    inverse = lax.rsqrt(jnp.mean(center * center, axis=-1, keepdims=True) + norm_eps)
    normed = center * inverse
    return (normed * gain + shift, normed, inverse)


def norm_rows_back(grad, normed, inverse, gain):
    scaled = grad * gain
    inner = (
        scaled
        - jnp.mean(scaled, axis=-1, keepdims=True)
        - normed * jnp.mean(scaled * normed, axis=-1, keepdims=True)
    )
    return (inner * inverse, jnp.sum(grad * normed, axis=0), jnp.sum(grad, axis=0))


def fast_forward(hidden, mats, downs, vecs, spans, seg_col, seg_row):
    query_b, value_b, proj_b, attn_g, attn_s, down_b, ffn_g, ffn_s, up_b = vecs
    width = hidden.shape[1]
    hidden_low = hidden.astype(BF16)
    query = (mm(mats[0], hidden_low, 0, 1) + query_b[:, None]).astype(BF16) * BF16(0.125)
    keys = mm(mats[1], hidden_low, 0, 1).astype(BF16)
    values = (mm(mats[2], hidden_low, 0, 1) + value_b[:, None]).astype(BF16)
    share = width // GROUP
    packed = jnp.concatenate(
        [part.reshape(GROUP, share, part.shape[1]) for part in (query, keys, values)], axis=1
    )
    qkv = swap(packed)
    low, out, lse = attend(qkv, spans, seg_col, seg_row)
    context = swap(low).reshape(width, low.shape[2])
    attn_out = mm(context, mats[3], 0, 0) + proj_b
    settled, normed_one, inverse_one = norm_rows(hidden + attn_out, attn_g, attn_s)
    settled_low = settled.astype(BF16)
    ffn_out = down_b
    actives, slopes = ([], [])
    for part in range(len(mats) - 4):
        before = mm(settled_low, mats[4 + part], 1, 0) + up_b[part * width : (part + 1) * width]
        below = 0.5 * (1.0 + lax.erf(before * 0.7071067811865476))
        active = (before * below).astype(BF16)
        slopes.append((below + before * jnp.exp(-0.5 * before * before) * 0.3989422804014327).astype(BF16))
        actives.append(active)
        ffn_out = ffn_out + mm(active, downs[part * width : (part + 1) * width], 1, 0)
    result, normed_two, inverse_two = norm_rows(settled + ffn_out, ffn_g, ffn_s)
    return result, (
        hidden_low, qkv, out, lse, context, normed_one, inverse_one, settled_low,
        actives, slopes, normed_two, inverse_two,
    )


def fast_backward(grad, mats, downs, vecs, saved, spans, seg_col, seg_row):
    query_b, value_b, proj_b, attn_g, attn_s, down_b, ffn_g, ffn_s, up_b = vecs
    (
        hidden_low, qkv, out, lse, context, normed_one, inverse_one, settled_low,
        actives, slopes, normed_two, inverse_two,
    ) = saved
    width = grad.shape[1]
    grad_two, ffn_g_sum, ffn_s_sum = norm_rows_back(grad, normed_two, inverse_two, ffn_g)
    grad_ffn = grad_two.astype(BF16)
    down_b_sum = jnp.sum(grad_ffn.astype(F32), axis=0)
    grad_settled = grad_two
    mat_grads = [None] * len(mats)
    down_grads, up_b_sums = ([], [])
    for part in range(len(actives)):
        rows = slice(part * width, (part + 1) * width)
        grad_before = (mm(grad_ffn, downs[rows], 1, 1) * slopes[part].astype(F32)).astype(BF16)
        down_grads.append(mm(actives[part], grad_ffn, 0, 0).astype(BF16))
        mat_grads[4 + part] = mm(settled_low, grad_before, 0, 0).astype(BF16)
        up_b_sums.append(jnp.sum(grad_before.astype(F32), axis=0))
        grad_settled = grad_settled + mm(grad_before, mats[4 + part], 1, 1)
    grad_one, attn_g_sum, attn_s_sum = norm_rows_back(grad_settled, normed_one, inverse_one, attn_g)
    grad_attn = grad_one.astype(BF16)
    proj_b_sum = jnp.sum(grad_attn.astype(F32), axis=0)
    grad_context = mm(mats[3], grad_attn, 1, 1).astype(BF16)
    mat_grads[3] = mm(context, grad_attn, 1, 0).astype(BF16)
    grad_out = swap(grad_context.reshape(GROUP, width // GROUP, grad_context.shape[1]))
    moved = swap(attend_back(qkv, grad_out, out, lse, spans, seg_col, seg_row))
    share = width // GROUP
    pieces = [
        moved[:, part * share : (part + 1) * share].reshape(width, moved.shape[2]) for part in range(3)
    ]
    grad_hidden = grad_one
    for part in range(3):
        mat_grads[part] = mm(hidden_low, pieces[part], 0, 1).astype(BF16)
        grad_hidden = grad_hidden + mm(pieces[part], mats[part], 0, 1)
    query_b_sum = jnp.sum(pieces[0].astype(F32), axis=1)
    value_b_sum = jnp.sum(pieces[2].astype(F32), axis=1)
    sums = [
        query_b_sum, value_b_sum, proj_b_sum, attn_g_sum, attn_s_sum, down_b_sum, ffn_g_sum, ffn_s_sum,
    ] + up_b_sums
    return grad_hidden, mat_grads, down_grads, sums


MESH = pl.DeviceIdType.MESH


def places():
    rep, shard = (lax.axis_index("rep"), lax.axis_index("shard"))
    core, y, z = (lax.rem(rep, 2), lax.rem(shard, 2), lax.div(shard, 2))
    across_x = lax.rem(rep + 2, 4)
    across_core = rep + 1 - 2 * core
    zs = (z, z + 1 - 2 * lax.rem(z, 2), lax.rem(z + 2, 4), 3 - z)
    return (rep, shard, core, y, across_x, across_core, zs)


def greet():
    rep, shard, core, y, across_x, across_core, zs = places()
    barrier = pltpu.get_barrier_semaphore()
    partners = [(rep, 2 * other + y) for other in zs[1:]]
    partners += [(rep, 2 * zs[0] + 1 - y), (across_x, shard), (across_core, shard)]
    for partner in partners:
        pl.semaphore_signal(barrier, inc=1, device_id=partner, device_id_type=MESH)
    pl.semaphore_wait(barrier, len(partners))


class Sends:
    def __init__(self, sems):
        self.sems = sems
        self.copies = []

    def push(self, source, target, arrived, device):
        copy = pltpu.make_async_remote_copy(
            source, target, self.sems.at[len(self.copies)], arrived, device_id=device, device_id_type=MESH
        )
        copy.start()
        self.copies.append(copy)

    def finish(self):
        for copy in self.copies:
            copy.wait_send()


def gather_kernel(own_mats, own_downs, mats, downs, local_sems, send_sems, mat_sems, down_sems):
    rep, shard, core, y, across_x, across_core, zs = places()
    greet()
    sends = Sends(send_sems)

    def mat_piece(chunk, quarter):
        return mats.at[:, chunk, quarter]

    def send_mat(chunk, quarter, device, source=None):
        target = mat_piece(chunk, quarter)
        sends.push(target if source is None else source, target, mat_sems.at[chunk, quarter], device)

    def send_down(chunk, device, source=None):
        target = downs.at[chunk, core]
        sends.push(target if source is None else source, target, down_sems.at[chunk, core], device)

    def wait_mat(chunk, quarter):
        piece = mat_piece(chunk, quarter)
        pltpu.make_async_copy(piece, piece, mat_sems.at[chunk, quarter]).wait()

    def wait_down(chunk, half):
        piece = downs.at[chunk, half]
        pltpu.make_async_copy(piece, piece, down_sems.at[chunk, half]).wait()

    beside = (rep, 2 * zs[0] + 1 - y)
    own_mat, own_down = (own_mats.at[:, rep], own_downs.at[core])
    for k in (2, 3, 1):
        send_mat(shard, rep, (rep, 2 * zs[k] + y), own_mat)
    send_mat(shard, rep, beside, own_mat)
    for k in (2, 3, 1):
        send_down(shard, (rep, 2 * zs[k] + y), own_down)
    send_down(shard, beside, own_down)
    local = [
        pltpu.make_async_copy(own_mats, mats.at[:, shard], local_sems.at[0]),
        pltpu.make_async_copy(own_downs, downs.at[shard], local_sems.at[1]),
    ]
    for copy in local:
        copy.start()

    events = ((0, 1), (1, 0), (2, 0), (1, 1), (3, 0), (2, 1), (3, 1))
    chunks = [2 * zs[k] + (1 - y if far else y) for k, far in events]

    def from_x(chunk):
        wait_mat(chunk, across_x)
        send_mat(chunk, across_x, (across_core, shard))

    for at, (chunk, (k, far)) in enumerate(zip(chunks, events)):
        wait_mat(chunk, rep)
        if not far:
            send_mat(chunk, rep, beside)
        send_mat(chunk, rep, (across_x, shard))
        send_mat(chunk, rep, (across_core, shard))
        wait_down(chunk, core)
        if not far:
            send_down(chunk, beside)
        send_down(chunk, (across_core, shard))
        if at >= 3:
            from_x(chunks[at - 3])
    for chunk in chunks[-3:]:
        from_x(chunk)
    for chunk in chunks:
        wait_mat(chunk, across_core)
        wait_mat(chunk, lax.rem(across_core + 2, 4))
        wait_down(chunk, 1 - core)
    for copy in local:
        copy.wait()
    sends.finish()


def gather_fast(own, down):
    count, rows, width = own.shape
    full, half = pl.pallas_call(
        gather_kernel,
        name="gather",
        out_shape=(
            jax.ShapeDtypeStruct((count, 8, 4, rows // 4, width), BF16),
            jax.ShapeDtypeStruct((8, 2, down.shape[0] // 2, width), BF16),
        ),
        in_specs=in_vmem(2),
        out_specs=[pl.BlockSpec(memory_space=pl.ANY)] * 2,
        scratch_shapes=[
            pltpu.SemaphoreType.DMA((2,)),
            pltpu.SemaphoreType.DMA((42,)),
            pltpu.SemaphoreType.DMA((8, 4)),
            pltpu.SemaphoreType.DMA((8, 2)),
        ],
        compiler_params=pltpu.CompilerParams(collective_id=0, has_side_effects=True),
    )(own.reshape(count, 4, rows // 4, width), down.reshape(2, down.shape[0] // 2, width))
    return (full.reshape(count, 8 * rows, width), half.reshape(8 * down.shape[0], width))


def gather_weights(mats, downs):
    return (
        lax.all_gather(mats, "shard", axis=1, tiled=True),
        lax.all_gather(downs, "shard", axis=0, tiled=True),
    )


def reduce_kernel(
    mats, downs, qkv_out, proj_out, up_out, down_out,
    core_mats, x_mats, y_mats, z_mats, core_downs, y_downs, z_downs, x_down,
    x_stage, y_stage, z_stage, yd_stage, zd_stage, xd_stage, all_mats, all_downs,
    send_sems, core_sems, x_sems, y_sems, z_sems, core_d_sems, y_d_sems, z_d_sems, x_d_sem,
    all_sems, all_d_sems,
):
    rep, shard, core, y, across_x, across_core, zs = places()
    x = lax.div(rep, 2)
    beside, past_x, past_core = ((rep, 2 * zs[0] + 1 - y), (across_x, shard), (across_core, shard))
    greet()
    sends = Sends(send_sems)

    def arrive(ref, sem):
        pltpu.make_async_copy(ref, ref, sem).wait()

    def chunk_of(k, far):
        return 2 * zs[k] + (1 - y if far else y)

    def add_mats(target, parts):
        def body(block, carry):
            total = parts[0][block].astype(F32)
            for part in parts[1:]:
                total = total + part[block].astype(F32)
            target[block] = total.astype(BF16)
            return carry

        lax.fori_loop(0, mats.shape[2], body, 0)

    def add_downs(target, parts):
        rows = 32

        def body(step, carry):
            at = pl.ds(pl.multiple_of(step * rows, rows), rows)
            total = parts[0][at].astype(F32)
            for part in parts[1:]:
                total = total + part[at].astype(F32)
            target[at] = total.astype(BF16)
            return carry

        lax.fori_loop(0, downs.shape[2] // rows, body, 0)

    far_order = [(k, 1) for k in (2, 3, 1, 0)]
    near_order = [(k, 0) for k in (2, 3, 1)]
    own = (0, 0)

    def mat_at(chunk, quarter):
        return mats.at[chunk, quarter]

    for k, far in far_order + near_order + [own]:
        chunk = chunk_of(k, far)
        for side in (1, 0):
            which = (1 - x) if side else x
            sends.push(
                mat_at(chunk, 2 * which + 1 - core),
                core_mats.at[chunk, which],
                core_sems.at[chunk, which],
                past_core,
            )
        sends.push(downs.at[chunk, 1 - core], core_downs.at[chunk], core_d_sems.at[chunk], past_core)

    def step_x(slot, place):
        chunk = chunk_of(*place)
        arrive(core_mats.at[chunk, 1 - x], core_sems.at[chunk, 1 - x])
        add_mats(x_stage.at[slot], [mat_at(chunk, across_x), core_mats.at[chunk, 1 - x]])
        sends.push(x_stage.at[slot], x_mats.at[chunk], x_sems.at[chunk], past_x)

    def mat_parts(chunk):
        arrive(core_mats.at[chunk, x], core_sems.at[chunk, x])
        arrive(x_mats.at[chunk], x_sems.at[chunk])
        return [mat_at(chunk, rep), core_mats.at[chunk, x], x_mats.at[chunk]]

    def down_parts(chunk):
        arrive(core_downs.at[chunk], core_d_sems.at[chunk])
        return [downs.at[chunk, core], core_downs.at[chunk]]

    def step_y(place):
        k = place[0]
        add_mats(y_stage.at[k], mat_parts(chunk_of(*place)))
        sends.push(y_stage.at[k], y_mats.at[k], y_sems.at[k], beside)

    def step_yd(place):
        k = place[0]
        add_downs(yd_stage.at[k], down_parts(chunk_of(*place)))
        sends.push(yd_stage.at[k], y_downs.at[k], y_d_sems.at[k], beside)

    def step_z(place):
        k = place[0]
        parts = mat_parts(chunk_of(*place))
        arrive(y_mats.at[k], y_sems.at[k])
        add_mats(z_stage.at[k - 1], parts + [y_mats.at[k]])
        sends.push(z_stage.at[k - 1], z_mats.at[k - 1], z_sems.at[k - 1], (rep, 2 * zs[k] + y))

    def step_zd(place):
        k = place[0]
        parts = down_parts(chunk_of(*place))
        arrive(y_downs.at[k], y_d_sems.at[k])
        add_downs(zd_stage.at[k - 1], parts + [y_downs.at[k]])
        sends.push(zd_stage.at[k - 1], z_downs.at[k - 1], z_d_sems.at[k - 1], (rep, 2 * zs[k] + y))

    far, near = (far_order, near_order)
    step_x(0, far[0])
    step_yd(far[0])
    step_x(1, far[1])
    step_yd(far[1])
    step_x(2, far[2])
    step_yd(far[2])
    step_yd(far[3])
    step_y(far[0])
    step_x(3, far[3])
    step_y(far[1])
    step_x(4, near[0])
    step_zd(near[0])
    step_y(far[2])
    step_x(5, near[1])
    step_zd(near[1])
    step_y(far[3])
    step_x(6, near[2])
    step_zd(near[2])
    step_z(near[0])
    step_x(7, own)
    step_z(near[1])
    step_z(near[2])

    parts = down_parts(shard)
    arrive(y_downs.at[0], y_d_sems.at[0])
    for k in range(3):
        arrive(z_downs.at[k], z_d_sems.at[k])
    add_downs(xd_stage, parts + [y_downs.at[0]] + [z_downs.at[k] for k in range(3)])
    sends.push(xd_stage, x_down, x_d_sem, past_x)

    parts = mat_parts(shard)
    arrive(y_mats.at[0], y_sems.at[0])
    for k in range(3):
        arrive(z_mats.at[k], z_sems.at[k])
    add_mats(all_mats.at[rep], parts + [y_mats.at[0]] + [z_mats.at[k] for k in range(3)])
    sends.push(all_mats.at[rep], all_mats.at[rep], all_sems.at[rep], past_x)
    sends.push(all_mats.at[rep], all_mats.at[rep], all_sems.at[rep], past_core)

    arrive(x_down, x_d_sem)
    add_downs(all_downs.at[core], [xd_stage, x_down])
    sends.push(all_downs.at[core], all_downs.at[core], all_d_sems.at[core], past_core)

    arrive(all_mats.at[across_x], all_sems.at[across_x])
    sends.push(all_mats.at[across_x], all_mats.at[across_x], all_sems.at[across_x], past_core)
    opposite = lax.rem(across_core + 2, 4)
    arrive(all_mats.at[across_core], all_sems.at[across_core])
    arrive(all_mats.at[opposite], all_sems.at[opposite])
    arrive(all_downs.at[1 - core], all_d_sems.at[1 - core])

    quarter, width = (mats.shape[3], mats.shape[4])
    for q in range(4):
        rows = slice(q * quarter, (q + 1) * quarter)
        for block in range(all_mats.shape[1]):
            piece = all_mats[q, block].astype(F32)
            if block < 3:
                qkv_out[rows, block * width : (block + 1) * width] = piece
            elif block == 3:
                proj_out[rows, :] = piece
            else:
                up_out[rows, (block - 4) * width : (block - 3) * width] = piece
    half = all_downs.shape[1]
    for c in range(2):
        down_out[c * half : (c + 1) * half, :] = all_downs[c].astype(F32)
    sends.finish()


def reduce_fast(mat_grads, down_grads):
    count = len(mat_grads)
    width = mat_grads[0].shape[1]
    quarter = mat_grads[0].shape[0] // 32
    mats = jnp.stack([item.reshape(8, 4, quarter, width) for item in mat_grads], axis=2)
    downs = jnp.concatenate(down_grads, axis=0)
    half = downs.shape[0] // 16
    downs = downs.reshape(8, 2, half, width)

    def mat_buf(*lead):
        return pltpu.VMEM(lead + (count, quarter, width), BF16)

    def down_buf(*lead):
        return pltpu.VMEM(lead + (half, width), BF16)

    dma = pltpu.SemaphoreType.DMA
    return pl.pallas_call(
        reduce_kernel,
        name="reduce",
        out_shape=(
            jax.ShapeDtypeStruct((4 * quarter, 3 * width), F32),
            jax.ShapeDtypeStruct((4 * quarter, width), F32),
            jax.ShapeDtypeStruct((4 * quarter, (count - 4) * width), F32),
            jax.ShapeDtypeStruct((2 * half, width), F32),
        ),
        in_specs=in_vmem(2),
        out_specs=in_vmem(4),
        scratch_shapes=[
            mat_buf(8, 2), mat_buf(8), mat_buf(4), mat_buf(3),
            down_buf(8), down_buf(4), down_buf(3), down_buf(),
            mat_buf(8), mat_buf(4), mat_buf(3),
            down_buf(4), down_buf(3), down_buf(),
            mat_buf(4), down_buf(2),
            dma((51,)), dma((8, 2)), dma((8,)), dma((4,)), dma((3,)),
            dma((8,)), dma((4,)), dma((3,)), dma(()), dma((4,)), dma((2,)),
        ],
        compiler_params=pltpu.CompilerParams(
            collective_id=1, has_side_effects=True, vmem_limit_bytes=60 * 1024 * 1024
        ),
    )(mats, downs)


def spread_rep(piece):
    rep = lax.axis_index("rep")
    for bit in range(2):
        other = exchange(piece, "rep", 1 << bit)
        piece = ordered((rep >> bit) & 1 == 0, piece, other)
    return piece.reshape((4,) + piece.shape[2:])


def scatter_grads(mat_grads, down_grads):
    width = mat_grads[0].shape[1]
    rows = mat_grads[0].shape[0]

    def by_rep(tensor):
        split = tensor.reshape(8, 4, tensor.shape[0] // 32, width)
        return jnp.transpose(split, (1, 0, 2, 3)).reshape(tensor.shape)

    mats = lax.psum_scatter(
        jnp.stack([by_rep(item) for item in mat_grads]),
        ("rep", "shard"), scatter_dimension=1, tiled=True,
    )
    downs = lax.psum_scatter(
        by_rep(jnp.concatenate(down_grads, axis=0)),
        ("rep", "shard"), scatter_dimension=0, tiled=True,
    )
    mats = jnp.transpose(spread_rep(mats), (1, 0, 2, 3)).reshape(len(mat_grads), rows // 8, width)
    downs = spread_rep(downs).reshape(-1, width)

    def side(low, high):
        return jnp.concatenate(list(mats[low:high]), axis=1).astype(F32)

    return (side(0, 3), side(3, 4), side(4, len(mat_grads)), downs.astype(F32))


def on_device_fast(
    inputs, cotangent, segment_ids, memory_slot, memory_table,
    qkv_weight, query_bias, value_bias, proj_weight, proj_bias, attn_gain, attn_shift,
    up_weight, up_bias, down_weight, down_bias, ffn_gain, ffn_shift,
):
    index = lax.axis_index("shard")
    width = inputs.shape[2]
    share = memory_table.shape[1]
    ups = up_weight.shape[2] // width

    weights = []
    for layer in range(LAYERS):
        own = jnp.concatenate([qkv_weight[layer], proj_weight[layer], up_weight[layer]], axis=1)
        own = jnp.stack([own[:, part * width : (part + 1) * width] for part in range(4 + ups)])
        weights.append((gather_fast if layer == 0 else gather_weights)(own, down_weight[layer]))

    vec_args = (
        query_bias, value_bias, proj_bias, attn_gain, attn_shift, down_bias, ffn_gain, ffn_shift,
    )
    plain = len(vec_args)
    rows = [item[layer][None] for layer in range(LAYERS) for item in vec_args]
    rows += [up_bias[layer].reshape(ups, share) for layer in range(LAYERS)]
    rows.append(memory_table)
    small = gather_small(jnp.concatenate(rows, axis=0)).astype(F32)
    wide = jnp.transpose(small, (1, 0, 2)).reshape(small.shape[1], width)
    vecs = []
    for layer in range(LAYERS):
        start = LAYERS * plain + layer * ups
        vecs.append(
            [wide[layer * plain + item] for item in range(plain)]
            + [small[:, start : start + ups].reshape(ups * width)]
        )
    table = wide[LAYERS * (plain + ups) :].astype(BF16)

    segs = jnp.where(index < GROUP, segment_ids[0], segment_ids[1])
    tiles = segs.reshape(-1, BLOCK)
    first, last = (tiles[:, 0], tiles[:, -1])
    spans = (
        jnp.sum((last[None, :] < first[:, None]).astype(jnp.int32), axis=1),
        jnp.sum((first[None, :] <= last[:, None]).astype(jnp.int32), axis=1),
    )
    seg_row = tiles[:, None, :]
    seg_col = jnp.broadcast_to(segs[:, None], (segs.shape[0], 128))

    slots = to_groups(memory_slot[..., None], index)[:, 0]
    slot_hot = slots[:, None] == jnp.arange(MEMS, dtype=jnp.int32)
    hidden = to_groups(inputs, index).astype(F32) + mm(slot_hot.astype(BF16), table, 1, 0)
    saved = []
    for layer in range(LAYERS):
        mats, downs = weights[layer]
        hidden, state = fast_forward(hidden, mats, downs, vecs[layer], spans, seg_col, seg_row)
        saved.append(state)
    layer_output = from_groups(hidden, index)

    grad = to_groups(cotangent, index).astype(F32)
    sums, shares = ([None] * LAYERS, [None] * LAYERS)
    for layer in range(LAYERS - 1, -1, -1):
        mats, downs = weights[layer]
        grad, mat_grads, down_grads, sums[layer] = fast_backward(
            grad, mats, downs, vecs[layer], saved[layer], spans, seg_col, seg_row
        )
        shares[layer] = (reduce_fast if layer == 0 else scatter_grads)(mat_grads, down_grads)
    input_grad = from_groups(grad, index)
    memory_sum = lax.dot_general(
        slot_hot.astype(F32), grad, (((0,), (0,)), ((), ())), precision=lax.Precision.HIGHEST
    )
    flat = jnp.concatenate([jnp.stack(sums[layer]) for layer in range(LAYERS)] + [memory_sum], axis=0)
    flat = sum_small(flat)
    per = plain + ups
    own = lax.dynamic_slice_in_dim(flat, index * share, share, 1)
    vec_grads = [
        jnp.stack([own[layer * per + item] for layer in range(LAYERS)]) for item in range(plain)
    ]
    up_sums = jnp.stack([flat[layer * per + plain : (layer + 1) * per].reshape(-1) for layer in range(LAYERS)])
    upbias_grad = lax.dynamic_slice_in_dim(up_sums, index * share * ups, share * ups, 1)
    memory_grad = own[LAYERS * per :]

    def wide_grad(member):
        return jnp.stack([shares[layer][member] for layer in range(LAYERS)])

    return (
        layer_output,
        input_grad,
        memory_grad,
        wide_grad(0),
        vec_grads[0],
        vec_grads[1],
        wide_grad(1),
        vec_grads[2],
        vec_grads[3],
        vec_grads[4],
        wide_grad(2),
        upbias_grad,
        wide_grad(3),
        vec_grads[5],
        vec_grads[6],
        vec_grads[7],
    )


def fast_fits(mesh):
    return mesh.shape["shard"] == 2 * GROUP and mesh.shape["rep"] == 4


def solution(mesh):
    return jax.shard_map(
        on_device_fast if fast_fits(mesh) else on_device,
        mesh=mesh,
        in_specs=(
            P(None, ("rep", "shard"), None),
            P(None, ("rep", "shard"), None),
            P(None, "rep"),
            P(None, ("rep", "shard")),
            P(None, "shard"),
            P(None, "shard", None),
            P(None, "shard"),
            P(None, "shard"),
            P(None, "shard", None),
            P(None, "shard"),
            P(None, "shard"),
            P(None, "shard"),
            P(None, "shard", None),
            P(None, "shard"),
            P(None, "shard", None),
            P(None, "shard"),
            P(None, "shard"),
            P(None, "shard"),
        ),
        out_specs=(
            P(None, ("rep", "shard"), None),
            P(None, ("rep", "shard"), None),
            P(None, "shard"),
            P(None, "shard", None),
            P(None, "shard"),
            P(None, "shard"),
            P(None, "shard", None),
            P(None, "shard"),
            P(None, "shard"),
            P(None, "shard"),
            P(None, "shard", None),
            P(None, "shard"),
            P(None, "shard", None),
            P(None, "shard"),
            P(None, "shard"),
            P(None, "shard"),
        ),
        check_vma=False,
    )
```

```python
import functools

import jax
import jax.numpy as jnp
from jax import lax
from jax.experimental import pallas as pl
from jax.experimental.pallas import tpu as pltpu
from jax.sharding import PartitionSpec as P

HEADS = 12
HEAD_DIM = 64
LAYERS = 2
MEMS = 20
REACH = 4


norm_eps = 1e-12
masked_score = -1e30


def passed_along(block, axis, distance):
    devices = range(lax.axis_size(axis))
    route = [(i - distance, i) for i in devices if i - distance in devices]
    return lax.ppermute(block, axis, route)


def layer_norm(tensor, norm_gain, norm_shift):
    center = tensor - jnp.mean(tensor, axis=-1, keepdims=True)
    inverse = lax.rsqrt(jnp.mean(center * center, axis=-1, keepdims=True) + norm_eps)
    normed = center * inverse
    return (normed * norm_gain + norm_shift, normed, inverse)


def norm_backward(grad_out, normed, inverse, norm_gain):
    scaled = grad_out * norm_gain
    inner_term = (
        scaled
        - jnp.mean(scaled, axis=-1, keepdims=True)
        - normed * jnp.mean(scaled * normed, axis=-1, keepdims=True)
    )
    return (
        inner_term * inverse,
        jnp.sum(grad_out * normed, axis=(0, 1)),
        jnp.sum(grad_out, axis=(0, 1)),
    )


def gelu_exact(tensor):
    return jax.nn.gelu(tensor, approximate=False)


def split_heads(tensor):
    return tensor.reshape(tensor.shape[0], tensor.shape[1], HEADS, HEAD_DIM)


def merge_heads(tensor):
    return tensor.reshape(tensor.shape[0], tensor.shape[1], HEADS * HEAD_DIM)


def product(left_side, right_side):
    return jnp.einsum("btd,de->bte", left_side, right_side, preferred_element_type=jnp.float32)


def product_back(left_side, right_side):
    return jnp.einsum("bte,de->btd", left_side, right_side, preferred_element_type=jnp.float32)


def weight_grad(left_side, right_side):
    return jnp.einsum("btd,bte->de", left_side, right_side, preferred_element_type=jnp.float32)


def token_sum(tensor):
    return jnp.sum(tensor.astype(jnp.float32), axis=(0, 1))


def piece_mask(segment_ids, seg_here, my_index, shards, row_count, offset):
    target = my_index + offset
    inside = jnp.logical_and(target >= 0, target < shards)
    start_row = jnp.clip(target, 0, shards - 1) * row_count
    seg_there = lax.dynamic_slice_in_dim(segment_ids, start_row, row_count, 1)
    key_mask = jnp.logical_and(seg_here[:, None, :, None] == seg_there[:, None, None, :], inside)
    return (key_mask, jnp.any(key_mask))


def scaled_scores(query_heads, key_part, key_mask):
    scores = (
        jnp.einsum(
            "bqhe,bkhe->bhqk",
            query_heads,
            split_heads(key_part),
            preferred_element_type=jnp.float32,
        )
        * 0.125
    )
    return jnp.where(key_mask, scores, masked_score)


def stats_update(carry_in, query_heads, key_part, key_mask):
    old_max, old_sum = carry_in
    scores = scaled_scores(query_heads, key_part, key_mask)
    new_max = jnp.maximum(old_max, jnp.max(scores, axis=-1))
    fresh = jnp.sum(jnp.where(key_mask, jnp.exp(scores - new_max[..., None]), 0.0), axis=-1)
    return (new_max, old_sum * jnp.exp(old_max - new_max) + fresh)


def stats_keep(carry_in, query_heads, key_part, key_mask):
    return carry_in


def mix_update(context, query_heads, key_part, value_part, key_mask, log_sum):
    scores = scaled_scores(query_heads, key_part, key_mask)
    soft_probs = jnp.where(key_mask, jnp.exp(scores - log_sum[..., None]), 0.0).astype(jnp.bfloat16)
    return context + jnp.einsum(
        "bhqk,bkhe->bqhe", soft_probs, split_heads(value_part), preferred_element_type=jnp.float32
    )


def mix_keep(context, query_heads, key_part, value_part, key_mask, log_sum):
    return context


def piece_update(
    grad_query, query_heads, grad_heads, key_part, value_part, key_mask, log_sum, row_delta
):
    scores = scaled_scores(query_heads, key_part, key_mask)
    soft_probs = jnp.where(key_mask, jnp.exp(scores - log_sum[..., None]), 0.0)
    grad_probs = jnp.einsum(
        "bqhe,bkhe->bhqk", grad_heads, split_heads(value_part), preferred_element_type=jnp.float32
    )
    grad_scores = (soft_probs * (grad_probs - row_delta[..., None])).astype(jnp.bfloat16)
    grad_query = grad_query + jnp.einsum(
        "bhqk,bkhe->bqhe", grad_scores, split_heads(key_part), preferred_element_type=jnp.float32
    )
    key_grad = jnp.einsum(
        "bhqk,bqhe->bkhe", grad_scores, query_heads, preferred_element_type=jnp.float32
    )
    value_grad = jnp.einsum(
        "bhqk,bqhe->bkhe",
        soft_probs.astype(jnp.bfloat16),
        grad_heads,
        preferred_element_type=jnp.float32,
    )
    return (grad_query, merge_heads(key_grad), merge_heads(value_grad))


def piece_skip(
    grad_query, query_heads, grad_heads, key_part, value_part, key_mask, log_sum, row_delta
):
    empty = jnp.zeros(key_part.shape, jnp.float32)
    return (grad_query, empty, empty)


def attend_forward(query_rows, key_rows, value_rows, offsets, key_masks):
    micro_count, row_count = (query_rows.shape[0], query_rows.shape[1])
    query_heads = split_heads(query_rows)
    pieces = [(key_rows, value_rows)]
    for offset in offsets:
        pieces.append(passed_along((key_rows, value_rows), "shard", -offset))
    row_max = jnp.full((micro_count, HEADS, row_count), masked_score, jnp.float32)
    row_sum = jnp.zeros((micro_count, HEADS, row_count), jnp.float32)
    for (key_part, value_part), (key_mask, is_live) in zip(pieces, key_masks):
        row_max, row_sum = lax.cond(
            is_live, stats_update, stats_keep, (row_max, row_sum), query_heads, key_part, key_mask
        )
    log_sum = row_max + jnp.log(row_sum)
    context = jnp.zeros((micro_count, row_count, HEADS, HEAD_DIM), jnp.float32)
    for (key_part, value_part), (key_mask, is_live) in zip(pieces, key_masks):
        context = lax.cond(
            is_live,
            mix_update,
            mix_keep,
            context,
            query_heads,
            key_part,
            value_part,
            key_mask,
            log_sum,
        )
    return (merge_heads(context), log_sum, pieces)


def attend_backward(query_rows, grad_context, context, log_sum, pieces, key_masks, offsets):
    query_heads = split_heads(query_rows)
    grad_heads = split_heads(grad_context)
    row_delta = jnp.transpose(
        jnp.sum(split_heads(grad_context.astype(jnp.float32) * context), axis=-1), (0, 2, 1)
    )
    grad_query = jnp.zeros(query_heads.shape, jnp.float32)
    own_keys = jnp.zeros(query_rows.shape, jnp.float32)
    own_values = jnp.zeros(query_rows.shape, jnp.float32)
    for index_num in range(len(pieces)):
        key_part, value_part = pieces[index_num]
        key_mask, is_live = key_masks[index_num]
        grad_query, key_grad, value_grad = lax.cond(
            is_live,
            piece_update,
            piece_skip,
            grad_query,
            query_heads,
            grad_heads,
            key_part,
            value_part,
            key_mask,
            log_sum,
            row_delta,
        )
        if index_num == 0:
            own_keys = key_grad
            own_values = value_grad
        else:
            back_keys, back_values = (
                passed_along(key_grad.astype(jnp.bfloat16), "shard", offsets[index_num - 1]).astype(
                    key_grad.dtype
                ),
                passed_along(
                    value_grad.astype(jnp.bfloat16), "shard", offsets[index_num - 1]
                ).astype(value_grad.dtype),
            )
            own_keys = own_keys + back_keys
            own_values = own_values + back_values
    query_out = (merge_heads(grad_query) * 0.125).astype(jnp.bfloat16)
    return (query_out, (own_keys * 0.125).astype(jnp.bfloat16), own_values.astype(jnp.bfloat16))


def layer_forward(hidden, weights, offsets, key_masks):
    (
        qkv_w,
        query_b,
        value_b,
        proj_w,
        proj_b,
        attn_g,
        attn_s,
        up_w,
        up_b,
        down_w,
        down_b,
        ffn_g,
        ffn_s,
    ) = weights
    model_width = qkv_w.shape[0]
    hidden_low = hidden.astype(jnp.bfloat16)
    mixed_all = product(hidden_low, qkv_w)
    query_rows = (mixed_all[..., :model_width] + query_b.astype(jnp.float32)).astype(jnp.bfloat16)
    key_rows = mixed_all[..., model_width : 2 * model_width].astype(jnp.bfloat16)
    value_rows = (mixed_all[..., 2 * model_width :] + value_b.astype(jnp.float32)).astype(
        jnp.bfloat16
    )
    context, log_sum, pieces = attend_forward(query_rows, key_rows, value_rows, offsets, key_masks)
    context_low = context.astype(jnp.bfloat16)
    attn_out = product(context_low, proj_w) + proj_b.astype(jnp.float32)
    settled, normed_one, inverse_one = layer_norm(
        hidden + attn_out, attn_g.astype(jnp.float32), attn_s.astype(jnp.float32)
    )
    settled_low = settled.astype(jnp.bfloat16)
    before = product(settled_low, up_w) + up_b.astype(jnp.float32)
    active = gelu_exact(before).astype(jnp.bfloat16)
    ffn_out = product(active, down_w) + down_b.astype(jnp.float32)
    result, normed_two, inverse_two = layer_norm(
        settled + ffn_out, ffn_g.astype(jnp.float32), ffn_s.astype(jnp.float32)
    )
    saved_state = (
        hidden_low,
        query_rows,
        key_rows,
        value_rows,
        context,
        log_sum,
        pieces,
        context_low,
        normed_one,
        inverse_one,
        settled_low,
        before,
        active,
        normed_two,
        inverse_two,
    )
    return (result, saved_state)


def layer_backward(grad_out, weights, saved_state, offsets, key_masks):
    (
        qkv_w,
        query_b,
        value_b,
        proj_w,
        proj_b,
        attn_g,
        attn_s,
        up_w,
        up_b,
        down_w,
        down_b,
        ffn_g,
        ffn_s,
    ) = weights
    (
        hidden_low,
        query_rows,
        key_rows,
        value_rows,
        context,
        log_sum,
        pieces,
        context_low,
        normed_one,
        inverse_one,
        settled_low,
        before,
        active,
        normed_two,
        inverse_two,
    ) = saved_state
    grad_two, ffngain_part, ffnshift_part = norm_backward(
        grad_out, normed_two, inverse_two, ffn_g.astype(jnp.float32)
    )
    grad_ffn = grad_two.astype(jnp.bfloat16)
    downweight_part = weight_grad(active, grad_ffn)
    downbias_part = token_sum(grad_ffn)
    grad_active = product_back(grad_ffn, down_w)
    gelu_pull = jax.vjp(gelu_exact, before)[1]
    grad_before = gelu_pull(grad_active)[0].astype(jnp.bfloat16)
    upweight_part = weight_grad(settled_low, grad_before)
    upbias_part = token_sum(grad_before)
    grad_settled = grad_two + product_back(grad_before, up_w)
    grad_one, attngain_part, attnshift_part = norm_backward(
        grad_settled, normed_one, inverse_one, attn_g.astype(jnp.float32)
    )
    grad_attn = grad_one.astype(jnp.bfloat16)
    proj_part = weight_grad(context_low, grad_attn)
    projbias_part = token_sum(grad_attn)
    grad_context = product_back(grad_attn, proj_w).astype(jnp.bfloat16)
    pieces = [(key_rows, value_rows)]
    for offset in offsets:
        pieces.append(passed_along((key_rows, value_rows), "shard", -offset))
    grad_query, grad_keys, grad_values = attend_backward(
        query_rows, grad_context, context, log_sum, pieces, key_masks, offsets
    )
    grad_mixed = jnp.concatenate([grad_query, grad_keys, grad_values], axis=-1)
    qkv_part = weight_grad(hidden_low, grad_mixed)
    querybias_part = token_sum(grad_query)
    valuebias_part = token_sum(grad_values)
    grad_hidden = grad_one + product_back(grad_mixed, qkv_w)
    layer_grads = (
        qkv_part,
        querybias_part,
        valuebias_part,
        proj_part,
        projbias_part,
        attngain_part,
        attnshift_part,
        upweight_part,
        upbias_part,
        downweight_part,
        downbias_part,
        ffngain_part,
        ffnshift_part,
    )
    return (grad_hidden, layer_grads)


def on_device(
    inputs,
    cotangent,
    segment_ids,
    memory_slot,
    memory_table,
    qkv_weight,
    query_bias,
    value_bias,
    proj_weight,
    proj_bias,
    attn_gain,
    attn_shift,
    up_weight,
    up_bias,
    down_weight,
    down_bias,
    ffn_gain,
    ffn_shift,
):
    shards = lax.axis_size("shard")
    my_index = lax.axis_index("shard")
    row_count = inputs.shape[1]
    reach_out = min(REACH, shards - 1)
    offsets = [offset for offset in range(-reach_out, reach_out + 1) if offset != 0]
    seg_here = lax.dynamic_slice_in_dim(segment_ids, my_index * row_count, row_count, 1)
    key_masks = [piece_mask(segment_ids, seg_here, my_index, shards, row_count, 0)]
    for offset in offsets:
        key_masks.append(piece_mask(segment_ids, seg_here, my_index, shards, row_count, offset))
    gathered = (
        lax.all_gather(qkv_weight, "shard", axis=1, tiled=True),
        lax.all_gather(query_bias, "shard", axis=1, tiled=True),
        lax.all_gather(value_bias, "shard", axis=1, tiled=True),
        lax.all_gather(proj_weight, "shard", axis=1, tiled=True),
        lax.all_gather(proj_bias, "shard", axis=1, tiled=True),
        lax.all_gather(attn_gain, "shard", axis=1, tiled=True),
        lax.all_gather(attn_shift, "shard", axis=1, tiled=True),
        lax.all_gather(up_weight, "shard", axis=1, tiled=True),
        lax.all_gather(up_bias, "shard", axis=1, tiled=True),
        lax.all_gather(down_weight, "shard", axis=1, tiled=True),
        lax.all_gather(down_bias, "shard", axis=1, tiled=True),
        lax.all_gather(ffn_gain, "shard", axis=1, tiled=True),
        lax.all_gather(ffn_shift, "shard", axis=1, tiled=True),
        lax.all_gather(memory_table, "shard", axis=1, tiled=True),
    )
    slot_range = jnp.arange(MEMS, dtype=jnp.int32)
    slot_hot = (memory_slot[..., None] == slot_range).astype(jnp.float32)
    hidden = inputs.astype(jnp.float32) + jnp.einsum(
        "btm,md->btd", slot_hot, gathered[13].astype(jnp.float32), precision=lax.Precision.HIGHEST
    )
    saved_list = []
    for layer_num in range(LAYERS):
        weights = tuple((item[layer_num] for item in gathered[:13]))
        hidden, saved_state = layer_forward(hidden, weights, offsets, key_masks)
        saved_list.append(saved_state)
    regathered = (
        lax.all_gather(qkv_weight, "shard", axis=1, tiled=True),
        lax.all_gather(query_bias, "shard", axis=1, tiled=True),
        lax.all_gather(value_bias, "shard", axis=1, tiled=True),
        lax.all_gather(proj_weight, "shard", axis=1, tiled=True),
        lax.all_gather(proj_bias, "shard", axis=1, tiled=True),
        lax.all_gather(attn_gain, "shard", axis=1, tiled=True),
        lax.all_gather(attn_shift, "shard", axis=1, tiled=True),
        lax.all_gather(up_weight, "shard", axis=1, tiled=True),
        lax.all_gather(up_bias, "shard", axis=1, tiled=True),
        lax.all_gather(down_weight, "shard", axis=1, tiled=True),
        lax.all_gather(down_bias, "shard", axis=1, tiled=True),
        lax.all_gather(ffn_gain, "shard", axis=1, tiled=True),
        lax.all_gather(ffn_shift, "shard", axis=1, tiled=True),
    )
    grad_hidden = cotangent.astype(jnp.float32)
    grads_by_layer = [None] * LAYERS
    for layer_num in range(LAYERS - 1, -1, -1):
        weights = tuple((item[layer_num] for item in regathered))
        grad_hidden, layer_grads = layer_backward(
            grad_hidden, weights, saved_list[layer_num], offsets, key_masks
        )
        grads_by_layer[layer_num] = layer_grads
    memory_full = jnp.einsum("btm,btd->md", slot_hot, grad_hidden, precision=lax.Precision.HIGHEST)
    stacked = [
        jnp.stack([grads_by_layer[layer_num][member] for layer_num in range(LAYERS)])
        for member in range(13)
    ]
    shares = (
        lax.psum_scatter(stacked[0], "shard", scatter_dimension=1, tiled=True),
        lax.psum_scatter(stacked[1], "shard", scatter_dimension=1, tiled=True),
        lax.psum_scatter(stacked[2], "shard", scatter_dimension=1, tiled=True),
        lax.psum_scatter(stacked[3], "shard", scatter_dimension=1, tiled=True),
        lax.psum_scatter(stacked[4], "shard", scatter_dimension=1, tiled=True),
        lax.psum_scatter(stacked[5], "shard", scatter_dimension=1, tiled=True),
        lax.psum_scatter(stacked[6], "shard", scatter_dimension=1, tiled=True),
        lax.psum_scatter(stacked[7], "shard", scatter_dimension=1, tiled=True),
        lax.psum_scatter(stacked[8], "shard", scatter_dimension=1, tiled=True),
        lax.psum_scatter(stacked[9], "shard", scatter_dimension=1, tiled=True),
        lax.psum_scatter(stacked[10], "shard", scatter_dimension=1, tiled=True),
        lax.psum_scatter(stacked[11], "shard", scatter_dimension=1, tiled=True),
        lax.psum_scatter(stacked[12], "shard", scatter_dimension=1, tiled=True),
        lax.psum_scatter(memory_full, "shard", scatter_dimension=1, tiled=True),
    )
    totals = (
        lax.psum(shares[0].astype(jnp.bfloat16), "rep").astype(jnp.float32),
        lax.psum(shares[1].astype(jnp.bfloat16), "rep").astype(jnp.float32),
        lax.psum(shares[2].astype(jnp.bfloat16), "rep").astype(jnp.float32),
        lax.psum(shares[3].astype(jnp.bfloat16), "rep").astype(jnp.float32),
        lax.psum(shares[4].astype(jnp.bfloat16), "rep").astype(jnp.float32),
        lax.psum(shares[5].astype(jnp.bfloat16), "rep").astype(jnp.float32),
        lax.psum(shares[6].astype(jnp.bfloat16), "rep").astype(jnp.float32),
        lax.psum(shares[7].astype(jnp.bfloat16), "rep").astype(jnp.float32),
        lax.psum(shares[8].astype(jnp.bfloat16), "rep").astype(jnp.float32),
        lax.psum(shares[9].astype(jnp.bfloat16), "rep").astype(jnp.float32),
        lax.psum(shares[10].astype(jnp.bfloat16), "rep").astype(jnp.float32),
        lax.psum(shares[11].astype(jnp.bfloat16), "rep").astype(jnp.float32),
        lax.psum(shares[12].astype(jnp.bfloat16), "rep").astype(jnp.float32),
        lax.psum(shares[13].astype(jnp.bfloat16), "rep").astype(jnp.float32),
    )
    return (
        hidden,
        grad_hidden,
        totals[13],
        totals[0],
        totals[1],
        totals[2],
        totals[3],
        totals[4],
        totals[5],
        totals[6],
        totals[7],
        totals[8],
        totals[9],
        totals[10],
        totals[11],
        totals[12],
    )


BLOCK = 256
GROUP = 4
BF16 = jnp.bfloat16
F32 = jnp.float32


def mm(left, right, left_dim, right_dim):
    return lax.dot_general(
        left, right, (((left_dim,), (right_dim,)), ((), ())), preferred_element_type=F32
    )


def exchange(tensor, axis, mask):
    count = lax.axis_size(axis)
    return lax.ppermute(tensor, axis, [(i, i ^ mask) for i in range(count)])


def ordered(first_is_mine, mine, other):
    return jnp.stack(
        [jnp.where(first_is_mine, mine, other), jnp.where(first_is_mine, other, mine)]
    )


def to_groups(tensor, index):
    low = index < GROUP
    mine = jnp.where(low, tensor[0], tensor[1])
    other = exchange(jnp.where(low, tensor[1], tensor[0]), "shard", GROUP)
    both = ordered(low, mine, other)
    return both.reshape((2 * tensor.shape[1],) + tensor.shape[2:])


def from_groups(tensor, index):
    low = index < GROUP
    half = tensor.shape[0] // 2
    mine = jnp.where(low, tensor[:half], tensor[half:])
    other = exchange(
        jnp.where(low, tensor[half:], tensor[:half]).astype(BF16), "shard", GROUP
    ).astype(tensor.dtype)
    return ordered(low, mine, other)


def swap(tensor):
    shape = tensor.shape
    flat = tensor.reshape((shape[0] * shape[1],) + shape[2:])
    moved = lax.all_to_all(
        flat, "shard", 0, 0, axis_index_groups=[[0, 1, 2, 3], [4, 5, 6, 7]], tiled=True
    )
    return moved.reshape(shape)


def block_cols(block):
    half = block // GROUP
    return pl.ds(pl.multiple_of(half * BLOCK, BLOCK), BLOCK)


def flipped(tensor):
    return jnp.transpose(tensor.astype(F32)).astype(BF16)


def pair_mask(seg_col, seg_row, keys, queries):
    col = seg_col[pl.ds(pl.multiple_of(keys * BLOCK, BLOCK), BLOCK), :]
    col = jnp.concatenate([col] * (BLOCK // 128), axis=1)
    return col == seg_row[queries]


def attend_kernel(
    lo_ref, hi_ref, x_ref, seg_col, seg_row, low_ref, out_ref, lse_ref, keys_nat, acc, top, total,
):
    heads = x_ref.shape[1] // (3 * HEAD_DIM)
    width = heads * HEAD_DIM
    blocks = seg_row.shape[0]

    def flip(block, carry):
        for h in range(heads):
            keys_nat[h, block] = flipped(
                x_ref[block % GROUP, width + h * HEAD_DIM : width + (h + 1) * HEAD_DIM, block_cols(block)]
            )
        return carry

    lax.fori_loop(0, blocks, flip, 0)

    def per_query(i, carry):
        src, cols = (i % GROUP, block_cols(i))
        for h in range(heads):
            top[h] = jnp.full(top.shape[1:], masked_score, F32)
            total[h] = jnp.zeros(total.shape[1:], F32)
            acc[h] = jnp.zeros(acc.shape[1:], F32)

        def per_key(j, inner):
            allowed = pair_mask(seg_col, seg_row, j, i)
            olds = [top[h] for h in range(heads)]
            sums = [total[h] for h in range(heads)]
            mixes = [acc[h] for h in range(heads)]
            scores = [
                mm(keys_nat[h, j], x_ref[src, h * HEAD_DIM : (h + 1) * HEAD_DIM, cols], 1, 0)
                for h in range(heads)
            ]
            scores = [jnp.where(allowed, item, masked_score) for item in scores]
            news = [
                jnp.maximum(old, jnp.max(item, axis=0, keepdims=True)) for old, item in zip(olds, scores)
            ]
            raised = [jnp.exp(item - new) for item, new in zip(scores, news)]
            adds = [
                mm(
                    x_ref[j % GROUP, 2 * width + h * HEAD_DIM : 2 * width + (h + 1) * HEAD_DIM, block_cols(j)],
                    raised[h].astype(BF16), 1, 0,
                )
                for h in range(heads)
            ]
            for h in range(heads):
                fade = jnp.exp(olds[h] - news[h])
                top[h] = news[h]
                total[h] = sums[h] * fade + jnp.sum(raised[h], axis=0, keepdims=True)
                acc[h] = mixes[h] * fade + adds[h]
            return inner

        lax.fori_loop(lo_ref[i], hi_ref[i], per_key, 0)
        for h in range(heads):
            out = acc[h] / total[h]
            out_ref[src, h * HEAD_DIM : (h + 1) * HEAD_DIM, cols] = out
            low_ref[src, h * HEAD_DIM : (h + 1) * HEAD_DIM, cols] = out.astype(BF16)
            lse_ref[h, i] = top[h] + jnp.log(total[h])
        return carry

    lax.fori_loop(0, blocks, per_query, 0)


def attend_back_kernel(
    lo_ref, hi_ref, x_ref, go_ref, out_ref, lse_ref, seg_col, seg_row, dx_ref,
    keys_nat, values_nat, delta, dq, dk, dv,
):
    heads = x_ref.shape[1] // (3 * HEAD_DIM)
    width = heads * HEAD_DIM
    blocks = seg_row.shape[0]

    def prepare(block, carry):
        src, cols = (block % GROUP, block_cols(block))
        for h in range(heads):
            low, high = (h * HEAD_DIM, (h + 1) * HEAD_DIM)
            keys_nat[h, block] = flipped(x_ref[src, width + low : width + high, cols])
            values_nat[h, block] = flipped(x_ref[src, 2 * width + low : 2 * width + high, cols])
            delta[h, block] = jnp.sum(
                go_ref[src, low:high, cols].astype(F32) * out_ref[src, low:high, cols],
                axis=0,
                keepdims=True,
            )
            dq[h, block] = jnp.zeros(dq.shape[2:], F32)
        return carry

    lax.fori_loop(0, blocks, prepare, 0)

    def per_key(j, carry):
        key_src, key_cols = (j % GROUP, block_cols(j))
        for h in range(heads):
            dk[h] = jnp.zeros(dk.shape[1:], F32)
            dv[h] = jnp.zeros(dv.shape[1:], F32)

        def per_query(i, inner):
            src, cols = (i % GROUP, block_cols(i))
            allowed = pair_mask(seg_col, seg_row, j, i)
            spots = [slice(h * HEAD_DIM, (h + 1) * HEAD_DIM) for h in range(heads)]
            old_dv = [dv[h] for h in range(heads)]
            old_dk = [dk[h] for h in range(heads)]
            old_dq = [dq[h, i] for h in range(heads)]
            queries = [x_ref[src, spot, cols] for spot in spots]
            grads = [go_ref[src, spot, cols] for spot in spots]
            scores = [mm(keys_nat[h, j], queries[h], 1, 0) for h in range(heads)]
            grad_probs = [mm(values_nat[h, j], grads[h], 1, 0) for h in range(heads)]
            probs = [
                jnp.exp(jnp.where(allowed, scores[h], masked_score) - lse_ref[h, i]) for h in range(heads)
            ]
            grad_scores = [
                (probs[h] * (grad_probs[h] - delta[h, i])).astype(BF16) for h in range(heads)
            ]
            add_dv = [mm(grads[h], probs[h].astype(BF16), 1, 1) for h in range(heads)]
            add_dk = [mm(queries[h], grad_scores[h], 1, 1) for h in range(heads)]
            add_dq = [
                mm(x_ref[key_src, width + h * HEAD_DIM : width + (h + 1) * HEAD_DIM, key_cols], grad_scores[h], 1, 0)
                for h in range(heads)
            ]
            for h in range(heads):
                dv[h] = old_dv[h] + add_dv[h]
                dk[h] = old_dk[h] + add_dk[h]
                dq[h, i] = old_dq[h] + add_dq[h]
            return inner

        lax.fori_loop(lo_ref[j], hi_ref[j], per_query, 0)
        for h in range(heads):
            low, high = (h * HEAD_DIM, (h + 1) * HEAD_DIM)
            dx_ref[key_src, width + low : width + high, key_cols] = dk[h].astype(BF16)
            dx_ref[key_src, 2 * width + low : 2 * width + high, key_cols] = dv[h].astype(BF16)
        return carry

    lax.fori_loop(0, blocks, per_key, 0)

    def finish(block, carry):
        src, cols = (block % GROUP, block_cols(block))
        for h in range(heads):
            dx_ref[src, h * HEAD_DIM : (h + 1) * HEAD_DIM, cols] = (dq[h, block] * 0.125).astype(BF16)
        return carry

    lax.fori_loop(0, blocks, finish, 0)


def in_vmem(count):
    return [pl.BlockSpec(memory_space=pltpu.VMEM)] * count


def attend(qkv, spans, seg_col, seg_row):
    heads = qkv.shape[1] // (3 * HEAD_DIM)
    blocks = seg_row.shape[0]
    return pl.pallas_call(
        attend_kernel,
        name="attend",
        out_shape=(
            jax.ShapeDtypeStruct((GROUP, heads * HEAD_DIM, qkv.shape[2]), BF16),
            jax.ShapeDtypeStruct((GROUP, heads * HEAD_DIM, qkv.shape[2]), F32),
            jax.ShapeDtypeStruct((heads, blocks, 1, BLOCK), F32),
        ),
        in_specs=[pl.BlockSpec(memory_space=pltpu.SMEM)] * 2 + in_vmem(3),
        out_specs=in_vmem(3),
        scratch_shapes=[
            pltpu.VMEM((heads, blocks, BLOCK, HEAD_DIM), BF16),
            pltpu.VMEM((heads, HEAD_DIM, BLOCK), F32),
            pltpu.VMEM((heads, 1, BLOCK), F32),
            pltpu.VMEM((heads, 1, BLOCK), F32),
        ],
    )(*spans, qkv, seg_col, seg_row)


def attend_back(qkv, grad_out, out, lse, spans, seg_col, seg_row):
    heads = qkv.shape[1] // (3 * HEAD_DIM)
    blocks = seg_row.shape[0]
    return pl.pallas_call(
        attend_back_kernel,
        name="attend_back",
        out_shape=jax.ShapeDtypeStruct(qkv.shape, BF16),
        in_specs=[pl.BlockSpec(memory_space=pltpu.SMEM)] * 2 + in_vmem(6),
        out_specs=in_vmem(1)[0],
        scratch_shapes=[
            pltpu.VMEM((heads, blocks, BLOCK, HEAD_DIM), BF16),
            pltpu.VMEM((heads, blocks, BLOCK, HEAD_DIM), BF16),
            pltpu.VMEM((heads, blocks, 1, BLOCK), F32),
            pltpu.VMEM((heads, blocks, HEAD_DIM, BLOCK), F32),
            pltpu.VMEM((heads, HEAD_DIM, BLOCK), F32),
            pltpu.VMEM((heads, HEAD_DIM, BLOCK), F32),
        ],
    )(*spans, qkv, grad_out, out, lse, seg_col, seg_row)


def norm_rows(tensor, gain, shift):
    center = tensor - jnp.mean(tensor, axis=-1, keepdims=True)
    inverse = lax.rsqrt(jnp.mean(center * center, axis=-1, keepdims=True) + norm_eps)
    normed = center * inverse
    return (normed * gain + shift, normed, inverse)


def norm_rows_back(grad, normed, inverse, gain):
    scaled = grad * gain
    inner = (
        scaled
        - jnp.mean(scaled, axis=-1, keepdims=True)
        - normed * jnp.mean(scaled * normed, axis=-1, keepdims=True)
    )
    return (inner * inverse, jnp.sum(grad * normed, axis=0), jnp.sum(grad, axis=0))


def fast_forward(hidden, weights, vecs, spans, seg_col, seg_row):
    query_b, value_b, proj_b, attn_g, attn_s, down_b, ffn_g, ffn_s, up_b = vecs
    width = hidden.shape[1]
    hidden_low = hidden.astype(BF16)
    qkv_w, later = weights
    mixed = mm(qkv_w, hidden_low, 0, 1)
    query = (mixed[:width] + query_b[:, None]).astype(BF16) * BF16(0.125)
    keys = mixed[width : 2 * width].astype(BF16)
    values = (mixed[2 * width :] + value_b[:, None]).astype(BF16)
    share = width // GROUP
    packed = jnp.concatenate(
        [part.reshape(GROUP, share, part.shape[1]) for part in (query, keys, values)], axis=1
    )
    proj_w, up_w, down_w, qkv = later(packed)
    low, out, lse = attend(qkv, spans, seg_col, seg_row)
    context = swap(low).reshape(width, low.shape[2])
    attn_out = mm(context, proj_w, 0, 0) + proj_b
    settled, normed_one, inverse_one = norm_rows(hidden + attn_out, attn_g, attn_s)
    settled_low = settled.astype(BF16)
    before = mm(settled_low, up_w, 1, 0) + up_b
    below = 0.5 * (1.0 + lax.erf(before * 0.7071067811865476))
    active = (before * below).astype(BF16)
    slope = (below + before * jnp.exp(-0.5 * before * before) * 0.3989422804014327).astype(BF16)
    ffn_out = mm(active, down_w, 1, 0) + down_b
    result, normed_two, inverse_two = norm_rows(settled + ffn_out, ffn_g, ffn_s)
    return result, (qkv_w, proj_w, up_w, down_w), (
        hidden_low, qkv, out, lse, context, normed_one, inverse_one, settled_low,
        active, slope, normed_two, inverse_two,
    )


def fast_backward(grad, weights, vecs, saved, spans, seg_col, seg_row):
    query_b, value_b, proj_b, attn_g, attn_s, down_b, ffn_g, ffn_s, up_b = vecs
    qkv_w, proj_w, up_w, down_w = weights
    (
        hidden_low, qkv, out, lse, context, normed_one, inverse_one, settled_low,
        active, slope, normed_two, inverse_two,
    ) = saved
    width = grad.shape[1]
    grad_two, ffn_g_sum, ffn_s_sum = norm_rows_back(grad, normed_two, inverse_two, ffn_g)
    grad_ffn = grad_two.astype(BF16)
    down_b_sum = jnp.sum(grad_ffn.astype(F32), axis=0)
    grad_before = (mm(grad_ffn, down_w, 1, 1) * slope.astype(F32)).astype(BF16)
    down_grad = mm(active, grad_ffn, 0, 0).astype(BF16)
    up_grad = mm(settled_low, grad_before, 0, 0).astype(BF16)
    up_b_sum = jnp.sum(grad_before.astype(F32), axis=0)
    grad_settled = grad_two + mm(grad_before, up_w, 1, 1)
    grad_one, attn_g_sum, attn_s_sum = norm_rows_back(grad_settled, normed_one, inverse_one, attn_g)
    grad_attn = grad_one.astype(BF16)
    proj_b_sum = jnp.sum(grad_attn.astype(F32), axis=0)
    grad_context = mm(proj_w, grad_attn, 1, 1).astype(BF16)
    proj_grad = mm(context, grad_attn, 1, 0).astype(BF16)
    grad_out = swap(grad_context.reshape(GROUP, width // GROUP, grad_context.shape[1]))
    moved = swap(attend_back(qkv, grad_out, out, lse, spans, seg_col, seg_row))
    share = width // GROUP
    mixed = jnp.transpose(moved.reshape(GROUP, 3, share, moved.shape[2]), (1, 0, 2, 3))
    mixed = mixed.reshape(3 * width, moved.shape[2])
    qkv_grad = mm(hidden_low, mixed, 0, 1).astype(BF16)
    grad_hidden = grad_one + mm(mixed, qkv_w, 0, 1)
    mixed_sum = jnp.sum(mixed.astype(F32), axis=1)
    sums = [
        mixed_sum[:width], mixed_sum[2 * width :], proj_b_sum, attn_g_sum, attn_s_sum, down_b_sum,
        ffn_g_sum, ffn_s_sum,
    ]
    sums += [up_b_sum[part * width : (part + 1) * width] for part in range(up_w.shape[1] // width)]
    return grad_hidden, (qkv_grad, proj_grad, up_grad, down_grad), sums


MESH = pl.DeviceIdType.MESH


def places():
    rep, shard = (lax.axis_index("rep"), lax.axis_index("shard"))
    core, y, z = (lax.rem(rep, 2), lax.rem(shard, 2), lax.div(shard, 2))
    across_x = lax.rem(rep + 2, 4)
    across_core = rep + 1 - 2 * core
    zs = (z, z + 1 - 2 * lax.rem(z, 2), lax.rem(z + 2, 4), 3 - z)
    return (rep, shard, core, y, across_x, across_core, zs)


def greet(diagonal=False):
    rep, shard, core, y, across_x, across_core, zs = places()
    barrier = pltpu.get_barrier_semaphore()
    partners = [(rep, 2 * other + y) for other in zs[1:]]
    partners += [(rep, 2 * zs[0] + 1 - y), (across_x, shard), (across_core, shard)]
    if diagonal:
        partners += [(rep, 2 * other + 1 - y) for other in zs[1:]]
    for partner in partners:
        pl.semaphore_signal(barrier, inc=1, device_id=partner, device_id_type=MESH)
    pl.semaphore_wait(barrier, len(partners))


class Sends:
    def __init__(self, sems):
        self.sems = sems
        self.copies = []

    def push(self, source, target, arrived, device):
        copy = pltpu.make_async_remote_copy(
            source, target, self.sems.at[len(self.copies)], arrived, device_id=device, device_id_type=MESH
        )
        copy.start()
        self.copies.append(copy)

    def finish(self):
        for copy in self.copies:
            copy.wait_send()


def gather_kernel(fourths, smalls, swaps, *refs):
    count = fourths + smalls
    total = count + swaps
    owns, fulls = (refs[:total], refs[total : 2 * total])
    local_sems, send_sems, fourth_sems, small_sems, swap_sems = refs[2 * total :]
    rep, shard, core, y, across_x, across_core, zs = places()
    member = lax.rem(shard, GROUP)
    greet(smalls + swaps > 0)
    sends = Sends(send_sems)
    beside, past_x, past_core = ((rep, 2 * zs[0] + 1 - y), (across_x, shard), (across_core, shard))

    def send(n, chunk, part, device, own=False):
        target = fulls[n].at[chunk, part]
        source = owns[n].at[part] if own else target
        sends.push(source, target, fourth_sems.at[n, chunk, part], device)

    def arrive(n, chunk, part):
        piece = fulls[n].at[chunk, part]
        pltpu.make_async_copy(piece, piece, fourth_sems.at[n, chunk, part]).wait()

    near_members = ((1, y), (0, 1 - y), (1, 1 - y))
    for n in range(smalls):
        for k in range(4):
            for other in (y, 1 - y) if k else (1 - y,):
                sends.push(
                    owns[fourths + n],
                    fulls[fourths + n].at[shard],
                    small_sems.at[shard],
                    (rep, 2 * zs[k] + other),
                )
    for n in range(fourths):
        send(n, shard, rep, beside, True)
        for k in (1, 2, 3):
            send(n, shard, rep, (rep, 2 * zs[k] + y), True)
    for n in range(swaps):
        for k, other in near_members:
            target = 2 * zs[k] + other
            sends.push(
                owns[count + n].at[lax.rem(target, GROUP)],
                fulls[count + n].at[member],
                swap_sems.at[n, member],
                (rep, target),
            )
    local = [
        pltpu.make_async_copy(owns[n], fulls[n].at[shard], local_sems.at[n]) for n in range(count)
    ]
    local += [
        pltpu.make_async_copy(owns[n].at[member], fulls[n].at[member], local_sems.at[n])
        for n in range(count, total)
    ]
    for copy in local:
        copy.start()

    events = ((0, 1), (1, 0), (2, 0), (1, 1), (3, 0), (2, 1), (3, 1))
    chunks = [2 * zs[k] + (1 - y if far else y) for k, far in events]

    def from_x(chunk):
        for n in range(fourths):
            arrive(n, chunk, across_x)
            send(n, chunk, across_x, past_core)

    for at, (chunk, (k, far)) in enumerate(zip(chunks, events)):
        for n in range(fourths):
            arrive(n, chunk, rep)
            if not far:
                send(n, chunk, rep, beside)
            send(n, chunk, rep, past_x)
            send(n, chunk, rep, past_core)
        if at >= 3:
            from_x(chunks[at - 3])
    for chunk in chunks[-3:]:
        from_x(chunk)
    for chunk in chunks:
        for n in range(fourths):
            arrive(n, chunk, across_core)
            arrive(n, chunk, lax.rem(across_core + 2, 4))
        for n in range(smalls):
            piece = fulls[fourths + n].at[chunk]
            pltpu.make_async_copy(piece, piece, small_sems.at[chunk]).wait()
    for n in range(swaps):
        for k, other in near_members:
            source = lax.rem(2 * zs[k] + other, GROUP)
            piece = fulls[count + n].at[source]
            pltpu.make_async_copy(piece, piece, swap_sems.at[n, source]).wait()
    for copy in local:
        copy.wait()
    sends.finish()


def gather_fast(fourths, smalls, swaps, name, collective_id):
    split = [item.reshape(4, item.shape[0] // 4, item.shape[1]) for item in fourths] + smalls
    owns = split + swaps
    dma = pltpu.SemaphoreType.DMA
    fulls = pl.pallas_call(
        functools.partial(gather_kernel, len(fourths), len(smalls), len(swaps)),
        name=name,
        out_shape=[jax.ShapeDtypeStruct((8,) + item.shape, BF16) for item in split]
        + [jax.ShapeDtypeStruct(item.shape, BF16) for item in swaps],
        in_specs=in_vmem(len(owns)),
        out_specs=[pl.BlockSpec(memory_space=pl.ANY)] * len(owns),
        scratch_shapes=[
            dma((len(owns),)),
            dma((28 * len(fourths) + 7 * len(smalls) + 3 * len(swaps),)),
            dma((len(fourths), 8, 4)),
            dma((8,)),
            dma((max(1, len(swaps)), GROUP)),
        ],
        compiler_params=pltpu.CompilerParams(collective_id=collective_id, has_side_effects=True),
    )(*owns)
    wide = len(fourths)
    return [item.reshape(-1, item.shape[3]) for item in fulls[:wide]] + list(fulls[wide:])


def reduce_kernel(
    qkv_grad, proj_grad, down_grad, small, qkv_out, proj_out, down_out, small_out, *scratch
):
    kinds = 2
    mats, core_mats, x_mats, y_mats, z_mats, x_stage, y_stage, z_stage, all_mats = [
        scratch[kinds * n : kinds * n + kinds] for n in range(9)
    ]
    (
        small_sum, small_got, local_sems, send_sems, core_sems, x_sems, y_sems, z_sems, all_sems, small_sems,
    ) = scratch[9 * kinds :]
    rep, shard, core, y, across_x, across_core, zs = places()
    x = lax.div(rep, 2)
    beside, past_x, past_core = ((rep, 2 * zs[0] + 1 - y), (across_x, shard), (across_core, shard))
    cut = qkv_grad.shape[3]
    local = [
        pltpu.make_async_copy(qkv_grad, mats[0].at[:, :, :, :cut], local_sems.at[0]),
        pltpu.make_async_copy(proj_grad, mats[0].at[:, :, :, cut:], local_sems.at[1]),
        pltpu.make_async_copy(down_grad, mats[1], local_sems.at[2]),
    ]
    for copy in local:
        copy.start()
    small_sum[0] = small[...]
    greet()
    sends = Sends(send_sems)

    def arrive(ref, sem):
        pltpu.make_async_copy(ref, ref, sem).wait()

    def chunk_of(k, far):
        return 2 * zs[k] + (1 - y if far else y)

    def add(target, parts):
        steps = 6
        lanes = target.shape[1] // steps

        def body(step, carry):
            at = pl.ds(pl.multiple_of(step * lanes, lanes), lanes)
            total = parts[0][:, at].astype(F32)
            for part in parts[1:]:
                total = total + part[:, at].astype(F32)
            target[:, at] = total.astype(BF16)
            return carry

        lax.fori_loop(0, steps, body, 0)

    small_partners = (past_core, past_x, beside, (rep, 2 * zs[1] + y), (rep, 2 * zs[2] + y))

    def small_send(step):
        sends.push(small_sum.at[step], small_got.at[step], small_sems.at[step], small_partners[step])

    def small_step(step):
        arrive(small_got.at[step], small_sems.at[step])
        small_sum[step + 1] = small_sum[step] + small_got[step]
        if step + 1 < len(small_partners):
            small_send(step + 1)

    small_send(0)
    far = [(k, 1) for k in (2, 3, 1, 0)]
    near = [(k, 0) for k in (2, 3, 1)]
    own = (0, 0)
    for copy in local:
        copy.wait()
    for place in far + near + [own]:
        chunk = chunk_of(*place)
        for n in range(kinds):
            for which in (1 - x, x):
                sends.push(
                    mats[n].at[chunk, 2 * which + 1 - core],
                    core_mats[n].at[chunk, which],
                    core_sems.at[n, chunk, which],
                    past_core,
                )

    def step_x(slot, place):
        chunk = chunk_of(*place)
        for n in range(kinds):
            arrive(core_mats[n].at[chunk, 1 - x], core_sems.at[n, chunk, 1 - x])
            add(x_stage[n].at[slot], [mats[n].at[chunk, across_x], core_mats[n].at[chunk, 1 - x]])
            sends.push(x_stage[n].at[slot], x_mats[n].at[chunk], x_sems.at[n, chunk], past_x)

    def parts_of(n, chunk):
        arrive(core_mats[n].at[chunk, x], core_sems.at[n, chunk, x])
        arrive(x_mats[n].at[chunk], x_sems.at[n, chunk])
        return [mats[n].at[chunk, rep], core_mats[n].at[chunk, x], x_mats[n].at[chunk]]

    def step_y(place):
        k = place[0]
        for n in range(kinds):
            add(y_stage[n].at[k], parts_of(n, chunk_of(*place)))
            sends.push(y_stage[n].at[k], y_mats[n].at[k], y_sems.at[n, k], beside)

    def step_z(place):
        k = place[0]
        for n in range(kinds):
            parts = parts_of(n, chunk_of(*place))
            arrive(y_mats[n].at[k], y_sems.at[n, k])
            add(z_stage[n].at[k - 1], parts + [y_mats[n].at[k]])
            sends.push(
                z_stage[n].at[k - 1], z_mats[n].at[k - 1], z_sems.at[n, k - 1], (rep, 2 * zs[k] + y)
            )

    step_x(0, far[0])
    step_x(1, far[1])
    step_x(2, far[2])
    small_step(0)
    step_y(far[0])
    step_x(3, far[3])
    step_y(far[1])
    step_x(4, near[0])
    small_step(1)
    step_y(far[2])
    step_x(5, near[1])
    step_y(far[3])
    step_x(6, near[2])
    small_step(2)
    step_z(near[0])
    step_x(7, own)
    step_z(near[1])
    small_step(3)
    step_z(near[2])
    small_step(4)
    small_out[...] = small_sum[len(small_partners)]

    for n in range(kinds):
        parts = parts_of(n, shard)
        arrive(y_mats[n].at[0], y_sems.at[n, 0])
        for k in range(3):
            arrive(z_mats[n].at[k], z_sems.at[n, k])
        mine = all_mats[n].at[rep]
        add(mine, parts + [y_mats[n].at[0]] + [z_mats[n].at[k] for k in range(3)])
        sends.push(mine, mine, all_sems.at[n, rep], past_x)
        sends.push(mine, mine, all_sems.at[n, rep], past_core)
    for n in range(kinds):
        theirs = all_mats[n].at[across_x]
        arrive(theirs, all_sems.at[n, across_x])
        sends.push(theirs, theirs, all_sems.at[n, across_x], past_core)
    opposite = lax.rem(across_core + 2, 4)
    for n in range(kinds):
        arrive(all_mats[n].at[across_core], all_sems.at[n, across_core])
        arrive(all_mats[n].at[opposite], all_sems.at[n, opposite])
    rows = mats[0].shape[2]
    tall = mats[1].shape[2]
    for q in range(4):
        qkv_out[q * rows : (q + 1) * rows, :] = all_mats[0][q, :, :cut].astype(F32)
        proj_out[q * rows : (q + 1) * rows, :] = all_mats[0][q, :, cut:].astype(F32)
        down_out[q * tall : (q + 1) * tall, :] = all_mats[1][q].astype(F32)
    sends.finish()


def reduce_fast(qkv_grad, proj_grad, down_grad, small):
    rows, tall = (proj_grad.shape[0] // 32, down_grad.shape[0] // 32)
    wide = qkv_grad.shape[1] + proj_grad.shape[1]
    sizes = ((rows, wide), (tall, down_grad.shape[1]))
    buffers = []
    for lead in ((8, 4), (8, 2), (8,), (4,), (3,), (8,), (4,), (3,), (4,)):
        buffers += [pltpu.VMEM(lead + size, BF16) for size in sizes]
    dma = pltpu.SemaphoreType.DMA
    return pl.pallas_call(
        reduce_kernel,
        name="reduce",
        out_shape=(
            jax.ShapeDtypeStruct((4 * rows, qkv_grad.shape[1]), F32),
            jax.ShapeDtypeStruct((4 * rows, proj_grad.shape[1]), F32),
            jax.ShapeDtypeStruct((4 * tall, down_grad.shape[1]), F32),
            jax.ShapeDtypeStruct(small.shape, F32),
        ),
        in_specs=[pl.BlockSpec(memory_space=pl.ANY)] * 3 + in_vmem(1),
        out_specs=in_vmem(4),
        scratch_shapes=buffers
        + [
            pltpu.VMEM((6,) + small.shape, F32), pltpu.VMEM((5,) + small.shape, F32),
            dma((3,)), dma((2 * 34 + 5,)), dma((2, 8, 2)), dma((2, 8)), dma((2, 4)), dma((2, 3)),
            dma((2, 4)), dma((5,)),
        ],
        compiler_params=pltpu.CompilerParams(
            collective_id=1, has_side_effects=True, vmem_limit_bytes=56 * 1024 * 1024
        ),
    )(
        qkv_grad.reshape(8, 4, rows, -1), proj_grad.reshape(8, 4, rows, -1),
        down_grad.reshape(8, 4, tall, -1), small,
    )


def by_rep(grad, width):
    blocks = grad.shape[1] // width
    split = grad.reshape(8, 4, grad.shape[0] // 32, blocks, width)
    return jnp.transpose(split, (1, 0, 3, 2, 4)).reshape(4, 8, grad.size // (32 * width), width)


def scatter_all(grads, width):
    packed = jnp.concatenate([by_rep(grad, width) for grad in grads], axis=2)
    flat = packed.reshape(-1, width)
    return lax.psum_scatter(flat, ("rep", "shard"), scatter_dimension=0, tiled=True)


def spread_rep(piece):
    rep = lax.axis_index("rep")
    for bit in range(2):
        other = exchange(piece, "rep", 1 << bit)
        piece = ordered((rep >> bit) & 1 == 0, piece, other)
    return piece.reshape((4,) + piece.shape[2:])


def unpack(pieces, start, blocks, rows):
    parts = [pieces[:, start + b * rows : start + (b + 1) * rows] for b in range(blocks)]
    return jnp.concatenate([part.reshape(-1, part.shape[2]) for part in parts], axis=1).astype(F32)


def on_device_fast(
    inputs, cotangent, segment_ids, memory_slot, memory_table,
    qkv_weight, query_bias, value_bias, proj_weight, proj_bias, attn_gain, attn_shift,
    up_weight, up_bias, down_weight, down_bias, ffn_gain, ffn_shift,
):
    index = lax.axis_index("shard")
    width = inputs.shape[2]
    share = memory_table.shape[1]
    ups = up_weight.shape[2] // width

    vec_args = (
        query_bias, value_bias, proj_bias, attn_gain, attn_shift, down_bias, ffn_gain, ffn_shift,
    )
    plain = len(vec_args)
    rows = [item[layer][None] for layer in range(LAYERS) for item in vec_args]
    rows += [up_bias[layer].reshape(ups, share) for layer in range(LAYERS)]
    rows.append(memory_table)
    small = jnp.concatenate(rows, axis=0)
    used = small.shape[0]
    small = jnp.pad(small, ((0, -used % 16), (0, 128 - share)))
    first_qkv, small = gather_fast([qkv_weight[0]], [small], [], "gather_first", 0)
    small = small[:, :used, :share].astype(F32)
    wide = jnp.transpose(small, (1, 0, 2)).reshape(used, width)
    vecs = []
    for layer in range(LAYERS):
        start = LAYERS * plain + layer * ups
        vecs.append(
            [wide[layer * plain + item] for item in range(plain)]
            + [small[:, start : start + ups].reshape(ups * width)]
        )
    table = wide[LAYERS * (plain + ups) :].astype(BF16)

    second_qkv = []

    def rest_first(packed):
        proj_w, up_w, qkv_w, down_w, qkv = gather_fast(
            [proj_weight[0], up_weight[0], qkv_weight[1], down_weight[0]], [], [packed],
            "gather_middle", 2,
        )
        second_qkv.append(qkv_w)
        return proj_w, up_w, down_w, qkv

    def rest_second(packed):
        return gather_fast(
            [proj_weight[1], up_weight[1], down_weight[1]], [], [packed], "gather_last", 3
        )

    rests = (rest_first, rest_second)

    segs = jnp.where(index < GROUP, segment_ids[0], segment_ids[1])
    tiles = segs.reshape(-1, BLOCK)
    first, last = (tiles[:, 0], tiles[:, -1])
    spans = (
        jnp.sum((last[None, :] < first[:, None]).astype(jnp.int32), axis=1),
        jnp.sum((first[None, :] <= last[:, None]).astype(jnp.int32), axis=1),
    )
    seg_row = tiles[:, None, :]
    seg_col = jnp.broadcast_to(segs[:, None], (segs.shape[0], 128))

    slots = to_groups(memory_slot[..., None], index)[:, 0]
    slot_hot = slots[:, None] == jnp.arange(MEMS, dtype=jnp.int32)
    hidden = to_groups(inputs, index).astype(F32) + mm(slot_hot.astype(BF16), table, 1, 0)
    saved, held = ([], [])
    for layer in range(LAYERS):
        qkv_w = second_qkv[0] if layer else first_qkv
        hidden, mats, state = fast_forward(
            hidden, (qkv_w, rests[layer]), vecs[layer], spans, seg_col, seg_row
        )
        saved.append(state)
        held.append(mats)
    layer_output = from_groups(hidden, index)

    grad = to_groups(cotangent, index).astype(F32)
    sums, shares = ([None] * LAYERS, [None] * LAYERS)
    for layer in range(LAYERS - 1, -1, -1):
        grad, (qkv_grad, proj_grad, up_grad, down_grad), sums[layer] = fast_backward(
            grad, held[layer], vecs[layer], saved[layer], spans, seg_col, seg_row
        )
        if layer:
            early = scatter_all([up_grad, down_grad], width)
            waiting = [qkv_grad, proj_grad]
    late = scatter_all(waiting + [up_grad], width)
    input_grad = from_groups(grad, index)
    memory_sum = lax.dot_general(
        slot_hot.astype(F32), grad, (((0,), (0,)), ((), ())), precision=lax.Precision.HIGHEST
    )
    flat = jnp.concatenate([jnp.stack(sums[layer]) for layer in range(LAYERS)] + [memory_sum], axis=0)
    used = flat.shape[0]
    flat = jnp.pad(flat, ((0, -used % 8), (0, 0)))
    qkv_own, proj_own, down_own, flat = reduce_fast(qkv_grad, proj_grad, down_grad, flat)
    flat = flat[:used]
    rows, tall = (width // 32, width * ups // 32)
    early, late = (spread_rep(early), spread_rep(late))
    shares[1] = (
        unpack(late, 0, 3, rows),
        unpack(late, 3 * rows, 1, rows),
        unpack(early, 0, ups, rows),
        unpack(early, ups * rows, 1, tall),
    )
    shares[0] = (qkv_own, proj_own, unpack(late, 4 * rows, ups, rows), down_own)
    per = plain + ups
    own = lax.dynamic_slice_in_dim(flat, index * share, share, 1)
    vec_grads = [
        jnp.stack([own[layer * per + item] for layer in range(LAYERS)]) for item in range(plain)
    ]
    up_sums = jnp.stack([flat[layer * per + plain : (layer + 1) * per].reshape(-1) for layer in range(LAYERS)])
    upbias_grad = lax.dynamic_slice_in_dim(up_sums, index * share * ups, share * ups, 1)
    memory_grad = own[LAYERS * per :]

    def wide_grad(member):
        return jnp.stack([shares[layer][member] for layer in range(LAYERS)])

    return (
        layer_output,
        input_grad,
        memory_grad,
        wide_grad(0),
        vec_grads[0],
        vec_grads[1],
        wide_grad(1),
        vec_grads[2],
        vec_grads[3],
        vec_grads[4],
        wide_grad(2),
        upbias_grad,
        wide_grad(3),
        vec_grads[5],
        vec_grads[6],
        vec_grads[7],
    )


def fast_fits(mesh):
    return mesh.shape["shard"] == 2 * GROUP and mesh.shape["rep"] == 4


def solution(mesh):
    return jax.shard_map(
        on_device_fast if fast_fits(mesh) else on_device,
        mesh=mesh,
        in_specs=(
            P(None, ("rep", "shard"), None),
            P(None, ("rep", "shard"), None),
            P(None, "rep"),
            P(None, ("rep", "shard")),
            P(None, "shard"),
            P(None, "shard", None),
            P(None, "shard"),
            P(None, "shard"),
            P(None, "shard", None),
            P(None, "shard"),
            P(None, "shard"),
            P(None, "shard"),
            P(None, "shard", None),
            P(None, "shard"),
            P(None, "shard", None),
            P(None, "shard"),
            P(None, "shard"),
            P(None, "shard"),
        ),
        out_specs=(
            P(None, ("rep", "shard"), None),
            P(None, ("rep", "shard"), None),
            P(None, "shard"),
            P(None, "shard", None),
            P(None, "shard"),
            P(None, "shard"),
            P(None, "shard", None),
            P(None, "shard"),
            P(None, "shard"),
            P(None, "shard"),
            P(None, "shard", None),
            P(None, "shard"),
            P(None, "shard", None),
            P(None, "shard"),
            P(None, "shard"),
            P(None, "shard"),
        ),
        check_vma=False,
    )
```

```python
import functools

import jax
import jax.numpy as jnp
from jax import lax
from jax.experimental import pallas as pl
from jax.experimental.pallas import tpu as pltpu
from jax.sharding import PartitionSpec as P

HEADS = 12
HEAD_DIM = 64
LAYERS = 2
MEMS = 20
REACH = 4


norm_eps = 1e-12
masked_score = -1e30


def passed_along(block, axis, distance):
    devices = range(lax.axis_size(axis))
    route = [(i - distance, i) for i in devices if i - distance in devices]
    return lax.ppermute(block, axis, route)


def layer_norm(tensor, norm_gain, norm_shift):
    center = tensor - jnp.mean(tensor, axis=-1, keepdims=True)
    inverse = lax.rsqrt(jnp.mean(center * center, axis=-1, keepdims=True) + norm_eps)
    normed = center * inverse
    return (normed * norm_gain + norm_shift, normed, inverse)


def norm_backward(grad_out, normed, inverse, norm_gain):
    scaled = grad_out * norm_gain
    inner_term = (
        scaled
        - jnp.mean(scaled, axis=-1, keepdims=True)
        - normed * jnp.mean(scaled * normed, axis=-1, keepdims=True)
    )
    return (
        inner_term * inverse,
        jnp.sum(grad_out * normed, axis=(0, 1)),
        jnp.sum(grad_out, axis=(0, 1)),
    )


def gelu_exact(tensor):
    return jax.nn.gelu(tensor, approximate=False)


def split_heads(tensor):
    return tensor.reshape(tensor.shape[0], tensor.shape[1], HEADS, HEAD_DIM)


def merge_heads(tensor):
    return tensor.reshape(tensor.shape[0], tensor.shape[1], HEADS * HEAD_DIM)


def product(left_side, right_side):
    return jnp.einsum("btd,de->bte", left_side, right_side, preferred_element_type=jnp.float32)


def product_back(left_side, right_side):
    return jnp.einsum("bte,de->btd", left_side, right_side, preferred_element_type=jnp.float32)


def weight_grad(left_side, right_side):
    return jnp.einsum("btd,bte->de", left_side, right_side, preferred_element_type=jnp.float32)


def token_sum(tensor):
    return jnp.sum(tensor.astype(jnp.float32), axis=(0, 1))


def piece_mask(segment_ids, seg_here, my_index, shards, row_count, offset):
    target = my_index + offset
    inside = jnp.logical_and(target >= 0, target < shards)
    start_row = jnp.clip(target, 0, shards - 1) * row_count
    seg_there = lax.dynamic_slice_in_dim(segment_ids, start_row, row_count, 1)
    key_mask = jnp.logical_and(seg_here[:, None, :, None] == seg_there[:, None, None, :], inside)
    return (key_mask, jnp.any(key_mask))


def scaled_scores(query_heads, key_part, key_mask):
    scores = (
        jnp.einsum(
            "bqhe,bkhe->bhqk",
            query_heads,
            split_heads(key_part),
            preferred_element_type=jnp.float32,
        )
        * 0.125
    )
    return jnp.where(key_mask, scores, masked_score)


def stats_update(carry_in, query_heads, key_part, key_mask):
    old_max, old_sum = carry_in
    scores = scaled_scores(query_heads, key_part, key_mask)
    new_max = jnp.maximum(old_max, jnp.max(scores, axis=-1))
    fresh = jnp.sum(jnp.where(key_mask, jnp.exp(scores - new_max[..., None]), 0.0), axis=-1)
    return (new_max, old_sum * jnp.exp(old_max - new_max) + fresh)


def stats_keep(carry_in, query_heads, key_part, key_mask):
    return carry_in


def mix_update(context, query_heads, key_part, value_part, key_mask, log_sum):
    scores = scaled_scores(query_heads, key_part, key_mask)
    soft_probs = jnp.where(key_mask, jnp.exp(scores - log_sum[..., None]), 0.0).astype(jnp.bfloat16)
    return context + jnp.einsum(
        "bhqk,bkhe->bqhe", soft_probs, split_heads(value_part), preferred_element_type=jnp.float32
    )


def mix_keep(context, query_heads, key_part, value_part, key_mask, log_sum):
    return context


def piece_update(
    grad_query, query_heads, grad_heads, key_part, value_part, key_mask, log_sum, row_delta
):
    scores = scaled_scores(query_heads, key_part, key_mask)
    soft_probs = jnp.where(key_mask, jnp.exp(scores - log_sum[..., None]), 0.0)
    grad_probs = jnp.einsum(
        "bqhe,bkhe->bhqk", grad_heads, split_heads(value_part), preferred_element_type=jnp.float32
    )
    grad_scores = (soft_probs * (grad_probs - row_delta[..., None])).astype(jnp.bfloat16)
    grad_query = grad_query + jnp.einsum(
        "bhqk,bkhe->bqhe", grad_scores, split_heads(key_part), preferred_element_type=jnp.float32
    )
    key_grad = jnp.einsum(
        "bhqk,bqhe->bkhe", grad_scores, query_heads, preferred_element_type=jnp.float32
    )
    value_grad = jnp.einsum(
        "bhqk,bqhe->bkhe",
        soft_probs.astype(jnp.bfloat16),
        grad_heads,
        preferred_element_type=jnp.float32,
    )
    return (grad_query, merge_heads(key_grad), merge_heads(value_grad))


def piece_skip(
    grad_query, query_heads, grad_heads, key_part, value_part, key_mask, log_sum, row_delta
):
    empty = jnp.zeros(key_part.shape, jnp.float32)
    return (grad_query, empty, empty)


def attend_forward(query_rows, key_rows, value_rows, offsets, key_masks):
    micro_count, row_count = (query_rows.shape[0], query_rows.shape[1])
    query_heads = split_heads(query_rows)
    pieces = [(key_rows, value_rows)]
    for offset in offsets:
        pieces.append(passed_along((key_rows, value_rows), "shard", -offset))
    row_max = jnp.full((micro_count, HEADS, row_count), masked_score, jnp.float32)
    row_sum = jnp.zeros((micro_count, HEADS, row_count), jnp.float32)
    for (key_part, value_part), (key_mask, is_live) in zip(pieces, key_masks):
        row_max, row_sum = lax.cond(
            is_live, stats_update, stats_keep, (row_max, row_sum), query_heads, key_part, key_mask
        )
    log_sum = row_max + jnp.log(row_sum)
    context = jnp.zeros((micro_count, row_count, HEADS, HEAD_DIM), jnp.float32)
    for (key_part, value_part), (key_mask, is_live) in zip(pieces, key_masks):
        context = lax.cond(
            is_live,
            mix_update,
            mix_keep,
            context,
            query_heads,
            key_part,
            value_part,
            key_mask,
            log_sum,
        )
    return (merge_heads(context), log_sum, pieces)


def attend_backward(query_rows, grad_context, context, log_sum, pieces, key_masks, offsets):
    query_heads = split_heads(query_rows)
    grad_heads = split_heads(grad_context)
    row_delta = jnp.transpose(
        jnp.sum(split_heads(grad_context.astype(jnp.float32) * context), axis=-1), (0, 2, 1)
    )
    grad_query = jnp.zeros(query_heads.shape, jnp.float32)
    own_keys = jnp.zeros(query_rows.shape, jnp.float32)
    own_values = jnp.zeros(query_rows.shape, jnp.float32)
    for index_num in range(len(pieces)):
        key_part, value_part = pieces[index_num]
        key_mask, is_live = key_masks[index_num]
        grad_query, key_grad, value_grad = lax.cond(
            is_live,
            piece_update,
            piece_skip,
            grad_query,
            query_heads,
            grad_heads,
            key_part,
            value_part,
            key_mask,
            log_sum,
            row_delta,
        )
        if index_num == 0:
            own_keys = key_grad
            own_values = value_grad
        else:
            back_keys, back_values = (
                passed_along(key_grad.astype(jnp.bfloat16), "shard", offsets[index_num - 1]).astype(
                    key_grad.dtype
                ),
                passed_along(
                    value_grad.astype(jnp.bfloat16), "shard", offsets[index_num - 1]
                ).astype(value_grad.dtype),
            )
            own_keys = own_keys + back_keys
            own_values = own_values + back_values
    query_out = (merge_heads(grad_query) * 0.125).astype(jnp.bfloat16)
    return (query_out, (own_keys * 0.125).astype(jnp.bfloat16), own_values.astype(jnp.bfloat16))


def layer_forward(hidden, weights, offsets, key_masks):
    (
        qkv_w,
        query_b,
        value_b,
        proj_w,
        proj_b,
        attn_g,
        attn_s,
        up_w,
        up_b,
        down_w,
        down_b,
        ffn_g,
        ffn_s,
    ) = weights
    model_width = qkv_w.shape[0]
    hidden_low = hidden.astype(jnp.bfloat16)
    mixed_all = product(hidden_low, qkv_w)
    query_rows = (mixed_all[..., :model_width] + query_b.astype(jnp.float32)).astype(jnp.bfloat16)
    key_rows = mixed_all[..., model_width : 2 * model_width].astype(jnp.bfloat16)
    value_rows = (mixed_all[..., 2 * model_width :] + value_b.astype(jnp.float32)).astype(
        jnp.bfloat16
    )
    context, log_sum, pieces = attend_forward(query_rows, key_rows, value_rows, offsets, key_masks)
    context_low = context.astype(jnp.bfloat16)
    attn_out = product(context_low, proj_w) + proj_b.astype(jnp.float32)
    settled, normed_one, inverse_one = layer_norm(
        hidden + attn_out, attn_g.astype(jnp.float32), attn_s.astype(jnp.float32)
    )
    settled_low = settled.astype(jnp.bfloat16)
    before = product(settled_low, up_w) + up_b.astype(jnp.float32)
    active = gelu_exact(before).astype(jnp.bfloat16)
    ffn_out = product(active, down_w) + down_b.astype(jnp.float32)
    result, normed_two, inverse_two = layer_norm(
        settled + ffn_out, ffn_g.astype(jnp.float32), ffn_s.astype(jnp.float32)
    )
    saved_state = (
        hidden_low,
        query_rows,
        key_rows,
        value_rows,
        context,
        log_sum,
        pieces,
        context_low,
        normed_one,
        inverse_one,
        settled_low,
        before,
        active,
        normed_two,
        inverse_two,
    )
    return (result, saved_state)


def layer_backward(grad_out, weights, saved_state, offsets, key_masks):
    (
        qkv_w,
        query_b,
        value_b,
        proj_w,
        proj_b,
        attn_g,
        attn_s,
        up_w,
        up_b,
        down_w,
        down_b,
        ffn_g,
        ffn_s,
    ) = weights
    (
        hidden_low,
        query_rows,
        key_rows,
        value_rows,
        context,
        log_sum,
        pieces,
        context_low,
        normed_one,
        inverse_one,
        settled_low,
        before,
        active,
        normed_two,
        inverse_two,
    ) = saved_state
    grad_two, ffngain_part, ffnshift_part = norm_backward(
        grad_out, normed_two, inverse_two, ffn_g.astype(jnp.float32)
    )
    grad_ffn = grad_two.astype(jnp.bfloat16)
    downweight_part = weight_grad(active, grad_ffn)
    downbias_part = token_sum(grad_ffn)
    grad_active = product_back(grad_ffn, down_w)
    gelu_pull = jax.vjp(gelu_exact, before)[1]
    grad_before = gelu_pull(grad_active)[0].astype(jnp.bfloat16)
    upweight_part = weight_grad(settled_low, grad_before)
    upbias_part = token_sum(grad_before)
    grad_settled = grad_two + product_back(grad_before, up_w)
    grad_one, attngain_part, attnshift_part = norm_backward(
        grad_settled, normed_one, inverse_one, attn_g.astype(jnp.float32)
    )
    grad_attn = grad_one.astype(jnp.bfloat16)
    proj_part = weight_grad(context_low, grad_attn)
    projbias_part = token_sum(grad_attn)
    grad_context = product_back(grad_attn, proj_w).astype(jnp.bfloat16)
    pieces = [(key_rows, value_rows)]
    for offset in offsets:
        pieces.append(passed_along((key_rows, value_rows), "shard", -offset))
    grad_query, grad_keys, grad_values = attend_backward(
        query_rows, grad_context, context, log_sum, pieces, key_masks, offsets
    )
    grad_mixed = jnp.concatenate([grad_query, grad_keys, grad_values], axis=-1)
    qkv_part = weight_grad(hidden_low, grad_mixed)
    querybias_part = token_sum(grad_query)
    valuebias_part = token_sum(grad_values)
    grad_hidden = grad_one + product_back(grad_mixed, qkv_w)
    layer_grads = (
        qkv_part,
        querybias_part,
        valuebias_part,
        proj_part,
        projbias_part,
        attngain_part,
        attnshift_part,
        upweight_part,
        upbias_part,
        downweight_part,
        downbias_part,
        ffngain_part,
        ffnshift_part,
    )
    return (grad_hidden, layer_grads)


def on_device(
    inputs,
    cotangent,
    segment_ids,
    memory_slot,
    memory_table,
    qkv_weight,
    query_bias,
    value_bias,
    proj_weight,
    proj_bias,
    attn_gain,
    attn_shift,
    up_weight,
    up_bias,
    down_weight,
    down_bias,
    ffn_gain,
    ffn_shift,
):
    shards = lax.axis_size("shard")
    my_index = lax.axis_index("shard")
    row_count = inputs.shape[1]
    reach_out = min(REACH, shards - 1)
    offsets = [offset for offset in range(-reach_out, reach_out + 1) if offset != 0]
    seg_here = lax.dynamic_slice_in_dim(segment_ids, my_index * row_count, row_count, 1)
    key_masks = [piece_mask(segment_ids, seg_here, my_index, shards, row_count, 0)]
    for offset in offsets:
        key_masks.append(piece_mask(segment_ids, seg_here, my_index, shards, row_count, offset))
    gathered = (
        lax.all_gather(qkv_weight, "shard", axis=1, tiled=True),
        lax.all_gather(query_bias, "shard", axis=1, tiled=True),
        lax.all_gather(value_bias, "shard", axis=1, tiled=True),
        lax.all_gather(proj_weight, "shard", axis=1, tiled=True),
        lax.all_gather(proj_bias, "shard", axis=1, tiled=True),
        lax.all_gather(attn_gain, "shard", axis=1, tiled=True),
        lax.all_gather(attn_shift, "shard", axis=1, tiled=True),
        lax.all_gather(up_weight, "shard", axis=1, tiled=True),
        lax.all_gather(up_bias, "shard", axis=1, tiled=True),
        lax.all_gather(down_weight, "shard", axis=1, tiled=True),
        lax.all_gather(down_bias, "shard", axis=1, tiled=True),
        lax.all_gather(ffn_gain, "shard", axis=1, tiled=True),
        lax.all_gather(ffn_shift, "shard", axis=1, tiled=True),
        lax.all_gather(memory_table, "shard", axis=1, tiled=True),
    )
    slot_range = jnp.arange(MEMS, dtype=jnp.int32)
    slot_hot = (memory_slot[..., None] == slot_range).astype(jnp.float32)
    hidden = inputs.astype(jnp.float32) + jnp.einsum(
        "btm,md->btd", slot_hot, gathered[13].astype(jnp.float32), precision=lax.Precision.HIGHEST
    )
    saved_list = []
    for layer_num in range(LAYERS):
        weights = tuple((item[layer_num] for item in gathered[:13]))
        hidden, saved_state = layer_forward(hidden, weights, offsets, key_masks)
        saved_list.append(saved_state)
    regathered = (
        lax.all_gather(qkv_weight, "shard", axis=1, tiled=True),
        lax.all_gather(query_bias, "shard", axis=1, tiled=True),
        lax.all_gather(value_bias, "shard", axis=1, tiled=True),
        lax.all_gather(proj_weight, "shard", axis=1, tiled=True),
        lax.all_gather(proj_bias, "shard", axis=1, tiled=True),
        lax.all_gather(attn_gain, "shard", axis=1, tiled=True),
        lax.all_gather(attn_shift, "shard", axis=1, tiled=True),
        lax.all_gather(up_weight, "shard", axis=1, tiled=True),
        lax.all_gather(up_bias, "shard", axis=1, tiled=True),
        lax.all_gather(down_weight, "shard", axis=1, tiled=True),
        lax.all_gather(down_bias, "shard", axis=1, tiled=True),
        lax.all_gather(ffn_gain, "shard", axis=1, tiled=True),
        lax.all_gather(ffn_shift, "shard", axis=1, tiled=True),
    )
    grad_hidden = cotangent.astype(jnp.float32)
    grads_by_layer = [None] * LAYERS
    for layer_num in range(LAYERS - 1, -1, -1):
        weights = tuple((item[layer_num] for item in regathered))
        grad_hidden, layer_grads = layer_backward(
            grad_hidden, weights, saved_list[layer_num], offsets, key_masks
        )
        grads_by_layer[layer_num] = layer_grads
    memory_full = jnp.einsum("btm,btd->md", slot_hot, grad_hidden, precision=lax.Precision.HIGHEST)
    stacked = [
        jnp.stack([grads_by_layer[layer_num][member] for layer_num in range(LAYERS)])
        for member in range(13)
    ]
    shares = (
        lax.psum_scatter(stacked[0], "shard", scatter_dimension=1, tiled=True),
        lax.psum_scatter(stacked[1], "shard", scatter_dimension=1, tiled=True),
        lax.psum_scatter(stacked[2], "shard", scatter_dimension=1, tiled=True),
        lax.psum_scatter(stacked[3], "shard", scatter_dimension=1, tiled=True),
        lax.psum_scatter(stacked[4], "shard", scatter_dimension=1, tiled=True),
        lax.psum_scatter(stacked[5], "shard", scatter_dimension=1, tiled=True),
        lax.psum_scatter(stacked[6], "shard", scatter_dimension=1, tiled=True),
        lax.psum_scatter(stacked[7], "shard", scatter_dimension=1, tiled=True),
        lax.psum_scatter(stacked[8], "shard", scatter_dimension=1, tiled=True),
        lax.psum_scatter(stacked[9], "shard", scatter_dimension=1, tiled=True),
        lax.psum_scatter(stacked[10], "shard", scatter_dimension=1, tiled=True),
        lax.psum_scatter(stacked[11], "shard", scatter_dimension=1, tiled=True),
        lax.psum_scatter(stacked[12], "shard", scatter_dimension=1, tiled=True),
        lax.psum_scatter(memory_full, "shard", scatter_dimension=1, tiled=True),
    )
    totals = (
        lax.psum(shares[0].astype(jnp.bfloat16), "rep").astype(jnp.float32),
        lax.psum(shares[1].astype(jnp.bfloat16), "rep").astype(jnp.float32),
        lax.psum(shares[2].astype(jnp.bfloat16), "rep").astype(jnp.float32),
        lax.psum(shares[3].astype(jnp.bfloat16), "rep").astype(jnp.float32),
        lax.psum(shares[4].astype(jnp.bfloat16), "rep").astype(jnp.float32),
        lax.psum(shares[5].astype(jnp.bfloat16), "rep").astype(jnp.float32),
        lax.psum(shares[6].astype(jnp.bfloat16), "rep").astype(jnp.float32),
        lax.psum(shares[7].astype(jnp.bfloat16), "rep").astype(jnp.float32),
        lax.psum(shares[8].astype(jnp.bfloat16), "rep").astype(jnp.float32),
        lax.psum(shares[9].astype(jnp.bfloat16), "rep").astype(jnp.float32),
        lax.psum(shares[10].astype(jnp.bfloat16), "rep").astype(jnp.float32),
        lax.psum(shares[11].astype(jnp.bfloat16), "rep").astype(jnp.float32),
        lax.psum(shares[12].astype(jnp.bfloat16), "rep").astype(jnp.float32),
        lax.psum(shares[13].astype(jnp.bfloat16), "rep").astype(jnp.float32),
    )
    return (
        hidden,
        grad_hidden,
        totals[13],
        totals[0],
        totals[1],
        totals[2],
        totals[3],
        totals[4],
        totals[5],
        totals[6],
        totals[7],
        totals[8],
        totals[9],
        totals[10],
        totals[11],
        totals[12],
    )


BLOCK = 256
GROUP = 4
BF16 = jnp.bfloat16
F32 = jnp.float32


def mm(left, right, left_dim, right_dim):
    return lax.dot_general(
        left, right, (((left_dim,), (right_dim,)), ((), ())), preferred_element_type=F32
    )


def exchange(tensor, axis, mask):
    count = lax.axis_size(axis)
    return lax.ppermute(tensor, axis, [(i, i ^ mask) for i in range(count)])


def ordered(first_is_mine, mine, other):
    return jnp.stack(
        [jnp.where(first_is_mine, mine, other), jnp.where(first_is_mine, other, mine)]
    )


def to_groups(tensor, index):
    low = index < GROUP
    mine = jnp.where(low, tensor[0], tensor[1])
    other = exchange(jnp.where(low, tensor[1], tensor[0]), "shard", GROUP)
    both = ordered(low, mine, other)
    return both.reshape((2 * tensor.shape[1],) + tensor.shape[2:])


def from_groups(tensor, index):
    low = index < GROUP
    half = tensor.shape[0] // 2
    mine = jnp.where(low, tensor[:half], tensor[half:])
    other = exchange(
        jnp.where(low, tensor[half:], tensor[:half]).astype(BF16), "shard", GROUP
    ).astype(tensor.dtype)
    return ordered(low, mine, other)


def swap(tensor):
    shape = tensor.shape
    flat = tensor.reshape((shape[0] * shape[1],) + shape[2:])
    moved = lax.all_to_all(
        flat, "shard", 0, 0, axis_index_groups=[[0, 1, 2, 3], [4, 5, 6, 7]], tiled=True
    )
    return moved.reshape(shape)


def block_cols(block):
    half = block // GROUP
    return pl.ds(pl.multiple_of(half * BLOCK, BLOCK), BLOCK)


def flipped(tensor):
    return jnp.transpose(tensor.astype(F32)).astype(BF16)


def pair_mask(seg_col, seg_row, keys, queries):
    col = seg_col[pl.ds(pl.multiple_of(keys * BLOCK, BLOCK), BLOCK), :]
    col = jnp.concatenate([col] * (BLOCK // 128), axis=1)
    return col == seg_row[queries]


def attend_kernel(
    lo_ref, hi_ref, x_ref, seg_col, seg_row, low_ref, out_ref, lse_ref, keys_nat, acc, top, total,
):
    heads = x_ref.shape[1] // (3 * HEAD_DIM)
    width = heads * HEAD_DIM
    blocks = seg_row.shape[0]

    def flip(block, carry):
        for h in range(heads):
            keys_nat[h, block] = flipped(
                x_ref[block % GROUP, width + h * HEAD_DIM : width + (h + 1) * HEAD_DIM, block_cols(block)]
            )
        return carry

    lax.fori_loop(0, blocks, flip, 0)

    def per_query(i, carry):
        src, cols = (i % GROUP, block_cols(i))
        for h in range(heads):
            top[h] = jnp.full(top.shape[1:], masked_score, F32)
            total[h] = jnp.zeros(total.shape[1:], F32)
            acc[h] = jnp.zeros(acc.shape[1:], F32)

        def per_key(j, inner):
            allowed = pair_mask(seg_col, seg_row, j, i)
            olds = [top[h] for h in range(heads)]
            sums = [total[h] for h in range(heads)]
            mixes = [acc[h] for h in range(heads)]
            scores = [
                mm(keys_nat[h, j], x_ref[src, h * HEAD_DIM : (h + 1) * HEAD_DIM, cols], 1, 0)
                for h in range(heads)
            ]
            scores = [jnp.where(allowed, item, masked_score) for item in scores]
            news = [
                jnp.maximum(old, jnp.max(item, axis=0, keepdims=True)) for old, item in zip(olds, scores)
            ]
            raised = [jnp.exp(item - new) for item, new in zip(scores, news)]
            adds = [
                mm(
                    x_ref[j % GROUP, 2 * width + h * HEAD_DIM : 2 * width + (h + 1) * HEAD_DIM, block_cols(j)],
                    raised[h].astype(BF16), 1, 0,
                )
                for h in range(heads)
            ]
            for h in range(heads):
                fade = jnp.exp(olds[h] - news[h])
                top[h] = news[h]
                total[h] = sums[h] * fade + jnp.sum(raised[h], axis=0, keepdims=True)
                acc[h] = mixes[h] * fade + adds[h]
            return inner

        lax.fori_loop(lo_ref[i], hi_ref[i], per_key, 0)
        for h in range(heads):
            out = acc[h] / total[h]
            out_ref[src, h * HEAD_DIM : (h + 1) * HEAD_DIM, cols] = out
            low_ref[src, h * HEAD_DIM : (h + 1) * HEAD_DIM, cols] = out.astype(BF16)
            lse_ref[h, i] = top[h] + jnp.log(total[h])
        return carry

    lax.fori_loop(0, blocks, per_query, 0)


def attend_back_kernel(
    lo_ref, hi_ref, x_ref, go_ref, out_ref, lse_ref, seg_col, seg_row, dx_ref,
    keys_nat, values_nat, delta, dq, dk, dv,
):
    heads = x_ref.shape[1] // (3 * HEAD_DIM)
    width = heads * HEAD_DIM
    blocks = seg_row.shape[0]

    def prepare(block, carry):
        src, cols = (block % GROUP, block_cols(block))
        for h in range(heads):
            low, high = (h * HEAD_DIM, (h + 1) * HEAD_DIM)
            keys_nat[h, block] = flipped(x_ref[src, width + low : width + high, cols])
            values_nat[h, block] = flipped(x_ref[src, 2 * width + low : 2 * width + high, cols])
            delta[h, block] = jnp.sum(
                go_ref[src, low:high, cols].astype(F32) * out_ref[src, low:high, cols],
                axis=0,
                keepdims=True,
            )
            dq[h, block] = jnp.zeros(dq.shape[2:], F32)
        return carry

    lax.fori_loop(0, blocks, prepare, 0)

    def per_key(j, carry):
        key_src, key_cols = (j % GROUP, block_cols(j))
        for h in range(heads):
            dk[h] = jnp.zeros(dk.shape[1:], F32)
            dv[h] = jnp.zeros(dv.shape[1:], F32)

        def per_query(i, inner):
            src, cols = (i % GROUP, block_cols(i))
            allowed = pair_mask(seg_col, seg_row, j, i)
            spots = [slice(h * HEAD_DIM, (h + 1) * HEAD_DIM) for h in range(heads)]
            old_dv = [dv[h] for h in range(heads)]
            old_dk = [dk[h] for h in range(heads)]
            old_dq = [dq[h, i] for h in range(heads)]
            queries = [x_ref[src, spot, cols] for spot in spots]
            grads = [go_ref[src, spot, cols] for spot in spots]
            scores = [mm(keys_nat[h, j], queries[h], 1, 0) for h in range(heads)]
            grad_probs = [mm(values_nat[h, j], grads[h], 1, 0) for h in range(heads)]
            probs = [
                jnp.exp(jnp.where(allowed, scores[h], masked_score) - lse_ref[h, i]) for h in range(heads)
            ]
            grad_scores = [
                (probs[h] * (grad_probs[h] - delta[h, i])).astype(BF16) for h in range(heads)
            ]
            add_dv = [mm(grads[h], probs[h].astype(BF16), 1, 1) for h in range(heads)]
            add_dk = [mm(queries[h], grad_scores[h], 1, 1) for h in range(heads)]
            add_dq = [
                mm(x_ref[key_src, width + h * HEAD_DIM : width + (h + 1) * HEAD_DIM, key_cols], grad_scores[h], 1, 0)
                for h in range(heads)
            ]
            for h in range(heads):
                dv[h] = old_dv[h] + add_dv[h]
                dk[h] = old_dk[h] + add_dk[h]
                dq[h, i] = old_dq[h] + add_dq[h]
            return inner

        lax.fori_loop(lo_ref[j], hi_ref[j], per_query, 0)
        for h in range(heads):
            low, high = (h * HEAD_DIM, (h + 1) * HEAD_DIM)
            dx_ref[key_src, width + low : width + high, key_cols] = dk[h].astype(BF16)
            dx_ref[key_src, 2 * width + low : 2 * width + high, key_cols] = dv[h].astype(BF16)
        return carry

    lax.fori_loop(0, blocks, per_key, 0)

    def finish(block, carry):
        src, cols = (block % GROUP, block_cols(block))
        for h in range(heads):
            dx_ref[src, h * HEAD_DIM : (h + 1) * HEAD_DIM, cols] = (dq[h, block] * 0.125).astype(BF16)
        return carry

    lax.fori_loop(0, blocks, finish, 0)


def in_vmem(count):
    return [pl.BlockSpec(memory_space=pltpu.VMEM)] * count


def attend(qkv, spans, seg_col, seg_row):
    heads = qkv.shape[1] // (3 * HEAD_DIM)
    blocks = seg_row.shape[0]
    return pl.pallas_call(
        attend_kernel,
        name="attend",
        out_shape=(
            jax.ShapeDtypeStruct((GROUP, heads * HEAD_DIM, qkv.shape[2]), BF16),
            jax.ShapeDtypeStruct((GROUP, heads * HEAD_DIM, qkv.shape[2]), F32),
            jax.ShapeDtypeStruct((heads, blocks, 1, BLOCK), F32),
        ),
        in_specs=[pl.BlockSpec(memory_space=pltpu.SMEM)] * 2 + in_vmem(3),
        out_specs=in_vmem(3),
        scratch_shapes=[
            pltpu.VMEM((heads, blocks, BLOCK, HEAD_DIM), BF16),
            pltpu.VMEM((heads, HEAD_DIM, BLOCK), F32),
            pltpu.VMEM((heads, 1, BLOCK), F32),
            pltpu.VMEM((heads, 1, BLOCK), F32),
        ],
    )(*spans, qkv, seg_col, seg_row)


def attend_back(qkv, grad_out, out, lse, spans, seg_col, seg_row):
    heads = qkv.shape[1] // (3 * HEAD_DIM)
    blocks = seg_row.shape[0]
    return pl.pallas_call(
        attend_back_kernel,
        name="attend_back",
        out_shape=jax.ShapeDtypeStruct(qkv.shape, BF16),
        in_specs=[pl.BlockSpec(memory_space=pltpu.SMEM)] * 2 + in_vmem(6),
        out_specs=in_vmem(1)[0],
        scratch_shapes=[
            pltpu.VMEM((heads, blocks, BLOCK, HEAD_DIM), BF16),
            pltpu.VMEM((heads, blocks, BLOCK, HEAD_DIM), BF16),
            pltpu.VMEM((heads, blocks, 1, BLOCK), F32),
            pltpu.VMEM((heads, blocks, HEAD_DIM, BLOCK), F32),
            pltpu.VMEM((heads, HEAD_DIM, BLOCK), F32),
            pltpu.VMEM((heads, HEAD_DIM, BLOCK), F32),
        ],
    )(*spans, qkv, grad_out, out, lse, seg_col, seg_row)


def norm_rows(tensor, gain, shift):
    center = tensor - jnp.mean(tensor, axis=-1, keepdims=True)
    inverse = lax.rsqrt(jnp.mean(center * center, axis=-1, keepdims=True) + norm_eps)
    normed = center * inverse
    return (normed * gain + shift, normed, inverse)


def norm_rows_back(grad, normed, inverse, gain):
    scaled = grad * gain
    inner = (
        scaled
        - jnp.mean(scaled, axis=-1, keepdims=True)
        - normed * jnp.mean(scaled * normed, axis=-1, keepdims=True)
    )
    return (inner * inverse, jnp.sum(grad * normed, axis=0), jnp.sum(grad, axis=0))


def fast_forward(hidden, weights, vecs, spans, seg_col, seg_row):
    query_b, value_b, proj_b, attn_g, attn_s, down_b, ffn_g, ffn_s, up_b = vecs
    width = hidden.shape[1]
    hidden_low = hidden.astype(BF16)
    qkv_w, later = weights
    mixed = mm(qkv_w, hidden_low, 0, 1)
    query = (mixed[:width] + query_b[:, None]).astype(BF16) * BF16(0.125)
    keys = mixed[width : 2 * width].astype(BF16)
    values = (mixed[2 * width :] + value_b[:, None]).astype(BF16)
    share = width // GROUP
    packed = jnp.concatenate(
        [part.reshape(GROUP, share, part.shape[1]) for part in (query, keys, values)], axis=1
    )
    proj_w, up_w, down_w, qkv = later(packed)
    low, out, lse = attend(qkv, spans, seg_col, seg_row)
    context = swap(low).reshape(width, low.shape[2])
    attn_out = mm(context, proj_w, 0, 0) + proj_b
    settled, normed_one, inverse_one = norm_rows(hidden + attn_out, attn_g, attn_s)
    settled_low = settled.astype(BF16)
    before = mm(settled_low, up_w, 1, 0) + up_b
    below = 0.5 * (1.0 + lax.erf(before * 0.7071067811865476))
    active = (before * below).astype(BF16)
    slope = (below + before * jnp.exp(-0.5 * before * before) * 0.3989422804014327).astype(BF16)
    ffn_out = mm(active, down_w, 1, 0) + down_b
    result, normed_two, inverse_two = norm_rows(settled + ffn_out, ffn_g, ffn_s)
    return result, (qkv_w, proj_w, up_w, down_w), (
        hidden_low, qkv, out, lse, context, normed_one, inverse_one, settled_low,
        active, slope, normed_two, inverse_two,
    )


def fast_backward(grad, weights, vecs, saved, spans, seg_col, seg_row, give_back):
    query_b, value_b, proj_b, attn_g, attn_s, down_b, ffn_g, ffn_s, up_b = vecs
    qkv_w, proj_w, up_w, down_w = weights
    (
        hidden_low, qkv, out, lse, context, normed_one, inverse_one, settled_low,
        active, slope, normed_two, inverse_two,
    ) = saved
    width = grad.shape[1]
    grad_two, ffn_g_sum, ffn_s_sum = norm_rows_back(grad, normed_two, inverse_two, ffn_g)
    grad_ffn = grad_two.astype(BF16)
    down_b_sum = jnp.sum(grad_ffn.astype(F32), axis=0)
    grad_before = (mm(grad_ffn, down_w, 1, 1) * slope.astype(F32)).astype(BF16)
    down_grad = mm(active, grad_ffn, 0, 0).astype(BF16)
    up_grad = mm(settled_low, grad_before, 0, 0).astype(BF16)
    up_b_sum = jnp.sum(grad_before.astype(F32), axis=0)
    grad_settled = grad_two + mm(grad_before, up_w, 1, 1)
    grad_one, attn_g_sum, attn_s_sum = norm_rows_back(grad_settled, normed_one, inverse_one, attn_g)
    grad_attn = grad_one.astype(BF16)
    proj_b_sum = jnp.sum(grad_attn.astype(F32), axis=0)
    grad_context = mm(proj_w, grad_attn, 1, 1).astype(BF16)
    proj_grad = mm(context, grad_attn, 1, 0).astype(BF16)
    grad_out = swap(grad_context.reshape(GROUP, width // GROUP, grad_context.shape[1]))
    moved = give_back(attend_back(qkv, grad_out, out, lse, spans, seg_col, seg_row))
    share = width // GROUP
    mixed = jnp.transpose(moved.reshape(GROUP, 3, share, moved.shape[2]), (1, 0, 2, 3))
    mixed = mixed.reshape(3 * width, moved.shape[2])
    qkv_grad = mm(hidden_low, mixed, 0, 1).astype(BF16)
    grad_hidden = grad_one + mm(mixed, qkv_w, 0, 1)
    mixed_sum = jnp.sum(mixed.astype(F32), axis=1)
    sums = [
        mixed_sum[:width], mixed_sum[2 * width :], proj_b_sum, attn_g_sum, attn_s_sum, down_b_sum,
        ffn_g_sum, ffn_s_sum,
    ]
    sums += [up_b_sum[part * width : (part + 1) * width] for part in range(up_w.shape[1] // width)]
    return grad_hidden, (qkv_grad, proj_grad, up_grad, down_grad), sums


MESH = pl.DeviceIdType.MESH


def places():
    rep, shard = (lax.axis_index("rep"), lax.axis_index("shard"))
    core, y, z = (lax.rem(rep, 2), lax.rem(shard, 2), lax.div(shard, 2))
    across_x = lax.rem(rep + 2, 4)
    across_core = rep + 1 - 2 * core
    zs = (z, z + 1 - 2 * lax.rem(z, 2), lax.rem(z + 2, 4), 3 - z)
    return (rep, shard, core, y, across_x, across_core, zs)


def greet(diagonal=False):
    rep, shard, core, y, across_x, across_core, zs = places()
    barrier = pltpu.get_barrier_semaphore()
    partners = [(rep, 2 * other + y) for other in zs[1:]]
    partners += [(rep, 2 * zs[0] + 1 - y), (across_x, shard), (across_core, shard)]
    if diagonal:
        partners += [(rep, 2 * other + 1 - y) for other in zs[1:]]
    for partner in partners:
        pl.semaphore_signal(barrier, inc=1, device_id=partner, device_id_type=MESH)
    pl.semaphore_wait(barrier, len(partners))


class Sends:
    def __init__(self, sems):
        self.sems = sems
        self.copies = []

    def push(self, source, target, arrived, device):
        copy = pltpu.make_async_remote_copy(
            source, target, self.sems.at[len(self.copies)], arrived, device_id=device, device_id_type=MESH
        )
        copy.start()
        self.copies.append(copy)

    def finish(self):
        for copy in self.copies:
            copy.wait_send()


def gather_kernel(fourths, smalls, swaps, *refs):
    count = fourths + smalls
    total = count + swaps
    owns, fulls = (refs[:total], refs[total : 2 * total])
    local_sems, send_sems, fourth_sems, small_sems, swap_sems = refs[2 * total :]
    rep, shard, core, y, across_x, across_core, zs = places()
    member = lax.rem(shard, GROUP)
    greet(smalls + swaps > 0)
    sends = Sends(send_sems)
    beside, past_x, past_core = ((rep, 2 * zs[0] + 1 - y), (across_x, shard), (across_core, shard))

    def send(n, chunk, part, device, own=False):
        target = fulls[n].at[chunk, part]
        source = owns[n].at[part] if own else target
        sends.push(source, target, fourth_sems.at[n, chunk, part], device)

    def arrive(n, chunk, part):
        piece = fulls[n].at[chunk, part]
        pltpu.make_async_copy(piece, piece, fourth_sems.at[n, chunk, part]).wait()

    near_members = ((1, y), (0, 1 - y), (1, 1 - y))
    for n in range(smalls):
        for k in range(4):
            for other in (y, 1 - y) if k else (1 - y,):
                sends.push(
                    owns[fourths + n],
                    fulls[fourths + n].at[shard],
                    small_sems.at[shard],
                    (rep, 2 * zs[k] + other),
                )
    for n in range(fourths):
        send(n, shard, rep, beside, True)
        for k in (1, 2, 3):
            send(n, shard, rep, (rep, 2 * zs[k] + y), True)
    for n in range(swaps):
        for k, other in near_members:
            target = 2 * zs[k] + other
            sends.push(
                owns[count + n].at[lax.rem(target, GROUP)],
                fulls[count + n].at[member],
                swap_sems.at[n, member],
                (rep, target),
            )
    local = [
        pltpu.make_async_copy(owns[n], fulls[n].at[shard], local_sems.at[n]) for n in range(count)
    ]
    local += [
        pltpu.make_async_copy(owns[n].at[member], fulls[n].at[member], local_sems.at[n])
        for n in range(count, total)
    ]
    for copy in local:
        copy.start()

    events = ((0, 1), (1, 0), (2, 0), (1, 1), (3, 0), (2, 1), (3, 1))
    chunks = [2 * zs[k] + (1 - y if far else y) for k, far in events]

    def from_x(chunk):
        for n in range(fourths):
            arrive(n, chunk, across_x)
            send(n, chunk, across_x, past_core)

    for at, (chunk, (k, far)) in enumerate(zip(chunks, events)):
        for n in range(fourths):
            arrive(n, chunk, rep)
            if not far:
                send(n, chunk, rep, beside)
            send(n, chunk, rep, past_x)
            send(n, chunk, rep, past_core)
        if at >= 3:
            from_x(chunks[at - 3])
    for chunk in chunks[-3:]:
        from_x(chunk)
    for chunk in chunks:
        for n in range(fourths):
            arrive(n, chunk, across_core)
            arrive(n, chunk, lax.rem(across_core + 2, 4))
        for n in range(smalls):
            piece = fulls[fourths + n].at[chunk]
            pltpu.make_async_copy(piece, piece, small_sems.at[chunk]).wait()
    for n in range(swaps):
        for k, other in near_members:
            source = lax.rem(2 * zs[k] + other, GROUP)
            piece = fulls[count + n].at[source]
            pltpu.make_async_copy(piece, piece, swap_sems.at[n, source]).wait()
    for copy in local:
        copy.wait()
    sends.finish()


def gather_fast(fourths, smalls, swaps, name, collective_id):
    split = [item.reshape(4, item.shape[0] // 4, item.shape[1]) for item in fourths] + smalls
    owns = split + swaps
    dma = pltpu.SemaphoreType.DMA
    fulls = pl.pallas_call(
        functools.partial(gather_kernel, len(fourths), len(smalls), len(swaps)),
        name=name,
        out_shape=[jax.ShapeDtypeStruct((8,) + item.shape, BF16) for item in split]
        + [jax.ShapeDtypeStruct(item.shape, BF16) for item in swaps],
        in_specs=in_vmem(len(owns)),
        out_specs=[pl.BlockSpec(memory_space=pl.ANY)] * len(owns),
        scratch_shapes=[
            dma((len(owns),)),
            dma((28 * len(fourths) + 7 * len(smalls) + 3 * len(swaps),)),
            dma((len(fourths), 8, 4)),
            dma((8,)),
            dma((max(1, len(swaps)), GROUP)),
        ],
        compiler_params=pltpu.CompilerParams(collective_id=collective_id, has_side_effects=True),
    )(*owns)
    wide = len(fourths)
    return [item.reshape(-1, item.shape[3]) for item in fulls[:wide]] + list(fulls[wide:])


def reduce_kernel(x_first, smalls, swaps, *refs):
    kinds = len(x_first)
    total = kinds + smalls + swaps
    grads, extra = (refs[:kinds], refs[kinds:total])
    outs, extra_out = (refs[total : total + kinds], refs[total + kinds : 2 * total])
    scratch = refs[2 * total :]
    mats, cores, ones, twos, threes, stage_one, stage_two, stage_three, alls = [
        scratch[kinds * n : kinds * n + kinds] for n in range(9)
    ]
    (
        small_sum, small_got, local_sems, send_sems, core_sems, one_sems, two_sems, three_sems, all_sems,
        small_sems, swap_sems,
    ) = scratch[9 * kinds :]
    rep, shard, core, y, across_x, across_core, zs = places()
    x = lax.div(rep, 2)
    member = lax.rem(shard, GROUP)
    beside, past_x, past_core = ((rep, 2 * zs[0] + 1 - y), (across_x, shard), (across_core, shard))
    local = [pltpu.make_async_copy(grads[n], mats[n], local_sems.at[n]) for n in range(kinds)]
    for copy in local:
        copy.start()
    greet(swaps > 0)
    sends = Sends(send_sems)

    def arrive(ref, sem):
        pltpu.make_async_copy(ref, ref, sem).wait()

    def mat(n, k, fy, fx, side=0):
        chunk = 2 * zs[k] + (1 - y if fy else y)
        return mats[n].at[chunk, 2 * (1 - x if fx else x) + (1 - core if side else core)]

    def add(target, parts):
        steps = 6
        lanes = target.shape[1] // steps

        def body(step, carry):
            at = pl.ds(pl.multiple_of(step * lanes, lanes), lanes)
            total = parts[0][:, at].astype(F32)
            for part in parts[1:]:
                total = total + part[:, at].astype(F32)
            target[:, at] = total.astype(BF16)
            return carry

        lax.fori_loop(0, steps, body, 0)

    small_partners = (past_core, past_x, beside, (rep, 2 * zs[1] + y), (rep, 2 * zs[2] + y))

    def small_send(step):
        sends.push(small_sum.at[step], small_got.at[step], small_sems.at[step], small_partners[step])

    def small_step(step):
        if not smalls:
            return
        arrive(small_got.at[step], small_sems.at[step])
        small_sum[step + 1] = small_sum[step] + small_got[step]
        if step + 1 < len(small_partners):
            small_send(step + 1)
        else:
            extra_out[0][...] = small_sum[step + 1]

    if smalls:
        small_sum[0] = extra[0][...]
        small_send(0)
    order = (2, 3, 1, 0)
    for copy in local:
        copy.wait()
    for fy in (1, 0):
        for k in order:
            for n in range(kinds):
                for fx in (1, 0):
                    sends.push(
                        mat(n, k, fy, fx, 1), cores[n].at[k, fy, fx], core_sems.at[n, k, fy, fx], past_core
                    )

    def cored(n, k, fy, fx):
        arrive(cores[n].at[k, fy, fx], core_sems.at[n, k, fy, fx])
        return [mat(n, k, fy, fx), cores[n].at[k, fy, fx]]

    def oned(n, k, fy, fx):
        flag = fy if x_first[n] else fx
        arrive(ones[n].at[k, flag], one_sems.at[n, k, flag])
        return cored(n, k, fy, fx) + [ones[n].at[k, flag]]

    def step_one(slot, k, flag):
        for n in range(kinds):
            stage = stage_one[n].at[slot]
            add(stage, cored(n, k, flag, 1) if x_first[n] else cored(n, k, 1, flag))
            sends.push(
                stage, ones[n].at[k, flag], one_sems.at[n, k, flag], past_x if x_first[n] else beside
            )

    def step_two(k):
        for n in range(kinds):
            stage = stage_two[n].at[k]
            add(stage, oned(n, k, 1, 0) if x_first[n] else oned(n, k, 0, 1))
            sends.push(stage, twos[n].at[k], two_sems.at[n, k], beside if x_first[n] else past_x)

    def twod(n, k):
        parts = oned(n, k, 0, 0)
        arrive(twos[n].at[k], two_sems.at[n, k])
        return parts + [twos[n].at[k]]

    def step_three(k):
        for n in range(kinds):
            stage = stage_three[n].at[k - 1]
            add(stage, twod(n, k))
            sends.push(stage, threes[n].at[k - 1], three_sems.at[n, k - 1], (rep, 2 * zs[k] + y))

    step_one(0, 2, 1)
    near_members = ((1, y), (0, 1 - y), (1, 1 - y))
    for n in range(swaps):
        for k, other in near_members:
            target = 2 * zs[k] + other
            sends.push(
                extra[smalls + n].at[lax.rem(target, GROUP)],
                extra_out[smalls + n].at[member],
                swap_sems.at[n, member],
                (rep, target),
            )
    own_swaps = [
        pltpu.make_async_copy(
            extra[smalls + n].at[member], extra_out[smalls + n].at[member], local_sems.at[kinds + n]
        )
        for n in range(swaps)
    ]
    for copy in own_swaps:
        copy.start()
    step_one(1, 3, 1)
    step_one(2, 1, 1)
    small_step(0)
    step_two(2)
    step_one(3, 0, 1)
    step_two(3)
    step_one(4, 2, 0)
    small_step(1)
    step_two(1)
    step_one(5, 3, 0)
    step_two(0)
    step_one(6, 1, 0)
    small_step(2)
    step_three(2)
    step_one(7, 0, 0)
    step_three(3)
    small_step(3)
    step_three(1)
    small_step(4)

    for n in range(kinds):
        parts = twod(n, 0)
        for k in range(3):
            arrive(threes[n].at[k], three_sems.at[n, k])
        mine = alls[n].at[rep]
        add(mine, parts + [threes[n].at[k] for k in range(3)])
        sends.push(mine, mine, all_sems.at[n, rep], past_x)
        sends.push(mine, mine, all_sems.at[n, rep], past_core)
    for n in range(kinds):
        theirs = alls[n].at[across_x]
        arrive(theirs, all_sems.at[n, across_x])
        sends.push(theirs, theirs, all_sems.at[n, across_x], past_core)
    opposite = lax.rem(across_core + 2, 4)
    for n in range(kinds):
        arrive(alls[n].at[across_core], all_sems.at[n, across_core])
        arrive(alls[n].at[opposite], all_sems.at[n, opposite])
        rows = mats[n].shape[2]
        for q in range(4):
            outs[n][q * rows : (q + 1) * rows, :] = alls[n][q].astype(F32)
    for n in range(swaps):
        for k, other in near_members:
            source = lax.rem(2 * zs[k] + other, GROUP)
            arrive(extra_out[smalls + n].at[source], swap_sems.at[n, source])
    for copy in own_swaps:
        copy.wait()
    sends.finish()


def reduce_fast(grads, x_first, small, swapped, name, collective_id):
    kinds = len(grads)
    extra = small + swapped
    sizes = [(item.shape[0] // 32, item.shape[1]) for item in grads]
    buffers = []
    for lead in ((8, 4), (4, 2, 2), (4, 2), (4,), (3,), (8,), (4,), (3,), (4,)):
        buffers += [pltpu.VMEM(lead + size, BF16) for size in sizes]
    small_shape = small[0].shape if small else (8, 128)
    dma = pltpu.SemaphoreType.DMA
    anywhere = pl.BlockSpec(memory_space=pl.ANY)
    return pl.pallas_call(
        functools.partial(reduce_kernel, x_first, len(small), len(swapped)),
        name=name,
        out_shape=[jax.ShapeDtypeStruct((4 * size[0], size[1]), F32) for size in sizes]
        + [jax.ShapeDtypeStruct(item.shape, item.dtype) for item in extra],
        in_specs=[anywhere] * kinds + in_vmem(len(extra)),
        out_specs=in_vmem(kinds + len(small)) + [anywhere] * len(swapped),
        scratch_shapes=buffers
        + [
            pltpu.VMEM((6,) + small_shape, F32), pltpu.VMEM((5,) + small_shape, F32),
            dma((kinds + 1,)), dma((34 * kinds + 8,)), dma((kinds, 4, 2, 2)), dma((kinds, 4, 2)),
            dma((kinds, 4)), dma((kinds, 3)), dma((kinds, 4)), dma((5,)), dma((1, GROUP)),
        ],
        compiler_params=pltpu.CompilerParams(
            collective_id=collective_id, has_side_effects=True, vmem_limit_bytes=58 * 1024 * 1024
        ),
    )(*[item.reshape((8, 4) + size) for item, size in zip(grads, sizes)], *extra)


def on_device_fast(
    inputs, cotangent, segment_ids, memory_slot, memory_table,
    qkv_weight, query_bias, value_bias, proj_weight, proj_bias, attn_gain, attn_shift,
    up_weight, up_bias, down_weight, down_bias, ffn_gain, ffn_shift,
):
    index = lax.axis_index("shard")
    width = inputs.shape[2]
    share = memory_table.shape[1]
    ups = up_weight.shape[2] // width

    vec_args = (
        query_bias, value_bias, proj_bias, attn_gain, attn_shift, down_bias, ffn_gain, ffn_shift,
    )
    plain = len(vec_args)
    rows = [item[layer][None] for layer in range(LAYERS) for item in vec_args]
    rows += [up_bias[layer].reshape(ups, share) for layer in range(LAYERS)]
    rows.append(memory_table)
    small = jnp.concatenate(rows, axis=0)
    used = small.shape[0]
    small = jnp.pad(small, ((0, -used % 16), (0, 128 - share)))
    first_qkv, small = gather_fast([qkv_weight[0]], [small], [], "gather_first", 0)
    small = small[:, :used, :share].astype(F32)
    wide = jnp.transpose(small, (1, 0, 2)).reshape(used, width)
    vecs = []
    for layer in range(LAYERS):
        start = LAYERS * plain + layer * ups
        vecs.append(
            [wide[layer * plain + item] for item in range(plain)]
            + [small[:, start : start + ups].reshape(ups * width)]
        )
    table = wide[LAYERS * (plain + ups) :].astype(BF16)

    second_qkv = []

    def rest_first(packed):
        proj_w, up_w, qkv_w, down_w, qkv = gather_fast(
            [proj_weight[0], up_weight[0], qkv_weight[1], down_weight[0]], [], [packed],
            "gather_middle", 2,
        )
        second_qkv.append(qkv_w)
        return proj_w, up_w, down_w, qkv

    def rest_second(packed):
        return gather_fast(
            [proj_weight[1], up_weight[1], down_weight[1]], [], [packed], "gather_last", 3
        )

    rests = (rest_first, rest_second)

    segs = jnp.where(index < GROUP, segment_ids[0], segment_ids[1])
    tiles = segs.reshape(-1, BLOCK)
    first, last = (tiles[:, 0], tiles[:, -1])
    spans = (
        jnp.sum((last[None, :] < first[:, None]).astype(jnp.int32), axis=1),
        jnp.sum((first[None, :] <= last[:, None]).astype(jnp.int32), axis=1),
    )
    seg_row = tiles[:, None, :]
    seg_col = jnp.broadcast_to(segs[:, None], (segs.shape[0], 128))

    slots = to_groups(memory_slot[..., None], index)[:, 0]
    slot_hot = slots[:, None] == jnp.arange(MEMS, dtype=jnp.int32)
    hidden = to_groups(inputs, index).astype(F32) + mm(slot_hot.astype(BF16), table, 1, 0)
    saved, held = ([], [])
    for layer in range(LAYERS):
        qkv_w = second_qkv[0] if layer else first_qkv
        hidden, mats, state = fast_forward(
            hidden, (qkv_w, rests[layer]), vecs[layer], spans, seg_col, seg_row
        )
        saved.append(state)
        held.append(mats)
    layer_output = from_groups(hidden, index)

    grad = to_groups(cotangent, index).astype(F32)
    sums, shares = ([None] * LAYERS, [None] * LAYERS)
    found = []

    def sum_second(grad_qkv):
        parts = reduce_fast(found[0], (1, 1, 1, 1), [], [grad_qkv], "reduce_second", 4)
        shares[1] = parts[:4]
        return parts[4]

    for layer in range(LAYERS - 1, -1, -1):
        grad, mat_grads, sums[layer] = fast_backward(
            grad, held[layer], vecs[layer], saved[layer], spans, seg_col, seg_row,
            swap if layer else sum_second,
        )
        found.append(mat_grads)
    input_grad = from_groups(grad, index)
    memory_sum = lax.dot_general(
        slot_hot.astype(F32), grad, (((0,), (0,)), ((), ())), precision=lax.Precision.HIGHEST
    )
    flat = jnp.concatenate([jnp.stack(sums[layer]) for layer in range(LAYERS)] + [memory_sum], axis=0)
    used = flat.shape[0]
    flat = jnp.pad(flat, ((0, -used % 8), (0, 0)))
    *first_shares, flat = reduce_fast(found[1], (0, 1, 1, 0), [flat], [], "reduce_first", 1)
    shares[0] = first_shares
    flat = flat[:used]
    per = plain + ups
    own = lax.dynamic_slice_in_dim(flat, index * share, share, 1)
    vec_grads = [
        jnp.stack([own[layer * per + item] for layer in range(LAYERS)]) for item in range(plain)
    ]
    up_sums = jnp.stack([flat[layer * per + plain : (layer + 1) * per].reshape(-1) for layer in range(LAYERS)])
    upbias_grad = lax.dynamic_slice_in_dim(up_sums, index * share * ups, share * ups, 1)
    memory_grad = own[LAYERS * per :]

    def wide_grad(member):
        return jnp.stack([shares[layer][member] for layer in range(LAYERS)])

    return (
        layer_output,
        input_grad,
        memory_grad,
        wide_grad(0),
        vec_grads[0],
        vec_grads[1],
        wide_grad(1),
        vec_grads[2],
        vec_grads[3],
        vec_grads[4],
        wide_grad(2),
        upbias_grad,
        wide_grad(3),
        vec_grads[5],
        vec_grads[6],
        vec_grads[7],
    )


def fast_fits(mesh):
    return mesh.shape["shard"] == 2 * GROUP and mesh.shape["rep"] == 4


def solution(mesh):
    return jax.shard_map(
        on_device_fast if fast_fits(mesh) else on_device,
        mesh=mesh,
        in_specs=(
            P(None, ("rep", "shard"), None),
            P(None, ("rep", "shard"), None),
            P(None, "rep"),
            P(None, ("rep", "shard")),
            P(None, "shard"),
            P(None, "shard", None),
            P(None, "shard"),
            P(None, "shard"),
            P(None, "shard", None),
            P(None, "shard"),
            P(None, "shard"),
            P(None, "shard"),
            P(None, "shard", None),
            P(None, "shard"),
            P(None, "shard", None),
            P(None, "shard"),
            P(None, "shard"),
            P(None, "shard"),
        ),
        out_specs=(
            P(None, ("rep", "shard"), None),
            P(None, ("rep", "shard"), None),
            P(None, "shard"),
            P(None, "shard", None),
            P(None, "shard"),
            P(None, "shard"),
            P(None, "shard", None),
            P(None, "shard"),
            P(None, "shard"),
            P(None, "shard"),
            P(None, "shard", None),
            P(None, "shard"),
            P(None, "shard", None),
            P(None, "shard"),
            P(None, "shard"),
            P(None, "shard"),
        ),
        check_vma=False,
    )
```

```python
import functools

import jax
import jax.numpy as jnp
from jax import lax
from jax.experimental import pallas as pl
from jax.experimental.pallas import tpu as pltpu
from jax.sharding import PartitionSpec as P

HEADS = 12
HEAD_DIM = 64
LAYERS = 2
MEMS = 20
REACH = 4


norm_eps = 1e-12
masked_score = -1e30


def passed_along(block, axis, distance):
    devices = range(lax.axis_size(axis))
    route = [(i - distance, i) for i in devices if i - distance in devices]
    return lax.ppermute(block, axis, route)


def layer_norm(tensor, norm_gain, norm_shift):
    center = tensor - jnp.mean(tensor, axis=-1, keepdims=True)
    inverse = lax.rsqrt(jnp.mean(center * center, axis=-1, keepdims=True) + norm_eps)
    normed = center * inverse
    return (normed * norm_gain + norm_shift, normed, inverse)


def norm_backward(grad_out, normed, inverse, norm_gain):
    scaled = grad_out * norm_gain
    inner_term = (
        scaled
        - jnp.mean(scaled, axis=-1, keepdims=True)
        - normed * jnp.mean(scaled * normed, axis=-1, keepdims=True)
    )
    return (
        inner_term * inverse,
        jnp.sum(grad_out * normed, axis=(0, 1)),
        jnp.sum(grad_out, axis=(0, 1)),
    )


def gelu_exact(tensor):
    return jax.nn.gelu(tensor, approximate=False)


def split_heads(tensor):
    return tensor.reshape(tensor.shape[0], tensor.shape[1], HEADS, HEAD_DIM)


def merge_heads(tensor):
    return tensor.reshape(tensor.shape[0], tensor.shape[1], HEADS * HEAD_DIM)


def product(left_side, right_side):
    return jnp.einsum("btd,de->bte", left_side, right_side, preferred_element_type=jnp.float32)


def product_back(left_side, right_side):
    return jnp.einsum("bte,de->btd", left_side, right_side, preferred_element_type=jnp.float32)


def weight_grad(left_side, right_side):
    return jnp.einsum("btd,bte->de", left_side, right_side, preferred_element_type=jnp.float32)


def token_sum(tensor):
    return jnp.sum(tensor.astype(jnp.float32), axis=(0, 1))


def piece_mask(segment_ids, seg_here, my_index, shards, row_count, offset):
    target = my_index + offset
    inside = jnp.logical_and(target >= 0, target < shards)
    start_row = jnp.clip(target, 0, shards - 1) * row_count
    seg_there = lax.dynamic_slice_in_dim(segment_ids, start_row, row_count, 1)
    key_mask = jnp.logical_and(seg_here[:, None, :, None] == seg_there[:, None, None, :], inside)
    return (key_mask, jnp.any(key_mask))


def scaled_scores(query_heads, key_part, key_mask):
    scores = (
        jnp.einsum(
            "bqhe,bkhe->bhqk",
            query_heads,
            split_heads(key_part),
            preferred_element_type=jnp.float32,
        )
        * 0.125
    )
    return jnp.where(key_mask, scores, masked_score)


def stats_update(carry_in, query_heads, key_part, key_mask):
    old_max, old_sum = carry_in
    scores = scaled_scores(query_heads, key_part, key_mask)
    new_max = jnp.maximum(old_max, jnp.max(scores, axis=-1))
    fresh = jnp.sum(jnp.where(key_mask, jnp.exp(scores - new_max[..., None]), 0.0), axis=-1)
    return (new_max, old_sum * jnp.exp(old_max - new_max) + fresh)


def stats_keep(carry_in, query_heads, key_part, key_mask):
    return carry_in


def mix_update(context, query_heads, key_part, value_part, key_mask, log_sum):
    scores = scaled_scores(query_heads, key_part, key_mask)
    soft_probs = jnp.where(key_mask, jnp.exp(scores - log_sum[..., None]), 0.0).astype(jnp.bfloat16)
    return context + jnp.einsum(
        "bhqk,bkhe->bqhe", soft_probs, split_heads(value_part), preferred_element_type=jnp.float32
    )


def mix_keep(context, query_heads, key_part, value_part, key_mask, log_sum):
    return context


def piece_update(
    grad_query, query_heads, grad_heads, key_part, value_part, key_mask, log_sum, row_delta
):
    scores = scaled_scores(query_heads, key_part, key_mask)
    soft_probs = jnp.where(key_mask, jnp.exp(scores - log_sum[..., None]), 0.0)
    grad_probs = jnp.einsum(
        "bqhe,bkhe->bhqk", grad_heads, split_heads(value_part), preferred_element_type=jnp.float32
    )
    grad_scores = (soft_probs * (grad_probs - row_delta[..., None])).astype(jnp.bfloat16)
    grad_query = grad_query + jnp.einsum(
        "bhqk,bkhe->bqhe", grad_scores, split_heads(key_part), preferred_element_type=jnp.float32
    )
    key_grad = jnp.einsum(
        "bhqk,bqhe->bkhe", grad_scores, query_heads, preferred_element_type=jnp.float32
    )
    value_grad = jnp.einsum(
        "bhqk,bqhe->bkhe",
        soft_probs.astype(jnp.bfloat16),
        grad_heads,
        preferred_element_type=jnp.float32,
    )
    return (grad_query, merge_heads(key_grad), merge_heads(value_grad))


def piece_skip(
    grad_query, query_heads, grad_heads, key_part, value_part, key_mask, log_sum, row_delta
):
    empty = jnp.zeros(key_part.shape, jnp.float32)
    return (grad_query, empty, empty)


def attend_forward(query_rows, key_rows, value_rows, offsets, key_masks):
    micro_count, row_count = (query_rows.shape[0], query_rows.shape[1])
    query_heads = split_heads(query_rows)
    pieces = [(key_rows, value_rows)]
    for offset in offsets:
        pieces.append(passed_along((key_rows, value_rows), "shard", -offset))
    row_max = jnp.full((micro_count, HEADS, row_count), masked_score, jnp.float32)
    row_sum = jnp.zeros((micro_count, HEADS, row_count), jnp.float32)
    for (key_part, value_part), (key_mask, is_live) in zip(pieces, key_masks):
        row_max, row_sum = lax.cond(
            is_live, stats_update, stats_keep, (row_max, row_sum), query_heads, key_part, key_mask
        )
    log_sum = row_max + jnp.log(row_sum)
    context = jnp.zeros((micro_count, row_count, HEADS, HEAD_DIM), jnp.float32)
    for (key_part, value_part), (key_mask, is_live) in zip(pieces, key_masks):
        context = lax.cond(
            is_live,
            mix_update,
            mix_keep,
            context,
            query_heads,
            key_part,
            value_part,
            key_mask,
            log_sum,
        )
    return (merge_heads(context), log_sum, pieces)


def attend_backward(query_rows, grad_context, context, log_sum, pieces, key_masks, offsets):
    query_heads = split_heads(query_rows)
    grad_heads = split_heads(grad_context)
    row_delta = jnp.transpose(
        jnp.sum(split_heads(grad_context.astype(jnp.float32) * context), axis=-1), (0, 2, 1)
    )
    grad_query = jnp.zeros(query_heads.shape, jnp.float32)
    own_keys = jnp.zeros(query_rows.shape, jnp.float32)
    own_values = jnp.zeros(query_rows.shape, jnp.float32)
    for index_num in range(len(pieces)):
        key_part, value_part = pieces[index_num]
        key_mask, is_live = key_masks[index_num]
        grad_query, key_grad, value_grad = lax.cond(
            is_live,
            piece_update,
            piece_skip,
            grad_query,
            query_heads,
            grad_heads,
            key_part,
            value_part,
            key_mask,
            log_sum,
            row_delta,
        )
        if index_num == 0:
            own_keys = key_grad
            own_values = value_grad
        else:
            back_keys, back_values = (
                passed_along(key_grad.astype(jnp.bfloat16), "shard", offsets[index_num - 1]).astype(
                    key_grad.dtype
                ),
                passed_along(
                    value_grad.astype(jnp.bfloat16), "shard", offsets[index_num - 1]
                ).astype(value_grad.dtype),
            )
            own_keys = own_keys + back_keys
            own_values = own_values + back_values
    query_out = (merge_heads(grad_query) * 0.125).astype(jnp.bfloat16)
    return (query_out, (own_keys * 0.125).astype(jnp.bfloat16), own_values.astype(jnp.bfloat16))


def layer_forward(hidden, weights, offsets, key_masks):
    (
        qkv_w,
        query_b,
        value_b,
        proj_w,
        proj_b,
        attn_g,
        attn_s,
        up_w,
        up_b,
        down_w,
        down_b,
        ffn_g,
        ffn_s,
    ) = weights
    model_width = qkv_w.shape[0]
    hidden_low = hidden.astype(jnp.bfloat16)
    mixed_all = product(hidden_low, qkv_w)
    query_rows = (mixed_all[..., :model_width] + query_b.astype(jnp.float32)).astype(jnp.bfloat16)
    key_rows = mixed_all[..., model_width : 2 * model_width].astype(jnp.bfloat16)
    value_rows = (mixed_all[..., 2 * model_width :] + value_b.astype(jnp.float32)).astype(
        jnp.bfloat16
    )
    context, log_sum, pieces = attend_forward(query_rows, key_rows, value_rows, offsets, key_masks)
    context_low = context.astype(jnp.bfloat16)
    attn_out = product(context_low, proj_w) + proj_b.astype(jnp.float32)
    settled, normed_one, inverse_one = layer_norm(
        hidden + attn_out, attn_g.astype(jnp.float32), attn_s.astype(jnp.float32)
    )
    settled_low = settled.astype(jnp.bfloat16)
    before = product(settled_low, up_w) + up_b.astype(jnp.float32)
    active = gelu_exact(before).astype(jnp.bfloat16)
    ffn_out = product(active, down_w) + down_b.astype(jnp.float32)
    result, normed_two, inverse_two = layer_norm(
        settled + ffn_out, ffn_g.astype(jnp.float32), ffn_s.astype(jnp.float32)
    )
    saved_state = (
        hidden_low,
        query_rows,
        key_rows,
        value_rows,
        context,
        log_sum,
        pieces,
        context_low,
        normed_one,
        inverse_one,
        settled_low,
        before,
        active,
        normed_two,
        inverse_two,
    )
    return (result, saved_state)


def layer_backward(grad_out, weights, saved_state, offsets, key_masks):
    (
        qkv_w,
        query_b,
        value_b,
        proj_w,
        proj_b,
        attn_g,
        attn_s,
        up_w,
        up_b,
        down_w,
        down_b,
        ffn_g,
        ffn_s,
    ) = weights
    (
        hidden_low,
        query_rows,
        key_rows,
        value_rows,
        context,
        log_sum,
        pieces,
        context_low,
        normed_one,
        inverse_one,
        settled_low,
        before,
        active,
        normed_two,
        inverse_two,
    ) = saved_state
    grad_two, ffngain_part, ffnshift_part = norm_backward(
        grad_out, normed_two, inverse_two, ffn_g.astype(jnp.float32)
    )
    grad_ffn = grad_two.astype(jnp.bfloat16)
    downweight_part = weight_grad(active, grad_ffn)
    downbias_part = token_sum(grad_ffn)
    grad_active = product_back(grad_ffn, down_w)
    gelu_pull = jax.vjp(gelu_exact, before)[1]
    grad_before = gelu_pull(grad_active)[0].astype(jnp.bfloat16)
    upweight_part = weight_grad(settled_low, grad_before)
    upbias_part = token_sum(grad_before)
    grad_settled = grad_two + product_back(grad_before, up_w)
    grad_one, attngain_part, attnshift_part = norm_backward(
        grad_settled, normed_one, inverse_one, attn_g.astype(jnp.float32)
    )
    grad_attn = grad_one.astype(jnp.bfloat16)
    proj_part = weight_grad(context_low, grad_attn)
    projbias_part = token_sum(grad_attn)
    grad_context = product_back(grad_attn, proj_w).astype(jnp.bfloat16)
    pieces = [(key_rows, value_rows)]
    for offset in offsets:
        pieces.append(passed_along((key_rows, value_rows), "shard", -offset))
    grad_query, grad_keys, grad_values = attend_backward(
        query_rows, grad_context, context, log_sum, pieces, key_masks, offsets
    )
    grad_mixed = jnp.concatenate([grad_query, grad_keys, grad_values], axis=-1)
    qkv_part = weight_grad(hidden_low, grad_mixed)
    querybias_part = token_sum(grad_query)
    valuebias_part = token_sum(grad_values)
    grad_hidden = grad_one + product_back(grad_mixed, qkv_w)
    layer_grads = (
        qkv_part,
        querybias_part,
        valuebias_part,
        proj_part,
        projbias_part,
        attngain_part,
        attnshift_part,
        upweight_part,
        upbias_part,
        downweight_part,
        downbias_part,
        ffngain_part,
        ffnshift_part,
    )
    return (grad_hidden, layer_grads)


def on_device(
    inputs,
    cotangent,
    segment_ids,
    memory_slot,
    memory_table,
    qkv_weight,
    query_bias,
    value_bias,
    proj_weight,
    proj_bias,
    attn_gain,
    attn_shift,
    up_weight,
    up_bias,
    down_weight,
    down_bias,
    ffn_gain,
    ffn_shift,
):
    shards = lax.axis_size("shard")
    my_index = lax.axis_index("shard")
    row_count = inputs.shape[1]
    reach_out = min(REACH, shards - 1)
    offsets = [offset for offset in range(-reach_out, reach_out + 1) if offset != 0]
    seg_here = lax.dynamic_slice_in_dim(segment_ids, my_index * row_count, row_count, 1)
    key_masks = [piece_mask(segment_ids, seg_here, my_index, shards, row_count, 0)]
    for offset in offsets:
        key_masks.append(piece_mask(segment_ids, seg_here, my_index, shards, row_count, offset))
    gathered = (
        lax.all_gather(qkv_weight, "shard", axis=1, tiled=True),
        lax.all_gather(query_bias, "shard", axis=1, tiled=True),
        lax.all_gather(value_bias, "shard", axis=1, tiled=True),
        lax.all_gather(proj_weight, "shard", axis=1, tiled=True),
        lax.all_gather(proj_bias, "shard", axis=1, tiled=True),
        lax.all_gather(attn_gain, "shard", axis=1, tiled=True),
        lax.all_gather(attn_shift, "shard", axis=1, tiled=True),
        lax.all_gather(up_weight, "shard", axis=1, tiled=True),
        lax.all_gather(up_bias, "shard", axis=1, tiled=True),
        lax.all_gather(down_weight, "shard", axis=1, tiled=True),
        lax.all_gather(down_bias, "shard", axis=1, tiled=True),
        lax.all_gather(ffn_gain, "shard", axis=1, tiled=True),
        lax.all_gather(ffn_shift, "shard", axis=1, tiled=True),
        lax.all_gather(memory_table, "shard", axis=1, tiled=True),
    )
    slot_range = jnp.arange(MEMS, dtype=jnp.int32)
    slot_hot = (memory_slot[..., None] == slot_range).astype(jnp.float32)
    hidden = inputs.astype(jnp.float32) + jnp.einsum(
        "btm,md->btd", slot_hot, gathered[13].astype(jnp.float32), precision=lax.Precision.HIGHEST
    )
    saved_list = []
    for layer_num in range(LAYERS):
        weights = tuple((item[layer_num] for item in gathered[:13]))
        hidden, saved_state = layer_forward(hidden, weights, offsets, key_masks)
        saved_list.append(saved_state)
    regathered = (
        lax.all_gather(qkv_weight, "shard", axis=1, tiled=True),
        lax.all_gather(query_bias, "shard", axis=1, tiled=True),
        lax.all_gather(value_bias, "shard", axis=1, tiled=True),
        lax.all_gather(proj_weight, "shard", axis=1, tiled=True),
        lax.all_gather(proj_bias, "shard", axis=1, tiled=True),
        lax.all_gather(attn_gain, "shard", axis=1, tiled=True),
        lax.all_gather(attn_shift, "shard", axis=1, tiled=True),
        lax.all_gather(up_weight, "shard", axis=1, tiled=True),
        lax.all_gather(up_bias, "shard", axis=1, tiled=True),
        lax.all_gather(down_weight, "shard", axis=1, tiled=True),
        lax.all_gather(down_bias, "shard", axis=1, tiled=True),
        lax.all_gather(ffn_gain, "shard", axis=1, tiled=True),
        lax.all_gather(ffn_shift, "shard", axis=1, tiled=True),
    )
    grad_hidden = cotangent.astype(jnp.float32)
    grads_by_layer = [None] * LAYERS
    for layer_num in range(LAYERS - 1, -1, -1):
        weights = tuple((item[layer_num] for item in regathered))
        grad_hidden, layer_grads = layer_backward(
            grad_hidden, weights, saved_list[layer_num], offsets, key_masks
        )
        grads_by_layer[layer_num] = layer_grads
    memory_full = jnp.einsum("btm,btd->md", slot_hot, grad_hidden, precision=lax.Precision.HIGHEST)
    stacked = [
        jnp.stack([grads_by_layer[layer_num][member] for layer_num in range(LAYERS)])
        for member in range(13)
    ]
    shares = (
        lax.psum_scatter(stacked[0], "shard", scatter_dimension=1, tiled=True),
        lax.psum_scatter(stacked[1], "shard", scatter_dimension=1, tiled=True),
        lax.psum_scatter(stacked[2], "shard", scatter_dimension=1, tiled=True),
        lax.psum_scatter(stacked[3], "shard", scatter_dimension=1, tiled=True),
        lax.psum_scatter(stacked[4], "shard", scatter_dimension=1, tiled=True),
        lax.psum_scatter(stacked[5], "shard", scatter_dimension=1, tiled=True),
        lax.psum_scatter(stacked[6], "shard", scatter_dimension=1, tiled=True),
        lax.psum_scatter(stacked[7], "shard", scatter_dimension=1, tiled=True),
        lax.psum_scatter(stacked[8], "shard", scatter_dimension=1, tiled=True),
        lax.psum_scatter(stacked[9], "shard", scatter_dimension=1, tiled=True),
        lax.psum_scatter(stacked[10], "shard", scatter_dimension=1, tiled=True),
        lax.psum_scatter(stacked[11], "shard", scatter_dimension=1, tiled=True),
        lax.psum_scatter(stacked[12], "shard", scatter_dimension=1, tiled=True),
        lax.psum_scatter(memory_full, "shard", scatter_dimension=1, tiled=True),
    )
    totals = (
        lax.psum(shares[0].astype(jnp.bfloat16), "rep").astype(jnp.float32),
        lax.psum(shares[1].astype(jnp.bfloat16), "rep").astype(jnp.float32),
        lax.psum(shares[2].astype(jnp.bfloat16), "rep").astype(jnp.float32),
        lax.psum(shares[3].astype(jnp.bfloat16), "rep").astype(jnp.float32),
        lax.psum(shares[4].astype(jnp.bfloat16), "rep").astype(jnp.float32),
        lax.psum(shares[5].astype(jnp.bfloat16), "rep").astype(jnp.float32),
        lax.psum(shares[6].astype(jnp.bfloat16), "rep").astype(jnp.float32),
        lax.psum(shares[7].astype(jnp.bfloat16), "rep").astype(jnp.float32),
        lax.psum(shares[8].astype(jnp.bfloat16), "rep").astype(jnp.float32),
        lax.psum(shares[9].astype(jnp.bfloat16), "rep").astype(jnp.float32),
        lax.psum(shares[10].astype(jnp.bfloat16), "rep").astype(jnp.float32),
        lax.psum(shares[11].astype(jnp.bfloat16), "rep").astype(jnp.float32),
        lax.psum(shares[12].astype(jnp.bfloat16), "rep").astype(jnp.float32),
        lax.psum(shares[13].astype(jnp.bfloat16), "rep").astype(jnp.float32),
    )
    return (
        hidden,
        grad_hidden,
        totals[13],
        totals[0],
        totals[1],
        totals[2],
        totals[3],
        totals[4],
        totals[5],
        totals[6],
        totals[7],
        totals[8],
        totals[9],
        totals[10],
        totals[11],
        totals[12],
    )


BLOCK = 256
GROUP = 4
BF16 = jnp.bfloat16
F32 = jnp.float32


def mm(left, right, left_dim, right_dim):
    return lax.dot_general(
        left, right, (((left_dim,), (right_dim,)), ((), ())), preferred_element_type=F32
    )


def exchange(tensor, axis, mask):
    count = lax.axis_size(axis)
    return lax.ppermute(tensor, axis, [(i, i ^ mask) for i in range(count)])


def ordered(first_is_mine, mine, other):
    return jnp.stack(
        [jnp.where(first_is_mine, mine, other), jnp.where(first_is_mine, other, mine)]
    )


def outgoing(tensor, index):
    return jnp.where(index < GROUP, tensor[1], tensor[0])


def to_groups(tensor, other, index):
    low = index < GROUP
    both = ordered(low, jnp.where(low, tensor[0], tensor[1]), other)
    return both.reshape((2 * tensor.shape[1],) + tensor.shape[2:])


def in_halves(tensor):
    return tensor.reshape((2, tensor.shape[0] // 2) + tensor.shape[1:])


def from_groups(tensor, other, index):
    low = index < GROUP
    halves = in_halves(tensor)
    return ordered(low, jnp.where(low, halves[0], halves[1]), other.astype(tensor.dtype))


def swap(tensor):
    shape = tensor.shape
    flat = tensor.reshape((shape[0] * shape[1],) + shape[2:])
    moved = lax.all_to_all(
        flat, "shard", 0, 0, axis_index_groups=[[0, 1, 2, 3], [4, 5, 6, 7]], tiled=True
    )
    return moved.reshape(shape)


def block_cols(block):
    half = block // GROUP
    return pl.ds(pl.multiple_of(half * BLOCK, BLOCK), BLOCK)


def flipped(tensor):
    return jnp.transpose(tensor.astype(F32)).astype(BF16)


def pair_mask(seg_col, seg_row, keys, queries):
    col = seg_col[pl.ds(pl.multiple_of(keys * BLOCK, BLOCK), BLOCK), :]
    col = jnp.concatenate([col] * (BLOCK // 128), axis=1)
    return col == seg_row[queries]


def attend_kernel(
    lo_ref, hi_ref, x_ref, seg_col, seg_row, low_ref, out_ref, lse_ref, keys_nat, acc, top, total,
):
    heads = x_ref.shape[1] // (3 * HEAD_DIM)
    width = heads * HEAD_DIM
    blocks = seg_row.shape[0]

    def flip(block, carry):
        for h in range(heads):
            keys_nat[h, block] = flipped(
                x_ref[block % GROUP, width + h * HEAD_DIM : width + (h + 1) * HEAD_DIM, block_cols(block)]
            )
        return carry

    lax.fori_loop(0, blocks, flip, 0)

    def per_query(i, carry):
        src, cols = (i % GROUP, block_cols(i))
        for h in range(heads):
            top[h] = jnp.full(top.shape[1:], masked_score, F32)
            total[h] = jnp.zeros(total.shape[1:], F32)
            acc[h] = jnp.zeros(acc.shape[1:], F32)

        def per_key(j, inner):
            allowed = pair_mask(seg_col, seg_row, j, i)
            olds = [top[h] for h in range(heads)]
            sums = [total[h] for h in range(heads)]
            mixes = [acc[h] for h in range(heads)]
            scores = [
                mm(keys_nat[h, j], x_ref[src, h * HEAD_DIM : (h + 1) * HEAD_DIM, cols], 1, 0)
                for h in range(heads)
            ]
            scores = [jnp.where(allowed, item, masked_score) for item in scores]
            news = [
                jnp.maximum(old, jnp.max(item, axis=0, keepdims=True)) for old, item in zip(olds, scores)
            ]
            raised = [jnp.exp(item - new) for item, new in zip(scores, news)]
            adds = [
                mm(
                    x_ref[j % GROUP, 2 * width + h * HEAD_DIM : 2 * width + (h + 1) * HEAD_DIM, block_cols(j)],
                    raised[h].astype(BF16), 1, 0,
                )
                for h in range(heads)
            ]
            for h in range(heads):
                fade = jnp.exp(olds[h] - news[h])
                top[h] = news[h]
                total[h] = sums[h] * fade + jnp.sum(raised[h], axis=0, keepdims=True)
                acc[h] = mixes[h] * fade + adds[h]
            return inner

        lax.fori_loop(lo_ref[i], hi_ref[i], per_key, 0)
        for h in range(heads):
            out = acc[h] / total[h]
            out_ref[src, h * HEAD_DIM : (h + 1) * HEAD_DIM, cols] = out
            low_ref[src, h * HEAD_DIM : (h + 1) * HEAD_DIM, cols] = out.astype(BF16)
            lse_ref[h, i] = top[h] + jnp.log(total[h])
        return carry

    lax.fori_loop(0, blocks, per_query, 0)


def attend_back_kernel(
    lo_ref, hi_ref, x_ref, go_ref, out_ref, lse_ref, seg_col, seg_row, dx_ref,
    keys_nat, values_nat, delta, dq, dk, dv,
):
    heads = x_ref.shape[1] // (3 * HEAD_DIM)
    width = heads * HEAD_DIM
    blocks = seg_row.shape[0]

    def prepare(block, carry):
        src, cols = (block % GROUP, block_cols(block))
        for h in range(heads):
            low, high = (h * HEAD_DIM, (h + 1) * HEAD_DIM)
            keys_nat[h, block] = flipped(x_ref[src, width + low : width + high, cols])
            values_nat[h, block] = flipped(x_ref[src, 2 * width + low : 2 * width + high, cols])
            delta[h, block] = jnp.sum(
                go_ref[src, low:high, cols].astype(F32) * out_ref[src, low:high, cols],
                axis=0,
                keepdims=True,
            )
            dq[h, block] = jnp.zeros(dq.shape[2:], F32)
        return carry

    lax.fori_loop(0, blocks, prepare, 0)

    def per_key(j, carry):
        key_src, key_cols = (j % GROUP, block_cols(j))
        for h in range(heads):
            dk[h] = jnp.zeros(dk.shape[1:], F32)
            dv[h] = jnp.zeros(dv.shape[1:], F32)

        def per_query(i, inner):
            src, cols = (i % GROUP, block_cols(i))
            allowed = pair_mask(seg_col, seg_row, j, i)
            spots = [slice(h * HEAD_DIM, (h + 1) * HEAD_DIM) for h in range(heads)]
            old_dv = [dv[h] for h in range(heads)]
            old_dk = [dk[h] for h in range(heads)]
            old_dq = [dq[h, i] for h in range(heads)]
            queries = [x_ref[src, spot, cols] for spot in spots]
            grads = [go_ref[src, spot, cols] for spot in spots]
            scores = [mm(keys_nat[h, j], queries[h], 1, 0) for h in range(heads)]
            grad_probs = [mm(values_nat[h, j], grads[h], 1, 0) for h in range(heads)]
            probs = [
                jnp.exp(jnp.where(allowed, scores[h], masked_score) - lse_ref[h, i]) for h in range(heads)
            ]
            grad_scores = [
                (probs[h] * (grad_probs[h] - delta[h, i])).astype(BF16) for h in range(heads)
            ]
            add_dv = [mm(grads[h], probs[h].astype(BF16), 1, 1) for h in range(heads)]
            add_dk = [mm(queries[h], grad_scores[h], 1, 1) for h in range(heads)]
            add_dq = [
                mm(x_ref[key_src, width + h * HEAD_DIM : width + (h + 1) * HEAD_DIM, key_cols], grad_scores[h], 1, 0)
                for h in range(heads)
            ]
            for h in range(heads):
                dv[h] = old_dv[h] + add_dv[h]
                dk[h] = old_dk[h] + add_dk[h]
                dq[h, i] = old_dq[h] + add_dq[h]
            return inner

        lax.fori_loop(lo_ref[j], hi_ref[j], per_query, 0)
        for h in range(heads):
            low, high = (h * HEAD_DIM, (h + 1) * HEAD_DIM)
            dx_ref[key_src, width + low : width + high, key_cols] = dk[h].astype(BF16)
            dx_ref[key_src, 2 * width + low : 2 * width + high, key_cols] = dv[h].astype(BF16)
        return carry

    lax.fori_loop(0, blocks, per_key, 0)

    def finish(block, carry):
        src, cols = (block % GROUP, block_cols(block))
        for h in range(heads):
            dx_ref[src, h * HEAD_DIM : (h + 1) * HEAD_DIM, cols] = (dq[h, block] * 0.125).astype(BF16)
        return carry

    lax.fori_loop(0, blocks, finish, 0)


def in_vmem(count):
    return [pl.BlockSpec(memory_space=pltpu.VMEM)] * count


def attend(qkv, spans, seg_col, seg_row):
    heads = qkv.shape[1] // (3 * HEAD_DIM)
    blocks = seg_row.shape[0]
    return pl.pallas_call(
        attend_kernel,
        name="attend",
        out_shape=(
            jax.ShapeDtypeStruct((GROUP, heads * HEAD_DIM, qkv.shape[2]), BF16),
            jax.ShapeDtypeStruct((GROUP, heads * HEAD_DIM, qkv.shape[2]), F32),
            jax.ShapeDtypeStruct((heads, blocks, 1, BLOCK), F32),
        ),
        in_specs=[pl.BlockSpec(memory_space=pltpu.SMEM)] * 2 + in_vmem(3),
        out_specs=in_vmem(3),
        scratch_shapes=[
            pltpu.VMEM((heads, blocks, BLOCK, HEAD_DIM), BF16),
            pltpu.VMEM((heads, HEAD_DIM, BLOCK), F32),
            pltpu.VMEM((heads, 1, BLOCK), F32),
            pltpu.VMEM((heads, 1, BLOCK), F32),
        ],
    )(*spans, qkv, seg_col, seg_row)


def attend_back(qkv, grad_out, out, lse, spans, seg_col, seg_row):
    heads = qkv.shape[1] // (3 * HEAD_DIM)
    blocks = seg_row.shape[0]
    return pl.pallas_call(
        attend_back_kernel,
        name="attend_back",
        out_shape=jax.ShapeDtypeStruct(qkv.shape, BF16),
        in_specs=[pl.BlockSpec(memory_space=pltpu.SMEM)] * 2 + in_vmem(6),
        out_specs=in_vmem(1)[0],
        scratch_shapes=[
            pltpu.VMEM((heads, blocks, BLOCK, HEAD_DIM), BF16),
            pltpu.VMEM((heads, blocks, BLOCK, HEAD_DIM), BF16),
            pltpu.VMEM((heads, blocks, 1, BLOCK), F32),
            pltpu.VMEM((heads, blocks, HEAD_DIM, BLOCK), F32),
            pltpu.VMEM((heads, HEAD_DIM, BLOCK), F32),
            pltpu.VMEM((heads, HEAD_DIM, BLOCK), F32),
        ],
    )(*spans, qkv, grad_out, out, lse, seg_col, seg_row)


def norm_rows(tensor, gain, shift):
    center = tensor - jnp.mean(tensor, axis=-1, keepdims=True)
    inverse = lax.rsqrt(jnp.mean(center * center, axis=-1, keepdims=True) + norm_eps)
    normed = center * inverse
    return (normed * gain + shift, normed, inverse)


def norm_rows_back(grad, normed, inverse, gain):
    scaled = grad * gain
    inner = (
        scaled
        - jnp.mean(scaled, axis=-1, keepdims=True)
        - normed * jnp.mean(scaled * normed, axis=-1, keepdims=True)
    )
    return (inner * inverse, jnp.sum(grad * normed, axis=0), jnp.sum(grad, axis=0))


def fast_forward(hidden, weights, vecs, spans, seg_col, seg_row):
    query_b, value_b, proj_b, attn_g, attn_s, down_b, ffn_g, ffn_s, up_b = vecs
    width = hidden.shape[1]
    hidden_low = hidden.astype(BF16)
    qkv_w, later = weights
    mixed = mm(qkv_w, hidden_low, 0, 1)
    query = (mixed[:width] + query_b[:, None]).astype(BF16) * BF16(0.125)
    keys = mixed[width : 2 * width].astype(BF16)
    values = (mixed[2 * width :] + value_b[:, None]).astype(BF16)
    share = width // GROUP
    packed = jnp.concatenate(
        [part.reshape(GROUP, share, part.shape[1]) for part in (query, keys, values)], axis=1
    )
    proj_w, up_w, down_w, qkv = later(packed)
    low, out, lse = attend(qkv, spans, seg_col, seg_row)
    context = swap(low).reshape(width, low.shape[2])
    attn_out = mm(context, proj_w, 0, 0) + proj_b
    settled, normed_one, inverse_one = norm_rows(hidden + attn_out, attn_g, attn_s)
    settled_low = settled.astype(BF16)
    before = mm(settled_low, up_w, 1, 0) + up_b
    below = 0.5 * (1.0 + lax.erf(before * 0.7071067811865476))
    active = (before * below).astype(BF16)
    slope = (below + before * jnp.exp(-0.5 * before * before) * 0.3989422804014327).astype(BF16)
    ffn_out = mm(active, down_w, 1, 0) + down_b
    result, normed_two, inverse_two = norm_rows(settled + ffn_out, ffn_g, ffn_s)
    return result, (qkv_w, proj_w, up_w, down_w), (
        hidden_low, qkv, out, lse, context, normed_one, inverse_one, settled_low,
        active, slope, normed_two, inverse_two,
    )


def fast_backward(grad, weights, vecs, saved, spans, seg_col, seg_row, give_back):
    query_b, value_b, proj_b, attn_g, attn_s, down_b, ffn_g, ffn_s, up_b = vecs
    qkv_w, proj_w, up_w, down_w = weights
    (
        hidden_low, qkv, out, lse, context, normed_one, inverse_one, settled_low,
        active, slope, normed_two, inverse_two,
    ) = saved
    width = grad.shape[1]
    grad_two, ffn_g_sum, ffn_s_sum = norm_rows_back(grad, normed_two, inverse_two, ffn_g)
    grad_ffn = grad_two.astype(BF16)
    down_b_sum = jnp.sum(grad_ffn.astype(F32), axis=0)
    grad_before = (mm(grad_ffn, down_w, 1, 1) * slope.astype(F32)).astype(BF16)
    down_grad = mm(active, grad_ffn, 0, 0).astype(BF16)
    up_grad = mm(settled_low, grad_before, 0, 0).astype(BF16)
    up_b_sum = jnp.sum(grad_before.astype(F32), axis=0)
    grad_settled = grad_two + mm(grad_before, up_w, 1, 1)
    grad_one, attn_g_sum, attn_s_sum = norm_rows_back(grad_settled, normed_one, inverse_one, attn_g)
    grad_attn = grad_one.astype(BF16)
    proj_b_sum = jnp.sum(grad_attn.astype(F32), axis=0)
    grad_context = mm(proj_w, grad_attn, 1, 1).astype(BF16)
    proj_grad = mm(context, grad_attn, 1, 0).astype(BF16)
    grad_out = swap(grad_context.reshape(GROUP, width // GROUP, grad_context.shape[1]))
    moved = give_back(attend_back(qkv, grad_out, out, lse, spans, seg_col, seg_row))
    share = width // GROUP
    mixed = jnp.transpose(moved.reshape(GROUP, 3, share, moved.shape[2]), (1, 0, 2, 3))
    mixed = mixed.reshape(3 * width, moved.shape[2])
    qkv_grad = mm(hidden_low, mixed, 0, 1).astype(BF16)
    grad_hidden = grad_one + mm(mixed, qkv_w, 0, 1)
    mixed_sum = jnp.sum(mixed.astype(F32), axis=1)
    sums = [
        mixed_sum[:width], mixed_sum[2 * width :], proj_b_sum, attn_g_sum, attn_s_sum, down_b_sum,
        ffn_g_sum, ffn_s_sum,
    ]
    sums += [up_b_sum[part * width : (part + 1) * width] for part in range(up_w.shape[1] // width)]
    return grad_hidden, (qkv_grad, proj_grad, up_grad, down_grad), sums


MESH = pl.DeviceIdType.MESH


def places():
    rep, shard = (lax.axis_index("rep"), lax.axis_index("shard"))
    core, y, z = (lax.rem(rep, 2), lax.rem(shard, 2), lax.div(shard, 2))
    across_x = lax.rem(rep + 2, 4)
    across_core = rep + 1 - 2 * core
    zs = (z, z + 1 - 2 * lax.rem(z, 2), lax.rem(z + 2, 4), 3 - z)
    return (rep, shard, core, y, across_x, across_core, zs)


def greet(diagonal=False):
    rep, shard, core, y, across_x, across_core, zs = places()
    barrier = pltpu.get_barrier_semaphore()
    partners = [(rep, 2 * other + y) for other in zs[1:]]
    partners += [(rep, 2 * zs[0] + 1 - y), (across_x, shard), (across_core, shard)]
    if diagonal:
        partners += [(rep, 2 * other + 1 - y) for other in zs[1:]]
    for partner in partners:
        pl.semaphore_signal(barrier, inc=1, device_id=partner, device_id_type=MESH)
    pl.semaphore_wait(barrier, len(partners))


class Sends:
    def __init__(self, sems):
        self.sems = sems
        self.copies = []

    def push(self, source, target, arrived, device):
        copy = pltpu.make_async_remote_copy(
            source, target, self.sems.at[len(self.copies)], arrived, device_id=device, device_id_type=MESH
        )
        copy.start()
        self.copies.append(copy)

    def finish(self):
        for copy in self.copies:
            copy.wait_send()


def gather_kernel(fourths, smalls, swaps, trades, *refs):
    count = fourths + smalls
    total = count + swaps
    every = total + trades
    owns, fulls = (refs[:every], refs[every : 2 * every])
    local_sems, send_sems, fourth_sems, small_sems, swap_sems, trade_sems = refs[2 * every :]
    rep, shard, core, y, across_x, across_core, zs = places()
    member = lax.rem(shard, GROUP)
    greet(smalls + swaps > 0)
    sends = Sends(send_sems)
    beside, past_x, past_core = ((rep, 2 * zs[0] + 1 - y), (across_x, shard), (across_core, shard))

    def send(n, chunk, part, device, own=False):
        target = fulls[n].at[chunk, part]
        source = owns[n].at[part] if own else target
        sends.push(source, target, fourth_sems.at[n, chunk, part], device)

    def arrive(n, chunk, part):
        piece = fulls[n].at[chunk, part]
        pltpu.make_async_copy(piece, piece, fourth_sems.at[n, chunk, part]).wait()

    near_members = ((1, y), (0, 1 - y), (1, 1 - y))
    for n in range(smalls):
        for k in range(4):
            for other in (y, 1 - y) if k else (1 - y,):
                sends.push(
                    owns[fourths + n],
                    fulls[fourths + n].at[shard],
                    small_sems.at[shard],
                    (rep, 2 * zs[k] + other),
                )
    for n in range(fourths):
        send(n, shard, rep, beside, True)
        for k in (1, 2, 3):
            send(n, shard, rep, (rep, 2 * zs[k] + y), True)
    for n in range(trades):
        sends.push(owns[total + n], fulls[total + n], trade_sems.at[n], (rep, 2 * zs[2] + y))
    for n in range(swaps):
        for k, other in near_members:
            target = 2 * zs[k] + other
            sends.push(
                owns[count + n].at[lax.rem(target, GROUP)],
                fulls[count + n].at[member],
                swap_sems.at[n, member],
                (rep, target),
            )
    local = [
        pltpu.make_async_copy(owns[n], fulls[n].at[shard], local_sems.at[n]) for n in range(count)
    ]
    local += [
        pltpu.make_async_copy(owns[n].at[member], fulls[n].at[member], local_sems.at[n])
        for n in range(count, total)
    ]
    for copy in local:
        copy.start()

    events = ((0, 1), (1, 0), (2, 0), (1, 1), (3, 0), (2, 1), (3, 1))
    chunks = [2 * zs[k] + (1 - y if far else y) for k, far in events]

    def from_x(chunk):
        for n in range(fourths):
            arrive(n, chunk, across_x)
            send(n, chunk, across_x, past_core)

    for at, (chunk, (k, far)) in enumerate(zip(chunks, events)):
        for n in range(fourths):
            arrive(n, chunk, rep)
            if not far:
                send(n, chunk, rep, beside)
            send(n, chunk, rep, past_x)
            send(n, chunk, rep, past_core)
        if at >= 3:
            from_x(chunks[at - 3])
    for chunk in chunks[-3:]:
        from_x(chunk)
    for chunk in chunks:
        for n in range(fourths):
            arrive(n, chunk, across_core)
            arrive(n, chunk, lax.rem(across_core + 2, 4))
        for n in range(smalls):
            piece = fulls[fourths + n].at[chunk]
            pltpu.make_async_copy(piece, piece, small_sems.at[chunk]).wait()
    for n in range(swaps):
        for k, other in near_members:
            source = lax.rem(2 * zs[k] + other, GROUP)
            piece = fulls[count + n].at[source]
            pltpu.make_async_copy(piece, piece, swap_sems.at[n, source]).wait()
    for n in range(trades):
        piece = fulls[total + n]
        pltpu.make_async_copy(piece, piece, trade_sems.at[n]).wait()
    for copy in local:
        copy.wait()
    sends.finish()


def gather_fast(fourths, smalls, swaps, trades, name, collective_id):
    split = [item.reshape(4, item.shape[0] // 4, item.shape[1]) for item in fourths] + smalls
    extra = swaps + trades
    owns = split + extra
    dma = pltpu.SemaphoreType.DMA
    fulls = pl.pallas_call(
        functools.partial(gather_kernel, len(fourths), len(smalls), len(swaps), len(trades)),
        name=name,
        out_shape=[jax.ShapeDtypeStruct((8,) + item.shape, BF16) for item in split]
        + [jax.ShapeDtypeStruct(item.shape, BF16) for item in extra],
        in_specs=in_vmem(len(owns)),
        out_specs=[pl.BlockSpec(memory_space=pl.ANY)] * len(owns),
        scratch_shapes=[
            dma((len(owns),)),
            dma((28 * len(fourths) + 7 * len(smalls) + 3 * len(swaps) + len(trades),)),
            dma((len(fourths), 8, 4)),
            dma((8,)),
            dma((max(1, len(swaps)), GROUP)),
            dma((max(1, len(trades)),)),
        ],
        compiler_params=pltpu.CompilerParams(collective_id=collective_id, has_side_effects=True),
    )(*owns)
    wide = len(fourths)
    return [item.reshape(-1, item.shape[3]) for item in fulls[:wide]] + list(fulls[wide:])


def reduce_kernel(x_first, groups, smalls, swaps, trades, *refs):
    kinds = len(x_first)
    total = kinds + smalls + swaps + trades
    grads, extra = (refs[:kinds], refs[kinds:total])
    outs, extra_out = (refs[total : total + kinds], refs[total + kinds : 2 * total])
    scratch = refs[2 * total :]
    mats, cores, ones, twos, threes, stage_one, stage_two, stage_three, alls = [
        scratch[kinds * n : kinds * n + kinds] for n in range(9)
    ]
    (
        small_sum, small_got, local_sems, send_sems, core_sems, one_sems, two_sems, three_sems, all_sems,
        small_sems, swap_sems, trade_sems,
    ) = scratch[9 * kinds :]
    rep, shard, core, y, across_x, across_core, zs = places()
    x = lax.div(rep, 2)
    member = lax.rem(shard, GROUP)
    beside, past_x, past_core = ((rep, 2 * zs[0] + 1 - y), (across_x, shard), (across_core, shard))
    local = [pltpu.make_async_copy(grads[n], mats[n], local_sems.at[n]) for n in range(kinds)]
    for copy in local:
        copy.start()
    greet(swaps > 0)
    sends = Sends(send_sems)

    def arrive(ref, sem):
        pltpu.make_async_copy(ref, ref, sem).wait()

    def mat(n, k, fy, fx, side=0):
        chunk = 2 * zs[k] + (1 - y if fy else y)
        return mats[n].at[chunk, 2 * (1 - x if fx else x) + (1 - core if side else core)]

    def add(target, parts):
        steps = 6
        lanes = target.shape[1] // steps

        def body(step, carry):
            at = pl.ds(pl.multiple_of(step * lanes, lanes), lanes)
            total = parts[0][:, at].astype(F32)
            for part in parts[1:]:
                total = total + part[:, at].astype(F32)
            target[:, at] = total.astype(BF16)
            return carry

        lax.fori_loop(0, steps, body, 0)

    small_partners = (past_core, past_x, beside, (rep, 2 * zs[1] + y), (rep, 2 * zs[2] + y))

    def small_send(step):
        sends.push(small_sum.at[step], small_got.at[step], small_sems.at[step], small_partners[step])

    def small_step(step):
        if not smalls:
            return
        arrive(small_got.at[step], small_sems.at[step])
        small_sum[step + 1] = small_sum[step] + small_got[step]
        if step + 1 < len(small_partners):
            small_send(step + 1)
        else:
            extra_out[0][...] = small_sum[step + 1]

    if smalls:
        small_sum[0] = extra[0][...]
        small_send(0)
    order = (2, 3, 1, 0)

    def open_group(group):
        for n in group:
            local[n].wait()
        for fy in (1, 0):
            for k in order:
                for n in group:
                    for fx in (1, 0):
                        sends.push(
                            mat(n, k, fy, fx, 1),
                            cores[n].at[k, fy, fx],
                            core_sems.at[n, k, fy, fx],
                            past_core,
                        )

    def cored(n, k, fy, fx):
        arrive(cores[n].at[k, fy, fx], core_sems.at[n, k, fy, fx])
        return [mat(n, k, fy, fx), cores[n].at[k, fy, fx]]

    def oned(n, k, fy, fx):
        flag = fy if x_first[n] else fx
        arrive(ones[n].at[k, flag], one_sems.at[n, k, flag])
        return cored(n, k, fy, fx) + [ones[n].at[k, flag]]

    def step_one(group, slot):
        k, flag = (order[slot % 4], 1 - slot // 4)
        for n in group:
            stage = stage_one[n].at[slot]
            add(stage, cored(n, k, flag, 1) if x_first[n] else cored(n, k, 1, flag))
            sends.push(
                stage, ones[n].at[k, flag], one_sems.at[n, k, flag], past_x if x_first[n] else beside
            )

    def step_two(group, at):
        k = order[at]
        for n in group:
            stage = stage_two[n].at[k]
            add(stage, oned(n, k, 1, 0) if x_first[n] else oned(n, k, 0, 1))
            sends.push(stage, twos[n].at[k], two_sems.at[n, k], beside if x_first[n] else past_x)

    def twod(n, k):
        parts = oned(n, k, 0, 0)
        arrive(twos[n].at[k], two_sems.at[n, k])
        return parts + [twos[n].at[k]]

    def step_three(group, at):
        k = order[at]
        for n in group:
            stage = stage_three[n].at[k - 1]
            add(stage, twod(n, k))
            sends.push(stage, threes[n].at[k - 1], three_sems.at[n, k - 1], (rep, 2 * zs[k] + y))

    def close(group):
        for n in group:
            parts = twod(n, 0)
            for k in range(3):
                arrive(threes[n].at[k], three_sems.at[n, k])
            mine = alls[n].at[rep]
            add(mine, parts + [threes[n].at[k] for k in range(3)])
            sends.push(mine, mine, all_sems.at[n, rep], past_x)
            sends.push(mine, mine, all_sems.at[n, rep], past_core)

    def spread(group):
        for n in group:
            theirs = alls[n].at[across_x]
            arrive(theirs, all_sems.at[n, across_x])
            sends.push(theirs, theirs, all_sems.at[n, across_x], past_core)

    def store(group):
        opposite = lax.rem(across_core + 2, 4)
        for n in group:
            arrive(alls[n].at[across_core], all_sems.at[n, across_core])
            arrive(alls[n].at[opposite], all_sems.at[n, opposite])
            rows = mats[n].shape[2]
            for q in range(4):
                outs[n][q * rows : (q + 1) * rows, :] = alls[n][q].astype(F32)

    one, two = groups
    open_group(one)
    step_one(one, 0)
    near_members = ((1, y), (0, 1 - y), (1, 1 - y))
    for n in range(swaps):
        for k, other in near_members:
            target = 2 * zs[k] + other
            sends.push(
                extra[smalls + n].at[lax.rem(target, GROUP)],
                extra_out[smalls + n].at[member],
                swap_sems.at[n, member],
                (rep, target),
            )
    own_swaps = [
        pltpu.make_async_copy(
            extra[smalls + n].at[member], extra_out[smalls + n].at[member], local_sems.at[kinds + n]
        )
        for n in range(swaps)
    ]
    for copy in own_swaps:
        copy.start()
    for n in range(trades):
        spot = smalls + swaps + n
        sends.push(extra[spot], extra_out[spot], trade_sems.at[n], (rep, 2 * zs[2] + y))
    step_one(one, 1)
    step_one(one, 2)
    open_group(two)
    small_step(0)
    step_one(one, 3)
    for at in range(4):
        step_one(one, 4 + at)
        step_two(one, at)
    small_step(1)
    step_one(two, 0)
    step_one(two, 1)
    for at in range(3):
        step_three(one, at)
        if at < 2:
            step_one(two, 2 + at)
    small_step(2)
    for at in range(4):
        step_one(two, 4 + at)
        step_two(two, at)
    small_step(3)
    close(one)
    for at in range(3):
        step_three(two, at)
    spread(one)
    small_step(4)
    close(two)
    store(one)
    spread(two)
    store(two)
    for n in range(swaps):
        for k, other in near_members:
            source = lax.rem(2 * zs[k] + other, GROUP)
            arrive(extra_out[smalls + n].at[source], swap_sems.at[n, source])
    for n in range(trades):
        arrive(extra_out[smalls + swaps + n], trade_sems.at[n])
    for copy in own_swaps:
        copy.wait()
    sends.finish()


def reduce_fast(grads, x_first, groups, small, swapped, traded, name, collective_id):
    kinds = len(grads)
    extra = small + swapped + traded
    away = len(swapped) + len(traded)
    sizes = [(item.shape[0] // 32, item.shape[1]) for item in grads]
    buffers = []
    for lead in ((8, 4), (4, 2, 2), (4, 2), (4,), (3,), (8,), (4,), (3,), (4,)):
        buffers += [pltpu.VMEM(lead + size, BF16) for size in sizes]
    small_shape = small[0].shape if small else (8, 128)
    dma = pltpu.SemaphoreType.DMA
    anywhere = pl.BlockSpec(memory_space=pl.ANY)
    return pl.pallas_call(
        functools.partial(reduce_kernel, x_first, groups, len(small), len(swapped), len(traded)),
        name=name,
        out_shape=[jax.ShapeDtypeStruct((4 * size[0], size[1]), F32) for size in sizes]
        + [jax.ShapeDtypeStruct(item.shape, item.dtype) for item in extra],
        in_specs=[anywhere] * kinds + in_vmem(len(extra)),
        out_specs=in_vmem(kinds + len(small)) + [anywhere] * away,
        scratch_shapes=buffers
        + [
            pltpu.VMEM((6,) + small_shape, F32), pltpu.VMEM((5,) + small_shape, F32),
            dma((kinds + 1,)), dma((34 * kinds + 9,)), dma((kinds, 4, 2, 2)), dma((kinds, 4, 2)),
            dma((kinds, 4)), dma((kinds, 3)), dma((kinds, 4)), dma((5,)), dma((1, GROUP)),
            dma((1,)),
        ],
        compiler_params=pltpu.CompilerParams(
            collective_id=collective_id, has_side_effects=True, vmem_limit_bytes=58 * 1024 * 1024
        ),
    )(*[item.reshape((8, 4) + size) for item, size in zip(grads, sizes)], *extra)


def on_device_fast(
    inputs, cotangent, segment_ids, memory_slot, memory_table,
    qkv_weight, query_bias, value_bias, proj_weight, proj_bias, attn_gain, attn_shift,
    up_weight, up_bias, down_weight, down_bias, ffn_gain, ffn_shift,
):
    index = lax.axis_index("shard")
    width = inputs.shape[2]
    share = memory_table.shape[1]
    ups = up_weight.shape[2] // width

    vec_args = (
        query_bias, value_bias, proj_bias, attn_gain, attn_shift, down_bias, ffn_gain, ffn_shift,
    )
    plain = len(vec_args)
    rows = [item[layer][None] for layer in range(LAYERS) for item in vec_args]
    rows += [up_bias[layer].reshape(ups, share) for layer in range(LAYERS)]
    rows.append(memory_table)
    small = jnp.concatenate(rows, axis=0)
    used = small.shape[0]
    small = jnp.pad(small, ((0, -used % 16), (0, 128 - share)))
    first_qkv, small, other_inputs = gather_fast(
        [qkv_weight[0]], [small], [], [outgoing(inputs, index)], "gather_first", 0
    )
    small = small[:, :used, :share].astype(F32)
    wide = jnp.transpose(small, (1, 0, 2)).reshape(used, width)
    vecs = []
    for layer in range(LAYERS):
        start = LAYERS * plain + layer * ups
        vecs.append(
            [wide[layer * plain + item] for item in range(plain)]
            + [small[:, start : start + ups].reshape(ups * width)]
        )
    table = wide[LAYERS * (plain + ups) :].astype(BF16)

    second_qkv, others = ([], [])

    def rest_first(packed):
        proj_w, up_w, qkv_w, down_w, qkv = gather_fast(
            [proj_weight[0], up_weight[0], qkv_weight[1], down_weight[0]], [], [packed], [],
            "gather_middle", 2,
        )
        second_qkv.append(qkv_w)
        return proj_w, up_w, down_w, qkv

    def rest_second(packed):
        *parts, other_cotangent = gather_fast(
            [proj_weight[1], up_weight[1], down_weight[1]], [], [packed],
            [outgoing(cotangent, index)], "gather_last", 3,
        )
        others.append(other_cotangent)
        return parts

    rests = (rest_first, rest_second)

    segs = jnp.where(index < GROUP, segment_ids[0], segment_ids[1])
    tiles = segs.reshape(-1, BLOCK)
    first, last = (tiles[:, 0], tiles[:, -1])
    spans = (
        jnp.sum((last[None, :] < first[:, None]).astype(jnp.int32), axis=1),
        jnp.sum((first[None, :] <= last[:, None]).astype(jnp.int32), axis=1),
    )
    seg_row = tiles[:, None, :]
    seg_col = jnp.broadcast_to(segs[:, None], (segs.shape[0], 128))

    other_slots = exchange(outgoing(memory_slot, index), "shard", GROUP)
    slots = to_groups(memory_slot, other_slots, index)
    slot_hot = slots[:, None] == jnp.arange(MEMS, dtype=jnp.int32)
    hidden = to_groups(inputs, other_inputs, index).astype(F32) + mm(slot_hot.astype(BF16), table, 1, 0)
    saved, held = ([], [])
    for layer in range(LAYERS):
        qkv_w = second_qkv[0] if layer else first_qkv
        hidden, mats, state = fast_forward(
            hidden, (qkv_w, rests[layer]), vecs[layer], spans, seg_col, seg_row
        )
        saved.append(state)
        held.append(mats)

    grad = to_groups(cotangent, others[0], index).astype(F32)
    sums, shares = ([None] * LAYERS, [None] * LAYERS)
    found = []

    def sum_second(grad_qkv):
        parts = reduce_fast(
            found[0], (1, 1, 1, 1), ((2, 3), (0, 1)), [], [grad_qkv],
            [outgoing(in_halves(hidden.astype(BF16)), index)], "reduce_second", 4,
        )
        shares[1] = parts[:4]
        others.append(parts[5])
        return parts[4]

    for layer in range(LAYERS - 1, -1, -1):
        grad, mat_grads, sums[layer] = fast_backward(
            grad, held[layer], vecs[layer], saved[layer], spans, seg_col, seg_row,
            swap if layer else sum_second,
        )
        found.append(mat_grads)
    layer_output = from_groups(hidden, others[1], index)
    memory_sum = lax.dot_general(
        slot_hot.astype(F32), grad, (((0,), (0,)), ((), ())), precision=lax.Precision.HIGHEST
    )
    flat = jnp.concatenate([jnp.stack(sums[layer]) for layer in range(LAYERS)] + [memory_sum], axis=0)
    used = flat.shape[0]
    flat = jnp.pad(flat, ((0, -used % 8), (0, 0)))
    *first_shares, flat, other_grad = reduce_fast(
        found[1], (0, 1, 1, 0), ((0, 2), (1, 3)), [flat], [],
        [outgoing(in_halves(grad.astype(BF16)), index)], "reduce_first", 1,
    )
    input_grad = from_groups(grad, other_grad, index)
    shares[0] = first_shares
    flat = flat[:used]
    per = plain + ups
    own = lax.dynamic_slice_in_dim(flat, index * share, share, 1)
    vec_grads = [
        jnp.stack([own[layer * per + item] for layer in range(LAYERS)]) for item in range(plain)
    ]
    up_sums = jnp.stack([flat[layer * per + plain : (layer + 1) * per].reshape(-1) for layer in range(LAYERS)])
    upbias_grad = lax.dynamic_slice_in_dim(up_sums, index * share * ups, share * ups, 1)
    memory_grad = own[LAYERS * per :]

    def wide_grad(member):
        return jnp.stack([shares[layer][member] for layer in range(LAYERS)])

    return (
        layer_output,
        input_grad,
        memory_grad,
        wide_grad(0),
        vec_grads[0],
        vec_grads[1],
        wide_grad(1),
        vec_grads[2],
        vec_grads[3],
        vec_grads[4],
        wide_grad(2),
        upbias_grad,
        wide_grad(3),
        vec_grads[5],
        vec_grads[6],
        vec_grads[7],
    )


def fast_fits(mesh):
    return mesh.shape["shard"] == 2 * GROUP and mesh.shape["rep"] == 4


def solution(mesh):
    return jax.shard_map(
        on_device_fast if fast_fits(mesh) else on_device,
        mesh=mesh,
        in_specs=(
            P(None, ("rep", "shard"), None),
            P(None, ("rep", "shard"), None),
            P(None, "rep"),
            P(None, ("rep", "shard")),
            P(None, "shard"),
            P(None, "shard", None),
            P(None, "shard"),
            P(None, "shard"),
            P(None, "shard", None),
            P(None, "shard"),
            P(None, "shard"),
            P(None, "shard"),
            P(None, "shard", None),
            P(None, "shard"),
            P(None, "shard", None),
            P(None, "shard"),
            P(None, "shard"),
            P(None, "shard"),
        ),
        out_specs=(
            P(None, ("rep", "shard"), None),
            P(None, ("rep", "shard"), None),
            P(None, "shard"),
            P(None, "shard", None),
            P(None, "shard"),
            P(None, "shard"),
            P(None, "shard", None),
            P(None, "shard"),
            P(None, "shard"),
            P(None, "shard"),
            P(None, "shard", None),
            P(None, "shard"),
            P(None, "shard", None),
            P(None, "shard"),
            P(None, "shard"),
            P(None, "shard"),
        ),
        check_vma=False,
    )
```
